32 devices in a mesh: req: 8 (over z, y), grp: 4 (over x, core).
Axes of the slice: x: 2, y: 2, z: 4, core: 2. Of those that a mesh axis runs over, the one named last changes fastest.
Arguments:
- tokens: bfloat16 [128, 64, 1024], P(('req', 'grp')), may hold values from -6 to 6
- kv_pool: bfloat16 [192, 256, 2048], P('req', 'grp'), may hold values from -70 to 70
- page_table: int32 [8, 16, 6], P(None, 'grp'), may hold values from 0 to 191, as said below
- cache_lens: int32 [128], P(('req', 'grp')), may hold values from 48 to 384
- draft_lengths: int32 [8, 16], P('req'), may hold values from 32 to 64, as said below
- draft_parents: int32 [128, 64], P(('req', 'grp')), may hold values from -1 to 62, as said below
- accepted_path: int32 [128, 64], P(('req', 'grp')), may hold values from -1 to 63, as said below
- prompt_group: int32 [128], P(('req', 'grp')), may hold values from 0 to 23
- memory_kv: bfloat16 [24, 256, 2048], P(None, 'req'), may hold values from -70 to 70
- w_query: bfloat16 [1024, 1024], replicated, may hold values from -0.1875 to 0.1875
- w_key: bfloat16 [1024, 1024], replicated, may hold values from -0.1875 to 0.1875
- w_value: bfloat16 [1024, 1024], replicated, may hold values from -0.1875 to 0.1875
- w_output: bfloat16 [1024, 1024], replicated, may hold values from -0.1875 to 0.1875
- w_cross_query: bfloat16 [1024, 1024], replicated, may hold values from -0.1875 to 0.1875
- w_cross_output: bfloat16 [1024, 1024], replicated, may hold values from -0.1875 to 0.1875
- w_in: bfloat16 [1024, 4096], P(None, 'grp'), may hold values from -0.1875 to 0.1875
- w_out: bfloat16 [4096, 1024], P('grp'), may hold values from -0.09375 to 0.09375
Outputs:
- layer_out: bfloat16 [128, 64, 1024], P(('req', 'grp'))
- accepted_kv: bfloat16 [128, 64, 2048], P(('req', 'grp'))
The draws below stay inside these ranges and needn't reach their ends.
Inputs may be any that keep to these rules, and one draw needn't show every extreme that they name: For each g < 4, the entries of page_table[:, g * 4 : (g + 1) * 4, :] name every row of kv_pool exactly once. Within one row r of page_table and one such g, at most 4 entries share the same value of e // 24, and for each g some row reaches 4. `draft_lengths`: each row sums to 704 and holds 64 at least once. `draft_parents`: position 0 has parent -1; position i >= 1 has its parent in max(0, i - 4) to i - 1. `accepted_path`: row n lists in increasing order the positions on the walk along draft_parents from one live draft position of request n back to position 0, then -1 in the remaining slots.
All inputs are finite; a program needn't handle non-finite values.
Results may differ from the reference program's by a relative error of at most 0.017.
Values may be sent and summed in bfloat16 or wider, within the bound.
A program may use at most 192 MiB of HBM per device.

```python
import jax
import jax.numpy as jnp
from jax import lax

D = 1024
HEADS = 16
FF = 4096
GROUPS = 24
SRC = 256
DRAFT = 64
MIN_DRAFT = 32
PAGE = 64
REQ_DEV = 4
PAGES = 6
CTX = 384
POOL_DEV = 24
CAP = 4
GROUP_TOK = 704
REQS = 128
N_REQ = 8
N_GRP = 4


def tree_tables(key):
    slot_count = N_GRP * REQ_DEV
    extra_span = DRAFT - MIN_DRAFT
    extra_units = GROUP_TOK - slot_count * MIN_DRAFT - extra_span

    def one_row(row_key):
        full_key, unit_key = jax.random.split(row_key)
        full_slot = jax.random.randint(full_key, (), 0, slot_count)
        unit_ids = jax.random.permutation(unit_key, (slot_count - 1) * extra_span)[:extra_units]
        owner_ids = unit_ids // extra_span
        counts = jnp.sum((owner_ids[:, None] == jnp.arange(slot_count - 1)[None, :]).astype(jnp.int32), axis=0)
        slot_ids = jnp.arange(slot_count)
        other_ids = jnp.clip(slot_ids - (slot_ids > full_slot).astype(jnp.int32), 0, slot_count - 2)
        row_lengths = jnp.where(slot_ids == full_slot, DRAFT, MIN_DRAFT + counts[other_ids]).astype(jnp.int32)
        return (row_lengths, slot_ids == full_slot)
    lengths, full_marks = jax.vmap(one_row)(jax.random.split(jax.random.fold_in(key, 101), N_REQ))
    positions = jnp.arange(DRAFT, dtype=jnp.int32)
    jumps = jax.random.randint(jax.random.fold_in(key, 102), (REQS, DRAFT), 0, 4)
    parents = jnp.where(positions[None, :] == 0, -1, jnp.maximum(positions[None, :] - 1 - jumps, 0)).astype(jnp.int32)
    random_leaf = jax.random.randint(jax.random.fold_in(key, 103), (REQS,), 0, lengths.reshape(REQS)).astype(jnp.int32)
    leaf = jnp.where(full_marks.reshape(REQS), DRAFT - 1, random_leaf).astype(jnp.int32)

    def walk_step(step_index, carry):
        current, marks = carry
        upward = jnp.take_along_axis(parents, current[:, None], axis=1)[:, 0]
        current = jnp.where(current > 0, upward, 0)
        marks = marks | (positions[None, :] == current[:, None])
        return (current, marks)
    start_marks = positions[None, :] == leaf[:, None]
    current, marks = lax.fori_loop(0, DRAFT - 1, walk_step, (leaf, start_marks))
    order_keys = jnp.where(marks, positions[None, :], DRAFT + positions[None, :])
    sorted_keys = jnp.sort(order_keys, axis=1)
    path_ids = jnp.where(sorted_keys < DRAFT, sorted_keys, -1).astype(jnp.int32)
    return (lengths, parents, path_ids)


def draw_draft_lengths(key, part):
    return tree_tables(key)[0]


def draw_draft_parents(key, part):
    return tree_tables(key)[1]


def draw_accepted_path(key, part):
    return tree_tables(key)[2]


def draw_page_table(key, part):
    owners = N_REQ
    pool_pages = POOL_DEV
    capacity = CAP

    def one_column(column_key):
        keys = jax.random.split(column_key, 5)
        residues = jax.random.permutation(keys[0], owners)
        positions = jnp.arange(pool_pages)
        spread_ids = jnp.where(positions < capacity, 0, 1 + (positions - capacity) % (owners - 1))
        offsets = residues[spread_ids][jax.random.permutation(keys[1], pool_pages)]
        mixer = jax.random.permutation(keys[2], owners)
        shuffle = jax.random.permutation(keys[3], owners)
        source = mixer[(shuffle[:, None] + offsets[None, :]) % owners]

        def slot_order(index):
            return jax.random.permutation(jax.random.fold_in(keys[4], index), pool_pages)
        slot_table = jax.vmap(slot_order)(jnp.arange(owners))
        slot_ids = slot_table[source, positions[None, :]]
        return (source * pool_pages + slot_ids).reshape(owners, REQ_DEV, PAGES).astype(jnp.int32)
    tables = jax.vmap(one_column)(jax.random.split(jax.random.fold_in(key, 201), N_GRP))
    return jnp.transpose(tables, (1, 0, 2, 3)).reshape(N_REQ, N_GRP * REQ_DEV, PAGES)


def spiked_field(key, shape, key_columns, value_scale):
    base_key = jax.random.fold_in(key, 0)
    values = jax.random.truncated_normal(base_key, -6.0, 6.0, shape, jnp.float32)
    boost = jnp.ones(shape[:-1] + (1,), jnp.float32)
    column_ids = jnp.arange(shape[-1])
    column_scale = jnp.where(column_ids < key_columns, boost, value_scale)
    return (values * column_scale).astype(jnp.bfloat16)


def draw_kv_pool(key, part):
    return spiked_field(jax.random.fold_in(key, 301), (N_REQ * POOL_DEV, N_GRP * PAGE, 2 * D), D, 1.0)


def draw_memory_kv(key, part):
    return spiked_field(jax.random.fold_in(key, 302), (GROUPS, SRC, 2 * D), D, 4.0)


def set_ends(result, rng, least, largest):
    place = [jax.random.randint(jax.random.fold_in(rng, axis), (), 0, length) for axis, length in enumerate(result.shape)]
    main_axis = result.shape.index(max(result.shape))
    neighbour = place[:main_axis] + [(place[main_axis] + 1) % result.shape[main_axis]] + place[main_axis + 1:]
    return result.at[tuple(place)].set(least).at[tuple(neighbour)].set(largest)


def levels(stream_key, dims, cuts, low, top_value):
    gain, own = 1.0, jax.random.fold_in(stream_key, 6)
    for position, shards_of in cuts:
        draws = jnp.exp(jax.random.uniform(jax.random.fold_in(own, position), (shards_of,), jnp.float32, low / len(cuts), top_value / len(cuts)))
        gain = gain * jnp.repeat(draws, dims[position] // shards_of).reshape([-1 if axis == position else 1 for axis in range(len(dims))])
    return gain


def bell_draw(own_key, extent, deviation, bound, shards=(), kind=jnp.bfloat16):
    values = deviation * jax.random.normal(own_key, extent, jnp.float32)
    if shards:
        values = values * levels(own_key, extent, shards, -0.22, 0.18)
    return jnp.clip(values, -bound, bound).astype(kind)


def setup_inputs(seed: int = 0) -> dict:
    streams_of = jax.random.split(jax.random.key(seed), 18)
    tokens = bell_draw(streams_of[0], (REQS, DRAFT, D), 1.0, 6.0, ((0, 32),))
    kv_pool = draw_kv_pool(jax.random.fold_in(streams_of[17], 71), 0)
    page_table = draw_page_table(jax.random.fold_in(streams_of[17], 71), 0)
    cache_lens = set_ends(jax.random.randint(streams_of[3], (REQS,), CTX // 8, CTX + 1), jax.random.fold_in(streams_of[3], 1), CTX // 8, CTX).astype(jnp.int32)
    draft_lengths = draw_draft_lengths(jax.random.fold_in(streams_of[17], 71), 0)
    draft_parents = draw_draft_parents(jax.random.fold_in(streams_of[17], 71), 0)
    accepted_path = draw_accepted_path(jax.random.fold_in(streams_of[17], 71), 0)
    prompt_group = set_ends(jax.random.randint(streams_of[7], (REQS,), 0, GROUPS), jax.random.fold_in(streams_of[7], 1), 0, GROUPS - 1).astype(jnp.int32)
    memory_kv = draw_memory_kv(jax.random.fold_in(streams_of[17], 71), 0)
    w_query = bell_draw(streams_of[9], (D, D), D ** -0.5, 0.1875)
    w_key = bell_draw(streams_of[10], (D, D), D ** -0.5, 0.1875)
    w_value = bell_draw(streams_of[11], (D, D), D ** -0.5, 0.1875)
    w_output = bell_draw(streams_of[12], (D, D), D ** -0.5, 0.1875)
    w_cross_query = bell_draw(streams_of[13], (D, D), D ** -0.5, 0.1875)
    w_cross_output = bell_draw(streams_of[14], (D, D), D ** -0.5, 0.1875)
    w_in = bell_draw(streams_of[15], (D, FF), D ** -0.5, 0.1875, ((1, 4),))
    w_out = bell_draw(streams_of[16], (FF, D), FF ** -0.5, 0.09375, ((0, 4),))
    return {"tokens": tokens, "kv_pool": kv_pool, "page_table": page_table, "cache_lens": cache_lens, "draft_lengths": draft_lengths, "draft_parents": draft_parents, "accepted_path": accepted_path, "prompt_group": prompt_group, "memory_kv": memory_kv, "w_query": w_query, "w_key": w_key, "w_value": w_value, "w_output": w_output, "w_cross_query": w_cross_query, "w_cross_output": w_cross_output, "w_in": w_in, "w_out": w_out}


EPSILON = 1e-05
NEGATIVE = -1e+30

def layer_norm(values):
    center = values - lax.optimization_barrier(jnp.mean(values, axis=-1, keepdims=True))
    spread = lax.optimization_barrier(jnp.mean(center * center, axis=-1, keepdims=True))
    return center * lax.rsqrt(spread + EPSILON)

def round_bf16(values):
    return lax.optimization_barrier(values.astype(jnp.bfloat16)).astype(jnp.float32)

def ancestors(parents):
    draft_len = parents.shape[-1]
    column_ids = jnp.arange(draft_len, dtype=jnp.int32)
    linked = (parents[:, :, None] == column_ids[None, None, :]).astype(jnp.float32)
    closure = linked + jnp.eye(draft_len, dtype=jnp.float32)[None]
    for sweep_index in range(draft_len.bit_length()):
        closure = jnp.minimum(jnp.einsum('nij,njk->nik', closure, closure, precision=lax.Precision.HIGHEST), 1.0)
    return closure

def reference(tokens, kv_pool, page_table, cache_lens, draft_lengths, draft_parents, accepted_path, prompt_group, memory_kv, w_query, w_key, w_value, w_output, w_cross_query, w_cross_output, w_in, w_out):
    draft_len = tokens.shape[1]
    model_width = tokens.shape[2]
    head_dim = model_width // HEADS
    score_scale = head_dim ** (-0.5)
    pool_blocks = kv_pool.reshape(N_REQ * POOL_DEV, N_GRP, PAGE, 2 * model_width)

    def split_heads(values):
        return values.reshape(values.shape[0], values.shape[1], HEADS, head_dim).astype(jnp.float32)

    def one_device(device):
        row_id = device // N_GRP
        col_id = device % N_GRP
        first_req = device * REQ_DEV
        zero_index = jnp.zeros((), jnp.int32)
        x_rows = lax.dynamic_slice_in_dim(tokens, first_req, REQ_DEV, 0)
        entries = lax.dynamic_slice(page_table, (row_id, col_id * REQ_DEV, zero_index), (1, REQ_DEV, PAGES)).reshape(REQ_DEV * PAGES)
        picked = jnp.take(pool_blocks, entries, axis=0)
        cache_rows = lax.dynamic_index_in_dim(picked, col_id, 1, keepdims=False).reshape(REQ_DEV, PAGES * PAGE, 2 * model_width)
        lengths = lax.dynamic_slice_in_dim(cache_lens, first_req, REQ_DEV, 0)
        counts = lax.dynamic_slice(draft_lengths, (row_id, col_id * REQ_DEV), (1, REQ_DEV))[0]
        parents = lax.dynamic_slice_in_dim(draft_parents, first_req, REQ_DEV, 0)
        path_ids = lax.dynamic_slice_in_dim(accepted_path, first_req, REQ_DEV, 0)
        groups = lax.dynamic_slice_in_dim(prompt_group, first_req, REQ_DEV, 0)
        flat_rows = x_rows.reshape(REQ_DEV * draft_len, model_width)
        query_rows = (jnp.dot(flat_rows, w_query, preferred_element_type=jnp.float32) * score_scale).astype(jnp.bfloat16)
        key_new = jnp.dot(flat_rows, w_key, preferred_element_type=jnp.float32).astype(jnp.bfloat16)
        value_new = jnp.dot(flat_rows, w_value, preferred_element_type=jnp.float32).astype(jnp.bfloat16)
        query_heads = split_heads(query_rows.reshape(REQ_DEV, draft_len, model_width))
        cache_keys = split_heads(cache_rows[:, :, :model_width])
        cache_values = split_heads(cache_rows[:, :, model_width:])
        new_keys = split_heads(key_new.reshape(REQ_DEV, draft_len, model_width))
        new_values = split_heads(value_new.reshape(REQ_DEV, draft_len, model_width))
        score_cache = jnp.einsum('nihd,nphd->nhip', query_heads, cache_keys)
        score_draft = jnp.einsum('nihd,njhd->nhij', query_heads, new_keys)
        positions = jnp.arange(cache_rows.shape[1], dtype=jnp.int32)
        score_cache = jnp.where((positions[None, :] < lengths[:, None])[:, None, None, :], score_cache, NEGATIVE)
        score_draft = jnp.where((ancestors(parents) > 0.5)[:, None, :, :], score_draft, NEGATIVE)
        top_score = jnp.maximum(lax.optimization_barrier(jnp.max(score_cache, axis=-1)), lax.optimization_barrier(jnp.max(score_draft, axis=-1)))[..., None]
        expo_cache = jnp.exp(score_cache - top_score)
        expo_draft = jnp.exp(score_draft - top_score)
        expo_total = lax.optimization_barrier(jnp.sum(expo_cache, axis=-1)) + lax.optimization_barrier(jnp.sum(expo_draft, axis=-1))
        mixed_heads = jnp.einsum('nhip,nphd->nihd', round_bf16(expo_cache), cache_values) + jnp.einsum('nhij,njhd->nihd', round_bf16(expo_draft), new_values)
        mixed_heads = mixed_heads / jnp.transpose(expo_total, (0, 2, 1))[..., None]
        self_mix = mixed_heads.reshape(REQ_DEV * draft_len, model_width).astype(jnp.bfloat16)
        first_norm = layer_norm(flat_rows.astype(jnp.float32) + jnp.dot(self_mix, w_output, preferred_element_type=jnp.float32)).astype(jnp.bfloat16)
        cross_query = (jnp.dot(first_norm, w_cross_query, preferred_element_type=jnp.float32) * score_scale).astype(jnp.bfloat16)
        cross_heads = split_heads(cross_query.reshape(REQ_DEV, draft_len, model_width))
        memory = jnp.take(memory_kv, groups, axis=0)
        memory_keys = split_heads(memory[:, :, :model_width])
        memory_values = split_heads(memory[:, :, model_width:])
        cross_scores = jnp.einsum('nihd,nphd->nhip', cross_heads, memory_keys)
        cross_top = lax.optimization_barrier(jnp.max(cross_scores, axis=-1, keepdims=True))
        cross_expo = jnp.exp(cross_scores - cross_top)
        cross_total = lax.optimization_barrier(jnp.sum(cross_expo, axis=-1))
        cross_heads_mix = jnp.einsum('nhip,nphd->nihd', round_bf16(cross_expo), memory_values)
        cross_heads_mix = cross_heads_mix / jnp.transpose(cross_total, (0, 2, 1))[..., None]
        cross_mix = cross_heads_mix.reshape(REQ_DEV * draft_len, model_width).astype(jnp.bfloat16)
        second_norm = layer_norm(first_norm.astype(jnp.float32) + jnp.dot(cross_mix, w_cross_output, preferred_element_type=jnp.float32)).astype(jnp.bfloat16)
        hidden = jax.nn.gelu(jnp.dot(second_norm, w_in, preferred_element_type=jnp.float32), approximate=False).astype(jnp.bfloat16)
        normed = layer_norm(second_norm.astype(jnp.float32) + jnp.dot(hidden, w_out, preferred_element_type=jnp.float32))
        live = (jnp.arange(draft_len, dtype=jnp.int32)[None, :] < counts[:, None]).reshape(REQ_DEV * draft_len)
        result_rows = jnp.where(live[:, None], normed, 0.0).astype(jnp.bfloat16)
        path_pick = (path_ids[:, :, None] == jnp.arange(draft_len, dtype=jnp.int32)[None, None, :]).astype(jnp.float32)
        kv_new = jnp.concatenate([key_new, value_new], axis=1).reshape(REQ_DEV, draft_len, 2 * model_width)
        accepted = jnp.einsum('nij,njc->nic', path_pick, kv_new.astype(jnp.float32)).astype(jnp.bfloat16)
        return (result_rows.reshape(REQ_DEV, draft_len, model_width), accepted)
    layer_rows, accepted_rows = lax.map(one_device, jnp.arange(N_REQ * N_GRP, dtype=jnp.int32))
    return (layer_rows.reshape(REQS, draft_len, model_width), accepted_rows.reshape(REQS, draft_len, 2 * model_width))
```

```python
import functools

import jax
import jax.numpy as jnp
from jax import lax
from jax.experimental import pallas as pl
from jax.experimental.pallas import tpu as pltpu
from jax.sharding import PartitionSpec as P

HEADS = 16
BUNDLE = 4


EPSILON = 1e-05
NEGATIVE = -1e30


def layer_norm(values):
    center = values - jnp.mean(values, axis=-1, keepdims=True)
    spread = jnp.mean(center * center, axis=-1, keepdims=True)
    return center * lax.rsqrt(spread + EPSILON)


def ancestors(parents):
    draft_len = parents.shape[-1]
    column_ids = jnp.arange(draft_len, dtype=jnp.int32)
    linked = (parents[:, :, None] == column_ids[None, None, :]).astype(jnp.float32)
    closure = linked + jnp.eye(draft_len, dtype=jnp.float32)[None]
    for sweep_index in range(draft_len.bit_length()):
        half = closure.astype(jnp.bfloat16)
        closure = jnp.minimum(
            jnp.einsum("nij,njk->nik", half, half, preferred_element_type=jnp.float32), 1.0
        )
    return closure


VMEM_BYTES = 24 * 1024 * 1024


def stream(sources, targets, held_ref, in_sems, out_sems):
    loads = [
        pltpu.make_async_copy(source, held_ref.at[slot], in_sems.at[slot])
        for slot, source in enumerate(sources)
    ]
    stores = [
        pltpu.make_async_copy(held_ref.at[slot], target, out_sems.at[slot])
        for slot, target in enumerate(targets)
    ]
    for load in loads:
        load.start()
    for load, store in zip(loads, stores):
        load.wait()
        store.start()
    for store in stores:
        store.wait()


def pack_kernel(count, ids_ref, source_ref, out_ref, held_ref, in_sems, out_sems):
    sources = [source_ref.at[ids_ref[slot]] for slot in range(count)]
    stream(sources, [out_ref.at[slot] for slot in range(count)], held_ref, in_sems, out_sems)


def take_blocks(source, ids):
    count = ids.shape[0]
    return pl.pallas_call(
        functools.partial(pack_kernel, count),
        in_specs=[
            pl.BlockSpec(memory_space=pltpu.SMEM),
            pl.BlockSpec(memory_space=pl.ANY),
        ],
        out_specs=pl.BlockSpec(memory_space=pl.ANY),
        out_shape=jax.ShapeDtypeStruct((count,) + source.shape[1:], source.dtype),
        scratch_shapes=[
            pltpu.VMEM((count,) + source.shape[1:], source.dtype),
            pltpu.SemaphoreType.DMA((count,)),
            pltpu.SemaphoreType.DMA((count,)),
        ],
        compiler_params=pltpu.CompilerParams(vmem_limit_bytes=VMEM_BYTES),
        cost_estimate=pl.CostEstimate(
            flops=0, bytes_accessed=4 * count * source[0].size, transcendentals=0
        ),
    )(ids, source)


def attend(query, keys, values, visible):
    rows, width = query.shape
    head_dim = width // HEADS
    bundle_width = BUNDLE * head_dim
    owner_row = lax.broadcasted_iota(jnp.int32, (BUNDLE * rows, bundle_width), 0) // rows
    owner_lane = lax.broadcasted_iota(jnp.int32, (BUNDLE * rows, bundle_width), 1) // head_dim
    own = owner_row == owner_lane
    if visible is not None:
        visible = jnp.concatenate([visible] * BUNDLE, axis=0)
    mixed = []
    for bundle in range(HEADS // BUNDLE):
        lanes = slice(bundle * bundle_width, (bundle + 1) * bundle_width)
        stacked = jnp.concatenate([query[:, lanes]] * BUNDLE, axis=0)
        stacked = jnp.where(own, stacked, jnp.zeros((), stacked.dtype))
        scores = lax.dot_general(
            stacked, keys[:, lanes], (((1,), (1,)), ((), ())), preferred_element_type=jnp.float32
        )
        if visible is not None:
            scores = jnp.where(visible, scores, NEGATIVE)
        expo = jnp.exp(scores - jnp.max(scores, axis=-1, keepdims=True))
        total = jnp.sum(expo, axis=-1, keepdims=True)
        mix = jnp.dot(
            expo.astype(jnp.bfloat16), values[:, lanes], preferred_element_type=jnp.float32
        )
        mix = jnp.where(own, mix / total, 0.0)
        folded = mix[:rows]
        for part in range(1, BUNDLE):
            folded = folded + mix[part * rows : (part + 1) * rows]
        mixed.append(folded.astype(jnp.bfloat16))
    return jnp.concatenate(mixed, axis=1)


def self_kernel(ids_ref, lens_ref, query_ref, key_ref, value_ref, reach_ref, *rest):
    page_refs, out_ref = rest[:-1], rest[-1]
    request = pl.program_id(0)
    width = query_ref.shape[1]
    rows = query_ref.shape[0]
    context = sum(ref.shape[1] for ref in page_refs)
    keys = jnp.concatenate([ref[0, :, :width] for ref in page_refs] + [key_ref[...]], axis=0)
    values = jnp.concatenate([ref[0, :, width:] for ref in page_refs] + [value_ref[...]], axis=0)
    positions = lax.broadcasted_iota(jnp.int32, (rows, context), 1)
    cached = jnp.where(positions < lens_ref[request], 1.0, 0.0)
    visible = jnp.concatenate([cached, reach_ref[0]], axis=1) > 0.5
    out_ref[...] = attend(query_ref[...], keys, values, visible)


def self_attention(query, key_new, value_new, pages, page_ids, cache_lens, reach):
    req_count, draft_len, _ = reach.shape
    width = query.shape[1]
    page_count = page_ids.shape[0] // req_count
    page_block = (1,) + pages.shape[1:]
    row_spec = pl.BlockSpec((draft_len, width), lambda n, ids, lens: (n, 0))

    def page_spec(place):
        return pl.BlockSpec(page_block, lambda n, ids, lens: (ids[n * page_count + place], 0, 0))

    keys_total = page_count * pages.shape[1] + draft_len
    return pl.pallas_call(
        self_kernel,
        grid_spec=pltpu.PrefetchScalarGridSpec(
            num_scalar_prefetch=2,
            grid=(req_count,),
            in_specs=[
                row_spec,
                row_spec,
                row_spec,
                pl.BlockSpec((1, draft_len, draft_len), lambda n, ids, lens: (n, 0, 0)),
            ]
            + [page_spec(place) for place in range(page_count)],
            out_specs=row_spec,
        ),
        out_shape=jax.ShapeDtypeStruct(query.shape, jnp.bfloat16),
        cost_estimate=pl.CostEstimate(
            flops=4 * BUNDLE * query.shape[0] * keys_total * width,
            bytes_accessed=4 * req_count * keys_total * width + 8 * query.size,
            transcendentals=query.shape[0] * keys_total * HEADS,
        ),
    )(page_ids, cache_lens, query, key_new, value_new, reach, *([pages] * page_count))


def cross_kernel(query_ref, memory_ref, out_ref):
    width = query_ref.shape[1]
    positions = memory_ref.shape[0] * memory_ref.shape[2]
    keys = memory_ref[:, 0, :, :width].reshape(positions, width)
    values = memory_ref[:, 0, :, width:].reshape(positions, width)
    out_ref[...] = attend(query_ref[...], keys, values, None)


def cross_attention(query, memory):
    owners, req_count, local_src, width_both = memory.shape
    rows, width = query.shape
    draft_len = rows // req_count
    row_spec = pl.BlockSpec((draft_len, width), lambda n: (n, 0))
    return pl.pallas_call(
        cross_kernel,
        grid=(req_count,),
        in_specs=[
            row_spec,
            pl.BlockSpec((owners, 1, local_src, width_both), lambda n: (0, n, 0, 0)),
        ],
        out_specs=row_spec,
        out_shape=jax.ShapeDtypeStruct(query.shape, jnp.bfloat16),
        cost_estimate=pl.CostEstimate(
            flops=4 * BUNDLE * rows * owners * local_src * width,
            bytes_accessed=2 * memory.size + 4 * query.size,
            transcendentals=rows * owners * local_src * HEADS,
        ),
    )(query, memory)


def page_plan(page_table, pool_pages, row_index):
    owners = page_table.shape[0]
    capacity = pool_pages // owners + 1
    page_map = page_table.reshape(owners, -1)
    source = page_map // pool_pages
    slot_ids = page_map % pool_pages
    from_here = source == row_index
    page_ids = jnp.arange(page_map.shape[1], dtype=jnp.int32)
    before = page_ids[None, :] < page_ids[:, None]
    send_order = jnp.sum((from_here[:, None, :] & before[None, :, :]).astype(jnp.int32), axis=2)
    slots = jnp.arange(capacity, dtype=jnp.int32)
    placing = from_here[:, :, None] & (send_order[:, :, None] == slots[None, None, :])
    send_ids = jnp.sum(jnp.where(placing, slot_ids[:, :, None], 0), axis=1).reshape(-1)
    my_source = lax.dynamic_index_in_dim(source, row_index, 0, keepdims=False)
    earlier = (my_source[:, None] == my_source[None, :]) & before
    page_rank = jnp.sum(earlier.astype(jnp.int32), axis=1)
    return send_ids, my_source * capacity + page_rank


def exchange(packed, owners):
    shaped = packed.reshape((owners, packed.shape[0] // owners) + packed.shape[1:])
    return lax.all_to_all(shaped, "req", split_axis=0, concat_axis=0, tiled=True)


def per_device(
    tokens,
    kv_pool,
    page_table,
    cache_lens,
    draft_lengths,
    draft_parents,
    accepted_path,
    prompt_group,
    memory_kv,
    w_query,
    w_key,
    w_value,
    w_output,
    w_cross_query,
    w_cross_output,
    w_in,
    w_out,
):
    req_count, draft_len, model_width = tokens.shape
    owners = page_table.shape[0]
    head_dim = model_width // HEADS
    scale = head_dim ** (-0.5)
    row_index = lax.axis_index("req")
    col_index = lax.axis_index("grp")
    send_ids, page_ids = page_plan(page_table, kv_pool.shape[0], row_index)
    all_groups = lax.all_gather(prompt_group, "req", axis=0, tiled=True)
    send_ids, all_groups = lax.optimization_barrier((send_ids, all_groups))
    pages = exchange(take_blocks(kv_pool, send_ids), owners)
    memory = exchange(take_blocks(memory_kv, all_groups), owners)
    pages = pages.reshape((-1,) + kv_pool.shape[1:])
    w_in_full = lax.all_gather(w_in, "grp", axis=1, tiled=True)
    w_out_full = lax.all_gather(w_out, "grp", axis=0, tiled=True)

    flat_rows = tokens.reshape(req_count * draft_len, model_width)
    query_rows = (jnp.dot(flat_rows, w_query, preferred_element_type=jnp.float32) * scale).astype(
        jnp.bfloat16
    )
    key_new = jnp.dot(flat_rows, w_key, preferred_element_type=jnp.float32).astype(jnp.bfloat16)
    value_new = jnp.dot(flat_rows, w_value, preferred_element_type=jnp.float32).astype(jnp.bfloat16)
    reach = ancestors(draft_parents)
    path_pick = (
        accepted_path[:, :, None] == jnp.arange(draft_len, dtype=jnp.int32)[None, None, :]
    ).astype(jnp.bfloat16)
    accepted_kv = jnp.concatenate(
        [
            jnp.einsum(
                "nij,njc->nic",
                path_pick,
                part.reshape(req_count, draft_len, model_width),
                preferred_element_type=jnp.float32,
            ).astype(jnp.bfloat16)
            for part in (key_new, value_new)
        ],
        axis=2,
    )
    self_mix = self_attention(query_rows, key_new, value_new, pages, page_ids, cache_lens, reach)
    first_norm = layer_norm(
        flat_rows.astype(jnp.float32)
        + jnp.dot(self_mix, w_output, preferred_element_type=jnp.float32)
    ).astype(jnp.bfloat16)
    cross_query = (
        jnp.dot(first_norm, w_cross_query, preferred_element_type=jnp.float32) * scale
    ).astype(jnp.bfloat16)
    cross_mix = cross_attention(cross_query, memory)
    second_norm = layer_norm(
        first_norm.astype(jnp.float32)
        + jnp.dot(cross_mix, w_cross_output, preferred_element_type=jnp.float32)
    ).astype(jnp.bfloat16)
    hidden = jax.nn.gelu(
        jnp.dot(second_norm, w_in_full, preferred_element_type=jnp.float32), approximate=False
    ).astype(jnp.bfloat16)
    summed = jnp.dot(hidden, w_out_full, preferred_element_type=jnp.float32)
    group_lengths = draft_lengths[0]
    own_counts = lax.dynamic_slice_in_dim(group_lengths, col_index * req_count, req_count, 0)
    live = (jnp.arange(draft_len, dtype=jnp.int32)[None, :] < own_counts[:, None]).reshape(
        req_count * draft_len
    )
    normed = layer_norm(second_norm.astype(jnp.float32) + summed).astype(jnp.bfloat16)
    result_rows = jnp.where(live[:, None], normed, jnp.zeros((), jnp.bfloat16))
    return (result_rows.reshape(req_count, draft_len, model_width), accepted_kv)


def solution(mesh):
    return jax.shard_map(
        per_device,
        mesh=mesh,
        in_specs=(
            P(("req", "grp"), None, None),
            P("req", "grp", None),
            P(None, "grp", None),
            P(("req", "grp")),
            P("req", None),
            P(("req", "grp"), None),
            P(("req", "grp"), None),
            P(("req", "grp")),
            P(None, "req", None),
            P(),
            P(),
            P(),
            P(),
            P(),
            P(),
            P(None, "grp"),
            P("grp", None),
        ),
        out_specs=(P(("req", "grp"), None, None), P(("req", "grp"), None, None)),
        check_vma=False,
    )
```

```python
import functools

import jax
import jax.numpy as jnp
from jax import lax
from jax.experimental import pallas as pl
from jax.experimental.pallas import tpu as pltpu
from jax.sharding import PartitionSpec as P

HEADS = 16
BUNDLE = 4
MESH = pl.DeviceIdType.MESH
ANY = pl.BlockSpec(memory_space=pl.ANY)
WHOLE = pl.BlockSpec(memory_space=pltpu.VMEM)
SCALARS = pl.BlockSpec(memory_space=pltpu.SMEM)
MIB = 1024 * 1024
RIGHT, LEFT, PAIR = 0, 1, 2

EPSILON = 1e-05
NEGATIVE = -1e30


def layer_norm(values):
    center = values - jnp.mean(values, axis=-1, keepdims=True)
    spread = jnp.mean(center * center, axis=-1, keepdims=True)
    return center * lax.rsqrt(spread + EPSILON)


def reach_down(parents):
    draft_len = parents.shape[-1]
    column_ids = jnp.arange(draft_len, dtype=jnp.int32)
    linked = (parents[:, None, :] == column_ids[None, :, None]).astype(jnp.float32)
    closure = linked + jnp.eye(draft_len, dtype=jnp.float32)[None]
    for sweep_index in range((draft_len - 1).bit_length()):
        half = closure.astype(jnp.bfloat16)
        closure = jnp.minimum(
            jnp.einsum("nij,njk->nik", half, half, preferred_element_type=jnp.float32), 1.0
        )
    return closure


def flip(index, bit):
    return index + bit - 2 * bit * ((index // bit) % 2)


def flips(index, mask):
    bit = 1
    while bit <= mask:
        if mask & bit:
            index = flip(index, bit)
        bit *= 2
    return index


class Line:
    def __init__(self, owners, items, send_sems, recv_sems):
        self.me = lax.axis_index("req")
        self.half = owners // 2
        self.place, self.side = self.me // 2, self.me % 2
        self.pair = flip(self.me, 1)
        self.right = lax.rem(self.place + 1, self.half) * 2 + self.side
        self.left = lax.rem(self.place + self.half - 1, self.half) * 2 + self.side
        self.items, self.send_sems, self.recv_sems = items, send_sems, recv_sems

    def copy(self, item, way, source, owner):
        target = (self.right, self.left, self.pair)[way]
        return pltpu.make_async_remote_copy(
            src_ref=source,
            dst_ref=self.items[item][1](owner),
            send_sem=self.send_sems.at[item, way, owner],
            recv_sem=self.recv_sems.at[item, owner],
            device_id={"req": target},
            device_id_type=MESH,
        )

    def arrive(self, item, owner):
        self.copy(item, PAIR, self.items[item][1](owner), owner).wait_recv()

    def both_ways(self, item, source, owner, act):
        pl.when(self.place < self.half - 1)(lambda: act(self.copy(item, RIGHT, source, owner)))
        pl.when(self.place > 0)(lambda: act(self.copy(item, LEFT, source, owner)))

    def owners_of(self, item, place):
        first = place * 2 + self.side
        return (first, flip(first, 1)) if self.items[item][2] else (first,)

    def start(self, item):
        source = self.items[item][0]
        self.both_ways(item, source, self.me, lambda copy: copy.start())
        self.copy(item, PAIR, source, self.me).start()

    def start_wide(self, item):
        if self.items[item][2]:
            self.arrive(item, self.pair)
            block = self.items[item][1](self.pair)
            self.both_ways(item, block, self.pair, lambda copy: copy.start())

    def step(self, item, distance):
        def forward(place, way, more):
            for owner in self.owners_of(item, place):
                self.arrive(item, owner)
                block = self.items[item][1](owner)
                pl.when(more)(lambda: self.copy(item, way, block, owner).start())
                if not self.items[item][2]:
                    self.copy(item, PAIR, block, owner).start()

        pl.when(self.place - distance >= 0)(
            lambda: forward(self.place - distance, RIGHT, self.place < self.half - 1)
        )
        pl.when(self.place + distance < self.half)(
            lambda: forward(self.place + distance, LEFT, self.place > 0)
        )

    def finish(self, item):
        source, target, wide = self.items[item]
        if not wide:
            for place in range(self.half):
                self.arrive(item, place * 2 + flip(self.side, 1))
        self.copy(item, PAIR, source, self.me).wait_send()
        self.both_ways(item, source, self.me, lambda copy: copy.wait_send())
        if wide:
            self.both_ways(item, source, self.pair, lambda copy: copy.wait_send())

        def sent(place, way, more):
            for owner in self.owners_of(item, place):
                pl.when(more)(lambda: self.copy(item, way, source, owner).wait_send())
                if not wide:
                    self.copy(item, PAIR, source, owner).wait_send()

        for distance in range(1, self.half):
            pl.when(self.place - distance >= 0)(
                lambda: sent(self.place - distance, RIGHT, self.place < self.half - 1)
            )
            pl.when(self.place + distance < self.half)(
                lambda: sent(self.place + distance, LEFT, self.place > 0)
            )


class Square:
    def __init__(self, source, out, send_sems, recv_sems):
        self.part = lax.axis_index("grp")
        self.near, self.far = flip(self.part, 1), flip(self.part, 2)
        self.source, self.out, self.send_sems, self.recv_sems = source, out, send_sems, recv_sems

    def copy(self, hop, source, owner):
        return pltpu.make_async_remote_copy(
            src_ref=source,
            dst_ref=self.out.at[owner],
            send_sem=self.send_sems.at[hop],
            recv_sem=self.recv_sems.at[owner],
            device_id={"grp": (self.far, self.near, self.near)[hop]},
            device_id_type=MESH,
        )

    def start(self):
        self.copy(0, self.source, self.part).start()
        self.copy(1, self.source, self.part).start()

    def forward(self):
        block = self.out.at[self.far]
        self.copy(2, block, self.far).wait_recv()
        self.copy(2, block, self.far).start()

    def finish(self):
        self.copy(1, self.source, self.near).wait_recv()
        self.copy(2, self.source, flip(self.far, 1)).wait_recv()
        self.copy(0, self.source, self.part).wait_send()
        self.copy(1, self.source, self.part).wait_send()
        self.copy(2, self.source, self.far).wait_send()


def meet(owners, parts):
    barrier = pltpu.get_barrier_semaphore()
    me, part = lax.axis_index("req"), lax.axis_index("grp")
    for offset in range(1, owners):
        other = lax.rem(me + offset, owners)
        pl.semaphore_signal(barrier, inc=1, device_id={"req": other}, device_id_type=MESH)
    for offset in range(1, parts):
        other = lax.rem(part + offset, parts)
        pl.semaphore_signal(barrier, inc=1, device_id={"grp": other}, device_id_type=MESH)
    pl.semaphore_wait(barrier, owners + parts - 2)


def line_sems(items, owners):
    return [pltpu.SemaphoreType.DMA((items, 3, owners)), pltpu.SemaphoreType.DMA((items, owners))]


def square_sems(parts):
    return [pltpu.SemaphoreType.DMA((3,)), pltpu.SemaphoreType.DMA((parts,))]


CUTS = 8


def first_kernel(owners, parts, query_ref, win_ref, small_ref, q_out, win_out, lens_out, grps_out,
                 query, win, load_sems, hold_sems, line_send, line_recv, win_send, win_recv,
                 small_send, small_recv):
    me, part = lax.axis_index("req"), lax.axis_index("grp")
    loads = [
        pltpu.make_async_copy(query_ref, query, load_sems.at[0]),
        pltpu.make_async_copy(win_ref, win, load_sems.at[1]),
    ]
    for copy in loads:
        copy.start()
    meet(owners, parts)
    rows = query.shape[0] // CUTS

    def slot(cut, owner):
        return q_out.at[owner, pl.ds(cut * rows, rows)]

    items = [
        (query.at[pl.ds(cut * rows, rows)], functools.partial(slot, cut), cut == 0) for cut in range(CUTS)
    ]
    line = Line(owners, items, line_send, line_recv)
    square = Square(win, win_out, win_send, win_recv)
    loads[0].wait()
    for item in range(CUTS):
        line.start(item)
    loads[1].wait()
    square.start()
    smalls = []
    for offset in range(1, owners):
        smalls.append(pltpu.make_async_remote_copy(
            src_ref=small_ref, dst_ref=lens_out.at[me],
            send_sem=small_send.at[offset], recv_sem=small_recv.at[offset],
            device_id={"req": lax.rem(me + offset, owners)}, device_id_type=MESH))
    for offset in range(1, parts):
        smalls.append(pltpu.make_async_remote_copy(
            src_ref=small_ref, dst_ref=grps_out.at[part],
            send_sem=small_send.at[owners + offset], recv_sem=small_recv.at[owners + offset],
            device_id={"grp": lax.rem(part + offset, parts)}, device_id_type=MESH))
    for copy in smalls:
        copy.start()
    holds = [
        pltpu.make_async_copy(query, q_out.at[me], hold_sems.at[0]),
        pltpu.make_async_copy(win, win_out.at[part], hold_sems.at[1]),
        pltpu.make_async_copy(small_ref, lens_out.at[me], hold_sems.at[2]),
        pltpu.make_async_copy(small_ref, grps_out.at[part], hold_sems.at[3]),
    ]
    for copy in holds:
        copy.start()
    for item in range(CUTS):
        line.start_wide(item)
    for distance in range(1, owners // 2):
        for item in range(CUTS):
            line.step(item, distance)
    square.forward()
    for item in range(CUTS):
        line.finish(item)
    square.finish()
    for copy in smalls + holds:
        copy.wait()


def first_gather(query, w_in, small, owners, parts):
    sds = jax.ShapeDtypeStruct
    return pl.pallas_call(
        functools.partial(first_kernel, owners, parts),
        in_specs=[ANY] * 3,
        out_specs=[ANY] * 4,
        out_shape=[
            sds((owners,) + query.shape, query.dtype),
            sds((parts,) + w_in.shape, w_in.dtype),
            sds((owners,) + small.shape, small.dtype),
            sds((parts,) + small.shape, small.dtype),
        ],
        scratch_shapes=[
            pltpu.VMEM(query.shape, query.dtype),
            pltpu.VMEM(w_in.shape, w_in.dtype),
            pltpu.SemaphoreType.DMA((2,)),
            pltpu.SemaphoreType.DMA((4,)),
            *line_sems(CUTS, owners),
            *square_sems(parts),
            pltpu.SemaphoreType.DMA((owners + parts,)),
            pltpu.SemaphoreType.DMA((owners + parts,)),
        ],
        compiler_params=pltpu.CompilerParams(
            collective_id=1, has_side_effects=True, vmem_limit_bytes=16 * MIB
        ),
    )(query, w_in, small)


def own_lanes(rows, head_dim):
    shape = (BUNDLE * rows, BUNDLE * head_dim)
    row = lax.broadcasted_iota(jnp.int32, shape, 0) // rows
    lane = lax.broadcasted_iota(jnp.int32, shape, 1) // head_dim
    return row == lane


def attend_down(query, keys, values, seen, own):
    rows = query.shape[0]
    stacked = jnp.where(own, jnp.concatenate([query] * BUNDLE, axis=0), jnp.zeros((), query.dtype))
    scores = lax.dot_general(
        keys, stacked, (((1,), (1,)), ((), ())), preferred_element_type=jnp.float32
    )
    if seen is not None:
        scores = jnp.where(seen, scores, NEGATIVE)
    top = jnp.max(scores, axis=0, keepdims=True)
    expo = jnp.exp(scores - top)
    total = jnp.sum(expo, axis=0, keepdims=True)
    mix = lax.dot_general(
        expo.astype(jnp.bfloat16), values, (((0,), (0,)), ((), ())), preferred_element_type=jnp.float32
    )
    mix = jnp.where(own, mix, 0.0)
    folded = mix[:rows]
    for part in range(1, BUNDLE):
        folded = folded + mix[part * rows : (part + 1) * rows]
    return folded, top, total


def pages_kernel(per_owner, per_req, table_ref, lens_ref, query_ref, pool_ref, key_ref, value_ref, reach_ref,
                 mix_out, stat_out, draft_out, draft_stat):
    me = lax.axis_index("req")
    width = query_ref.shape[1]
    pool_pages, page = pool_ref.shape[0], pool_ref.shape[1]
    requests = table_ref.shape[0] // per_req
    rows = query_ref.shape[0] // requests
    head_dim = width // HEADS
    span = BUNDLE * head_dim
    own = own_lanes(rows, head_dim)

    def store(out, stat, n, bundle, result):
        folded, top, total = result
        out[pl.ds(pl.multiple_of(n * rows, rows), rows), pl.ds(bundle * span, span)] = folded.astype(out.dtype)
        stat[n, pl.ds(bundle, 1), :] = top
        stat[n, pl.ds(BUNDLE + bundle, 1), :] = total

    def one(n, carry):
        length = lens_ref[n]
        count = jnp.int32(0)
        slots = [jnp.int32(0)] * per_req
        starts = [jnp.int32(0)] * per_req
        for place in range(per_req):
            entry = table_ref[n * per_req + place]
            hit = (entry // pool_pages == me) & (place * page < length)
            for k in range(place + 1):
                here = hit & (count == k)
                slots[k] = jnp.where(here, entry % pool_pages, slots[k])
                starts[k] = jnp.where(here, length - place * page, starts[k])
            count = count + hit.astype(jnp.int32)

        def work(uses):
            seen = lax.broadcasted_iota(jnp.int32, (page, BUNDLE * rows), 0)
            seen = jnp.concatenate([seen < starts[k] for k in range(uses)], axis=0)
            for bundle in range(HEADS // BUNDLE):
                low = bundle * span
                query = query_ref[pl.ds(pl.multiple_of(n * rows, rows), rows), low : low + span]
                keys = jnp.concatenate([pool_ref[slots[k], :, low : low + span] for k in range(uses)], axis=0)
                values = jnp.concatenate(
                    [pool_ref[slots[k], :, width + low : width + low + span] for k in range(uses)], axis=0
                )
                store(mix_out, stat_out, n, bundle, attend_down(query, keys, values, seen, own))

        @pl.when(count == 0)
        def _():
            at = pl.ds(pl.multiple_of(n * rows, rows), rows)
            mix_out[at, :] = jnp.zeros((rows, width), mix_out.dtype)
            stat_out[n, pl.ds(0, BUNDLE), :] = jnp.full((BUNDLE, BUNDLE * rows), NEGATIVE, jnp.float32)
            stat_out[n, pl.ds(BUNDLE, BUNDLE), :] = jnp.zeros((BUNDLE, BUNDLE * rows), jnp.float32)

        pl.when(count == 1)(lambda: work(1))
        pl.when(count == 2)(lambda: work(2))
        pl.when(count > 2)(lambda: work(per_req))
        return carry

    lax.fori_loop(0, requests, one, 0)

    def drafts(n, carry):
        at = pl.ds(pl.multiple_of(n * rows, rows), rows)
        mine = pl.ds(pl.multiple_of((me * per_owner + n) * rows, rows), rows)
        seen = jnp.concatenate([reach_ref[n]] * BUNDLE, axis=1) > 0.5
        for bundle in range(HEADS // BUNDLE):
            lanes = slice(bundle * span, (bundle + 1) * span)
            result = attend_down(query_ref[mine, lanes], key_ref[at, lanes], value_ref[at, lanes], seen, own)
            store(draft_out, draft_stat, n, bundle, result)
        return carry

    lax.fori_loop(0, per_owner, drafts, 0)


def page_partials(table, lens, query_all, pool, key_new, value_new, reach):
    owners, rows_both, width = query_all.shape
    per_owner = reach.shape[0]
    requests = owners * per_owner
    rows = rows_both // per_owner
    sds = jax.ShapeDtypeStruct
    return pl.pallas_call(
        functools.partial(pages_kernel, per_owner, table.shape[0] // requests),
        in_specs=[SCALARS, SCALARS] + [WHOLE] * 5,
        out_specs=[WHOLE] * 4,
        out_shape=[
            sds((requests * rows, width), query_all.dtype),
            sds((requests, 2 * BUNDLE, BUNDLE * rows), jnp.float32),
            sds((per_owner * rows, width), query_all.dtype),
            sds((per_owner, 2 * BUNDLE, BUNDLE * rows), jnp.float32),
        ],
        compiler_params=pltpu.CompilerParams(vmem_limit_bytes=58 * MIB),
    )(table, lens, query_all.reshape(requests * rows, width), pool, key_new, value_new, reach)


def widen(weights, eye, ones):
    high = weights.astype(jnp.bfloat16)
    low = (weights - high.astype(jnp.float32)).astype(jnp.bfloat16)
    zero = jnp.zeros((), jnp.bfloat16)
    spread = jnp.concatenate(
        [jnp.where(eye, jnp.broadcast_to(part, eye.shape), zero) for part in (high, low)], axis=1
    )
    return jnp.dot(spread, ones, preferred_element_type=jnp.float32)


def merge(sources, stats, out, stat_out, last):
    per_owner, rows, span, store = out
    lanes_of = (rows, BUNDLE * rows)
    eye = lax.broadcasted_iota(jnp.int32, lanes_of, 1) % rows == lax.broadcasted_iota(jnp.int32, lanes_of, 0)
    shape = (2 * BUNDLE * rows, span)
    row_head = (lax.broadcasted_iota(jnp.int32, shape, 0) % (BUNDLE * rows)) // rows
    ones = (row_head == lax.broadcasted_iota(jnp.int32, shape, 1) // (span // BUNDLE)).astype(jnp.float32)
    ones = ones.astype(jnp.bfloat16)

    def one(n, carry):
        read = [stat(n) for stat in stats]
        tops = [value[:BUNDLE] for value in read]
        sums = [value[BUNDLE:] for value in read]
        top = functools.reduce(jnp.maximum, tops)
        scales = [jnp.exp(value - top) for value in tops]
        total = functools.reduce(jnp.add, [scale * part for scale, part in zip(scales, sums)])
        if last:
            scales = [scale / total for scale in scales]
        else:
            stat_out(n, jnp.concatenate([top, total], axis=0))
        for bundle in range(HEADS // BUNDLE):
            lanes = slice(bundle * span, (bundle + 1) * span)
            mixed = functools.reduce(
                jnp.add,
                [
                    widen(scale[bundle : bundle + 1], eye, ones) * source(n, lanes).astype(jnp.float32)
                    for scale, source in zip(scales, sources)
                ],
            )
            store(n, lanes, mixed)
        return carry

    lax.fori_loop(0, per_owner, one, 0)


GROUP_CUTS = 2


def second_kernel(owners, parts, per_owner, mix_ref, stat_ref, draft_ref, draft_stat, memory_ref, wout_ref,
                  self_out, m_out, wout_out,
                  own, own_stat, got, got_stat, zin, zin_stat, memory, wout,
                  load_sems, own_sems, hold_sems, y_send, y_recv, z_send, z_recv,
                  line_send, line_recv, wout_send, wout_recv):
    me, part = lax.axis_index("req"), lax.axis_index("grp")
    half = owners // 2
    place, side = me // 2, me % 2
    pair = flip(me, 1)
    width = draft_ref.shape[1]
    rows = draft_ref.shape[0] // per_owner
    span = BUNDLE * (width // HEADS)
    groups = memory_ref.shape[0]
    wide = memory_ref.shape[2] // 2
    lanes_in = wide // parts

    own_loads = {}
    for mask in range(half - 1, -1, -1):
        dest = flips(place, mask)
        own_loads[mask] = [
            pltpu.make_async_copy(mix_ref.at[dest * 2 + side], own.at[dest], own_sems.at[0, mask]),
            pltpu.make_async_copy(stat_ref.at[dest * 2 + side], own_stat.at[dest], own_sems.at[1, mask]),
        ]
        for copy in own_loads[mask]:
            copy.start()
    loads = []
    for kind in range(2):
        lanes = pl.ds(pl.multiple_of(kind * wide + part * lanes_in, 128), lanes_in)
        loads.append(pltpu.make_async_copy(memory_ref.at[:, :, lanes], memory.at[kind], load_sems.at[kind]))
    loads.append(pltpu.make_async_copy(wout_ref, wout, load_sems.at[2]))
    for copy in loads:
        copy.start()
    meet(owners, parts)

    def to_pair(mask):
        dest = flips(place, mask)
        far = dest * 2 + flip(side, 1)
        return [
            pltpu.make_async_remote_copy(
                src_ref=source.at[far], dst_ref=target.at[dest], send_sem=y_send.at[k, mask],
                recv_sem=y_recv.at[k, mask], device_id={"req": pair}, device_id_type=MESH)
            for k, (source, target) in enumerate(((mix_ref, got), (stat_ref, got_stat)))
        ]

    def to_place(mask):
        dest = flips(place, mask)
        return [
            pltpu.make_async_remote_copy(
                src_ref=source.at[dest], dst_ref=target.at[mask], send_sem=z_send.at[k, mask],
                recv_sem=z_recv.at[k, mask], device_id={"req": dest * 2 + side}, device_id_type=MESH)
            for k, (source, target) in enumerate(((own, zin), (own_stat, zin_stat)))
        ]

    for mask in range(half - 1, -1, -1):
        for copy in to_pair(mask):
            copy.start()

    cut = groups // GROUP_CUTS

    def slot(kind, first, owner):
        return m_out.at[owner, kind, pl.ds(first, cut)]

    items = [
        (memory.at[kind, pl.ds(index * cut, cut)], functools.partial(slot, kind, index * cut), kind + index == 0)
        for kind in range(2)
        for index in range(GROUP_CUTS)
    ]
    line = Line(owners, items, line_send, line_recv)
    square = Square(wout, wout_out, wout_send, wout_recv)
    for copy in loads:
        copy.wait()
    for item in range(len(items)):
        line.start(item)
    square.start()
    holds = [
        pltpu.make_async_copy(memory, m_out.at[me], hold_sems.at[0]),
        pltpu.make_async_copy(wout, wout_out.at[part], hold_sems.at[1]),
    ]
    for copy in holds:
        copy.start()
    for item in range(len(items)):
        line.start_wide(item)

    def rows_at(n):
        return pl.ds(pl.multiple_of(n * rows, rows), rows)

    def take(ref, index):
        return lambda n, lanes: ref[index, rows_at(n), lanes]

    def take_stat(ref, index):
        return lambda n: ref[index, n]

    for mask in range(half - 1, -1, -1):
        dest = flips(place, mask)
        for copy in to_pair(mask):
            copy.wait_recv()
        for copy in own_loads[mask]:
            copy.wait()

        def store(n, lanes, value):
            own[dest, rows_at(n), lanes] = value.astype(own.dtype)

        def store_stat(n, value):
            own_stat[dest, n] = value

        merge([take(own, dest), take(got, dest)], [take_stat(own_stat, dest), take_stat(got_stat, dest)],
              (per_owner, rows, span, store), store_stat, False)
        if mask:
            for copy in to_place(mask):
                copy.start()
    for item in range(len(items)):
        line.step(item, 1)
    for mask in range(1, half):
        for copy in to_place(mask):
            copy.wait_recv()

    def store(n, lanes, value):
        self_out[rows_at(n), lanes] = value.astype(self_out.dtype)

    merge(
        [take(own, place)] + [take(zin, mask) for mask in range(1, half)] + [lambda n, lanes: draft_ref[rows_at(n), lanes]],
        [take_stat(own_stat, place)] + [take_stat(zin_stat, mask) for mask in range(1, half)] + [lambda n: draft_stat[n]],
        (per_owner, rows, span, store), None, True)
    for distance in range(2, half):
        for item in range(len(items)):
            line.step(item, distance)
    square.forward()
    for item in range(len(items)):
        line.finish(item)
    square.finish()
    for mask in range(half):
        for copy in to_pair(mask):
            copy.wait_send()
        if mask:
            for copy in to_place(mask):
                copy.wait_send()
    for copy in holds:
        copy.wait()


def second_exchange(mix, stat, draft, draft_stat, memory, w_out, owners, parts):
    per_owner = draft_stat.shape[0]
    groups, local, both = memory.shape
    half = owners // 2
    rows_both, width = draft.shape
    mix = mix.reshape(owners, rows_both, width)
    stat = stat.reshape((owners,) + draft_stat.shape)
    sds = jax.ShapeDtypeStruct
    chunk = pltpu.VMEM((half, rows_both, width), mix.dtype)
    chunk_stat = pltpu.VMEM((half,) + draft_stat.shape, stat.dtype)
    items = 2 * GROUP_CUTS
    return pl.pallas_call(
        functools.partial(second_kernel, owners, parts, per_owner),
        in_specs=[ANY, ANY, WHOLE, WHOLE, ANY, ANY],
        out_specs=[WHOLE, ANY, ANY],
        out_shape=[
            sds(draft.shape, draft.dtype),
            sds((owners, 2, groups, local, both // 2 // parts), memory.dtype),
            sds((parts,) + w_out.shape, w_out.dtype),
        ],
        scratch_shapes=[
            chunk, chunk_stat, chunk, chunk_stat, chunk, chunk_stat,
            pltpu.VMEM((2, groups, local, both // 2 // parts), memory.dtype),
            pltpu.VMEM(w_out.shape, w_out.dtype),
            pltpu.SemaphoreType.DMA((3,)),
            pltpu.SemaphoreType.DMA((2, half)),
            pltpu.SemaphoreType.DMA((2,)),
            pltpu.SemaphoreType.DMA((2, half)),
            pltpu.SemaphoreType.DMA((2, half)),
            pltpu.SemaphoreType.DMA((2, half)),
            pltpu.SemaphoreType.DMA((2, half)),
            *line_sems(items, owners),
            *square_sems(parts),
        ],
        compiler_params=pltpu.CompilerParams(
            collective_id=2, has_side_effects=True, vmem_limit_bytes=(16 * MIB if half < 8 else 48 * MIB)
        ),
    )(mix, stat, draft, draft_stat, memory, w_out)


def cross_kernel(ids_ref, query_ref, memory_ref, out_ref):
    rows, span = query_ref.shape
    positions = memory_ref.shape[0] * memory_ref.shape[3]
    keys = memory_ref[:, 0, 0].reshape(positions, span)
    values = memory_ref[:, 1, 0].reshape(positions, span)
    own = own_lanes(rows, span // BUNDLE)
    stacked = jnp.where(own, jnp.concatenate([query_ref[...]] * BUNDLE, axis=0), jnp.zeros((), query_ref.dtype))
    scores = lax.dot_general(
        stacked, keys, (((1,), (1,)), ((), ())), preferred_element_type=jnp.float32
    )
    expo = jnp.exp(scores - jnp.max(scores, axis=-1, keepdims=True))
    total = jnp.sum(expo, axis=-1, keepdims=True)
    mix = jnp.dot(expo.astype(jnp.bfloat16), values, preferred_element_type=jnp.float32)
    mix = jnp.where(own, mix / total, 0.0)
    folded = mix[:rows]
    for part in range(1, BUNDLE):
        folded = folded + mix[part * rows : (part + 1) * rows]
    out_ref[...] = folded.astype(out_ref.dtype)


def cross_attention(query, memory, group_ids, rows):
    owners, _, _, local, span = memory.shape
    row_spec = pl.BlockSpec((rows, span), lambda n, ids: (n, 0))
    return pl.pallas_call(
        cross_kernel,
        grid_spec=pltpu.PrefetchScalarGridSpec(
            num_scalar_prefetch=1,
            grid=(group_ids.shape[0],),
            in_specs=[row_spec, pl.BlockSpec((owners, 2, 1, local, span), lambda n, ids: (0, 0, ids[n], 0, 0))],
            out_specs=row_spec,
        ),
        out_shape=jax.ShapeDtypeStruct(query.shape, query.dtype),
    )(group_ids, query, memory)


def per_device(
    tokens,
    kv_pool,
    page_table,
    cache_lens,
    draft_lengths,
    draft_parents,
    accepted_path,
    prompt_group,
    memory_kv,
    w_query,
    w_key,
    w_value,
    w_output,
    w_cross_query,
    w_cross_output,
    w_in,
    w_out,
):
    req_count, draft_len, model_width = tokens.shape
    owners = page_table.shape[0]
    parts = lax.axis_size("grp")
    head_dim = model_width // HEADS
    scale = head_dim ** (-0.5)
    col_index = lax.axis_index("grp")

    flat_rows = tokens.reshape(req_count * draft_len, model_width)
    query_rows = (jnp.dot(flat_rows, w_query, preferred_element_type=jnp.float32) * scale).astype(
        jnp.bfloat16
    )
    small = jnp.zeros((8, 128), jnp.int32)
    small = small.at[0, :req_count].set(cache_lens).at[1, :req_count].set(prompt_group)
    query_all, w_in_all, lens_all, groups_all = first_gather(query_rows, w_in, small, owners, parts)
    lens = lens_all[:, 0, :req_count].reshape(-1)
    group_ids = groups_all[:, 1, :req_count].reshape(-1)

    key_new = jnp.dot(flat_rows, w_key, preferred_element_type=jnp.float32).astype(jnp.bfloat16)
    value_new = jnp.dot(flat_rows, w_value, preferred_element_type=jnp.float32).astype(jnp.bfloat16)
    reach = reach_down(draft_parents)
    path_pick = (
        accepted_path[:, :, None] == jnp.arange(draft_len, dtype=jnp.int32)[None, None, :]
    ).astype(jnp.bfloat16)
    accepted_kv = jnp.concatenate(
        [
            jnp.einsum(
                "nij,njc->nic",
                path_pick,
                part.reshape(req_count, draft_len, model_width),
                preferred_element_type=jnp.float32,
            ).astype(jnp.bfloat16)
            for part in (key_new, value_new)
        ],
        axis=2,
    )
    mix, stat, draft_mix, draft_stat = page_partials(
        page_table.reshape(-1), lens, query_all, kv_pool, key_new, value_new, reach
    )
    self_mix, memory_all, w_out_all = second_exchange(
        mix, stat, draft_mix, draft_stat, memory_kv, w_out, owners, parts
    )
    first_norm = layer_norm(
        flat_rows.astype(jnp.float32)
        + jnp.dot(self_mix, w_output, preferred_element_type=jnp.float32)
    ).astype(jnp.bfloat16)
    cross_query = (
        jnp.dot(first_norm, w_cross_query, preferred_element_type=jnp.float32) * scale
    ).astype(jnp.bfloat16)
    span = model_width // parts
    shared = lax.all_to_all(cross_query, "grp", split_axis=1, concat_axis=0, tiled=True)
    shared = cross_attention(shared, memory_all, group_ids, draft_len)
    cross_mix = lax.all_to_all(shared, "grp", split_axis=0, concat_axis=1, tiled=True)
    second_norm = layer_norm(
        first_norm.astype(jnp.float32)
        + jnp.dot(cross_mix, w_cross_output, preferred_element_type=jnp.float32)
    ).astype(jnp.bfloat16)
    summed = jnp.zeros((req_count * draft_len, model_width), jnp.float32)
    for part in range(parts):
        hidden = jax.nn.gelu(
            jnp.dot(second_norm, w_in_all[part], preferred_element_type=jnp.float32), approximate=False
        ).astype(jnp.bfloat16)
        summed = summed + jnp.dot(hidden, w_out_all[part], preferred_element_type=jnp.float32)
    group_lengths = draft_lengths[0]
    own_counts = lax.dynamic_slice_in_dim(group_lengths, col_index * req_count, req_count, 0)
    live = (jnp.arange(draft_len, dtype=jnp.int32)[None, :] < own_counts[:, None]).reshape(
        req_count * draft_len
    )
    normed = layer_norm(second_norm.astype(jnp.float32) + summed).astype(jnp.bfloat16)
    result_rows = jnp.where(live[:, None], normed, jnp.zeros((), jnp.bfloat16))
    return (result_rows.reshape(req_count, draft_len, model_width), accepted_kv)


def solution(mesh):
    return jax.shard_map(
        per_device,
        mesh=mesh,
        in_specs=(
            P(("req", "grp"), None, None),
            P("req", "grp", None),
            P(None, "grp", None),
            P(("req", "grp")),
            P("req", None),
            P(("req", "grp"), None),
            P(("req", "grp"), None),
            P(("req", "grp")),
            P(None, "req", None),
            P(),
            P(),
            P(),
            P(),
            P(),
            P(),
            P(None, "grp"),
            P("grp", None),
        ),
        out_specs=(P(("req", "grp"), None, None), P(("req", "grp"), None, None)),
        check_vma=False,
    )
```

```python
import functools

import jax
import jax.numpy as jnp
from jax import lax
from jax.experimental import pallas as pl
from jax.experimental.pallas import tpu as pltpu
from jax.sharding import PartitionSpec as P

HEADS = 16
BUNDLE = 4
MESH = pl.DeviceIdType.MESH
ANY = pl.BlockSpec(memory_space=pl.ANY)
WHOLE = pl.BlockSpec(memory_space=pltpu.VMEM)
SCALARS = pl.BlockSpec(memory_space=pltpu.SMEM)
MIB = 1024 * 1024
RIGHT, LEFT, PAIR = 0, 1, 2

EPSILON = 1e-05
NEGATIVE = -1e30


def layer_norm(values):
    center = values - jnp.mean(values, axis=-1, keepdims=True)
    spread = jnp.mean(center * center, axis=-1, keepdims=True)
    return center * lax.rsqrt(spread + EPSILON)


def flip(index, bit):
    return index + bit - 2 * bit * ((index // bit) % 2)


def flips(index, mask):
    bit = 1
    while bit <= mask:
        if mask & bit:
            index = flip(index, bit)
        bit *= 2
    return index


class Line:
    def __init__(self, owners, items, send_sems, recv_sems):
        self.me = lax.axis_index("req")
        self.half = owners // 2
        self.place, self.side = self.me // 2, self.me % 2
        self.pair = flip(self.me, 1)
        self.right = lax.rem(self.place + 1, self.half) * 2 + self.side
        self.left = lax.rem(self.place + self.half - 1, self.half) * 2 + self.side
        self.items, self.send_sems, self.recv_sems = items, send_sems, recv_sems

    def copy(self, item, way, source, owner):
        target = (self.right, self.left, self.pair)[way]
        return pltpu.make_async_remote_copy(
            src_ref=source,
            dst_ref=self.items[item][1](owner),
            send_sem=self.send_sems.at[item, way, owner],
            recv_sem=self.recv_sems.at[item, owner],
            device_id={"req": target},
            device_id_type=MESH,
        )

    def arrive(self, item, owner):
        self.copy(item, PAIR, self.items[item][1](owner), owner).wait_recv()

    def both_ways(self, item, source, owner, act):
        pl.when(self.place < self.half - 1)(lambda: act(self.copy(item, RIGHT, source, owner)))
        pl.when(self.place > 0)(lambda: act(self.copy(item, LEFT, source, owner)))

    def owners_of(self, item, place):
        first = place * 2 + self.side
        return (first, flip(first, 1)) if self.items[item][2] else (first,)

    def start(self, item):
        source = self.items[item][0]
        self.both_ways(item, source, self.me, lambda copy: copy.start())
        if self.items[item][2]:
            self.copy(item, PAIR, source, self.me).start()

    def hand(self, item, distance):
        if self.items[item][2]:
            return
        if distance == 0:
            self.copy(item, PAIR, self.items[item][0], self.me).start()
            return

        def give(place):
            owner = place * 2 + self.side
            self.copy(item, PAIR, self.items[item][1](owner), owner).start()

        pl.when(self.place - distance >= 0)(lambda: give(self.place - distance))
        pl.when(self.place + distance < self.half)(lambda: give(self.place + distance))

    def start_wide(self, item):
        if self.items[item][2]:
            self.arrive(item, self.pair)
            block = self.items[item][1](self.pair)
            self.both_ways(item, block, self.pair, lambda copy: copy.start())

    def step(self, item, distance):
        def forward(place, way, more):
            for owner in self.owners_of(item, place):
                self.arrive(item, owner)
                block = self.items[item][1](owner)
                pl.when(more)(lambda: self.copy(item, way, block, owner).start())

        pl.when(self.place - distance >= 0)(
            lambda: forward(self.place - distance, RIGHT, self.place < self.half - 1)
        )
        pl.when(self.place + distance < self.half)(
            lambda: forward(self.place + distance, LEFT, self.place > 0)
        )

    def finish(self, item):
        source, target, wide = self.items[item]
        if not wide:
            for place in range(self.half):
                self.arrive(item, place * 2 + flip(self.side, 1))
        self.copy(item, PAIR, source, self.me).wait_send()
        self.both_ways(item, source, self.me, lambda copy: copy.wait_send())
        if wide:
            self.both_ways(item, source, self.pair, lambda copy: copy.wait_send())

        def sent(place, way, more):
            for owner in self.owners_of(item, place):
                pl.when(more)(lambda: self.copy(item, way, source, owner).wait_send())
                if not wide:
                    self.copy(item, PAIR, source, owner).wait_send()

        for distance in range(1, self.half):
            pl.when(self.place - distance >= 0)(
                lambda: sent(self.place - distance, RIGHT, self.place < self.half - 1)
            )
            pl.when(self.place + distance < self.half)(
                lambda: sent(self.place + distance, LEFT, self.place > 0)
            )


class Square:
    def __init__(self, source, out, send_sems, recv_sems):
        self.part = lax.axis_index("grp")
        self.near, self.far = flip(self.part, 1), flip(self.part, 2)
        self.source, self.out, self.send_sems, self.recv_sems = source, out, send_sems, recv_sems

    def copy(self, hop, source, owner):
        return pltpu.make_async_remote_copy(
            src_ref=source,
            dst_ref=self.out.at[owner],
            send_sem=self.send_sems.at[hop],
            recv_sem=self.recv_sems.at[owner],
            device_id={"grp": (self.far, self.near, self.near)[hop]},
            device_id_type=MESH,
        )

    def start(self):
        self.copy(0, self.source, self.part).start()
        self.copy(1, self.source, self.part).start()

    def forward(self):
        block = self.out.at[self.far]
        self.copy(2, block, self.far).wait_recv()
        self.copy(2, block, self.far).start()

    def finish(self):
        self.copy(1, self.source, self.near).wait_recv()
        self.copy(2, self.source, flip(self.far, 1)).wait_recv()
        self.copy(0, self.source, self.part).wait_send()
        self.copy(1, self.source, self.part).wait_send()
        self.copy(2, self.source, self.far).wait_send()


def meet(owners, parts):
    barrier = pltpu.get_barrier_semaphore()
    me, part = lax.axis_index("req"), lax.axis_index("grp")
    for offset in range(1, owners):
        other = lax.rem(me + offset, owners)
        pl.semaphore_signal(barrier, inc=1, device_id={"req": other}, device_id_type=MESH)
    for offset in range(1, parts):
        other = lax.rem(part + offset, parts)
        pl.semaphore_signal(barrier, inc=1, device_id={"grp": other}, device_id_type=MESH)
    pl.semaphore_wait(barrier, owners + parts - 2)


def line_sems(items, owners):
    return [pltpu.SemaphoreType.DMA((items, 3, owners)), pltpu.SemaphoreType.DMA((items, owners))]


def square_sems(parts):
    return [pltpu.SemaphoreType.DMA((3,)), pltpu.SemaphoreType.DMA((parts,))]


CUTS = 8


def project(rows, weight_ref, out, scale=None, tile=256):
    for low in range(0, weight_ref.shape[1], tile):
        value = jnp.dot(rows, weight_ref[:, low : low + tile], preferred_element_type=jnp.float32)
        if scale is not None:
            value = value * scale
        out[:, low : low + tile] = value.astype(out.dtype)


def first_kernel(owners, parts, tokens_ref, wq_ref, wk_ref, wv_ref, parents_ref, path_ref, win_ref, small_ref,
                 q_out, win_out, lens_out, grps_out, accepted_out, draft_out, draft_stat,
                 tokens, wq, wk, wv, query, keys, values, win, load_sems, hold_sems, line_send, line_recv,
                 win_send, win_recv, small_send, small_recv):
    me, part = lax.axis_index("req"), lax.axis_index("grp")
    loads = [
        pltpu.make_async_copy(source, target, load_sems.at[index])
        for index, (source, target) in enumerate(
            ((tokens_ref, tokens), (wq_ref, wq), (win_ref, win), (wk_ref, wk), (wv_ref, wv))
        )
    ]
    for copy in loads:
        copy.start()
    width = tokens.shape[1]
    per_owner, rows = parents_ref.shape
    head_dim = width // HEADS
    loads[0].wait()
    loads[1].wait()
    project(tokens[...], wq, query, head_dim ** (-0.5))
    meet(owners, parts)
    cut_rows = query.shape[0] // CUTS

    def slot(cut, owner):
        return q_out.at[owner, pl.ds(cut * cut_rows, cut_rows)]

    items = [
        (query.at[pl.ds(cut * cut_rows, cut_rows)], functools.partial(slot, cut), cut == 0) for cut in range(CUTS)
    ]
    line = Line(owners, items, line_send, line_recv)
    square = Square(win, win_out, win_send, win_recv)
    for item in range(CUTS):
        line.start(item)
        line.hand(item, 0)
    loads[2].wait()
    square.start()
    smalls = []
    for offset in range(1, owners):
        smalls.append(pltpu.make_async_remote_copy(
            src_ref=small_ref, dst_ref=lens_out.at[me],
            send_sem=small_send.at[offset], recv_sem=small_recv.at[offset],
            device_id={"req": lax.rem(me + offset, owners)}, device_id_type=MESH))
    for offset in range(1, parts):
        smalls.append(pltpu.make_async_remote_copy(
            src_ref=small_ref, dst_ref=grps_out.at[part],
            send_sem=small_send.at[owners + offset], recv_sem=small_recv.at[owners + offset],
            device_id={"grp": lax.rem(part + offset, parts)}, device_id_type=MESH))
    for copy in smalls:
        copy.start()
    holds = [
        pltpu.make_async_copy(query, q_out.at[me], hold_sems.at[0]),
        pltpu.make_async_copy(win, win_out.at[part], hold_sems.at[1]),
        pltpu.make_async_copy(small_ref, lens_out.at[me], hold_sems.at[2]),
        pltpu.make_async_copy(small_ref, grps_out.at[part], hold_sems.at[3]),
    ]
    for copy in holds:
        copy.start()
    loads[3].wait()
    project(tokens[...], wk, keys)
    for item in range(CUTS):
        line.start_wide(item)

    def advance(distance):
        for item in range(CUTS):
            line.step(item, distance)
            line.hand(item, distance)

    loads[4].wait()
    if owners > 2:
        advance(1)
    project(tokens[...], wv, values)
    own = own_lanes(rows, head_dim)
    square_shape = (rows, rows)
    down = lax.broadcasted_iota(jnp.int32, square_shape, 0)
    eye = (down == lax.broadcasted_iota(jnp.int32, square_shape, 1)).astype(jnp.float32).astype(jnp.bfloat16)
    turn = (((1,), (1,)), ((), ()))
    span = BUNDLE * head_dim
    bundles = [slice(low, low + span) for low in range(0, width, span)]

    def drafts(n, carry):
        at = pl.ds(pl.multiple_of(n * rows, rows), rows)
        linked = (parents_ref[pl.ds(n, 1), :] == down).astype(jnp.float32).astype(jnp.bfloat16)
        closure = linked + eye
        for sweep_index in range((rows - 1).bit_length()):
            closure = jnp.minimum(jnp.dot(closure, closure, preferred_element_type=jnp.float32), 1.0)
            closure = closure.astype(jnp.bfloat16)
        reach = lax.dot_general(eye, closure, turn, preferred_element_type=jnp.float32)
        mixes, stats = attend(
            [query[at, lanes] for lanes in bundles],
            [keys[at, lanes] for lanes in bundles],
            [values[at, lanes] for lanes in bundles],
            jnp.concatenate([reach] * BUNDLE, axis=0) > 0.5, own)
        for lanes, mix in zip(bundles, mixes):
            draft_out[at, lanes] = mix.astype(draft_out.dtype)
        draft_stat[n] = stats
        chosen = (path_ref[pl.ds(n, 1), :] == down).astype(jnp.float32).astype(jnp.bfloat16)
        chosen = lax.dot_general(eye, chosen, turn, preferred_element_type=jnp.float32).astype(jnp.bfloat16)
        for low in range(0, width, 256):
            for offset, source in ((0, keys), (width, values)):
                picked = jnp.dot(chosen, source[at, low : low + 256], preferred_element_type=jnp.float32)
                accepted_out[n, :, offset + low : offset + low + 256] = picked.astype(accepted_out.dtype)
        return carry

    lax.fori_loop(0, per_owner, drafts, 0)
    for distance in range(2, owners // 2):
        advance(distance)
    square.forward()
    for item in range(CUTS):
        line.finish(item)
    square.finish()
    for copy in smalls + holds:
        copy.wait()


def first_gather(tokens, w_query, w_key, w_value, parents, path, w_in, small, owners, parts):
    sds = jax.ShapeDtypeStruct
    per_owner, rows = parents.shape
    weight = pltpu.VMEM(w_query.shape, w_query.dtype)
    block = pltpu.VMEM(tokens.shape, tokens.dtype)
    return pl.pallas_call(
        functools.partial(first_kernel, owners, parts),
        in_specs=[ANY] * 4 + [WHOLE] * 2 + [ANY] * 2,
        out_specs=[ANY] * 4 + [WHOLE] * 3,
        out_shape=[
            sds((owners,) + tokens.shape, tokens.dtype),
            sds((parts,) + w_in.shape, w_in.dtype),
            sds((owners,) + small.shape, small.dtype),
            sds((parts,) + small.shape, small.dtype),
            sds((per_owner, rows, 2 * tokens.shape[1]), tokens.dtype),
            sds(tokens.shape, tokens.dtype),
            sds((per_owner, 2 * (HEADS // BUNDLE), BUNDLE * rows), jnp.float32),
        ],
        scratch_shapes=[
            block, weight, weight, weight, block, block, block,
            pltpu.VMEM(w_in.shape, w_in.dtype),
            pltpu.SemaphoreType.DMA((5,)),
            pltpu.SemaphoreType.DMA((4,)),
            *line_sems(CUTS, owners),
            *square_sems(parts),
            pltpu.SemaphoreType.DMA((owners + parts,)),
            pltpu.SemaphoreType.DMA((owners + parts,)),
        ],
        compiler_params=pltpu.CompilerParams(
            collective_id=1, has_side_effects=True, vmem_limit_bytes=60 * MIB
        ),
    )(tokens, w_query, w_key, w_value, parents, path, w_in, small)


def own_lanes(rows, head_dim):
    shape = (BUNDLE * rows, BUNDLE * head_dim)
    row = lax.broadcasted_iota(jnp.int32, shape, 0) // rows
    lane = lax.broadcasted_iota(jnp.int32, shape, 1) // head_dim
    return row == lane


def attend(queries, keys, values, seen, own, final=False):
    rows = queries[0].shape[0]
    scores = []
    for query, key in zip(queries, keys):
        stacked = jnp.where(own, jnp.concatenate([query] * BUNDLE, axis=0), jnp.zeros((), query.dtype))
        scores.append(
            lax.dot_general(stacked, key, (((1,), (1,)), ((), ())), preferred_element_type=jnp.float32)
        )
    expos, tops, totals = [], [], []
    for score in scores:
        if seen is not None:
            score = jnp.where(seen, score, NEGATIVE)
        top = jnp.max(score, axis=1, keepdims=True)
        expo = jnp.exp(score - top)
        expos.append(expo.astype(jnp.bfloat16))
        tops.append(top)
        totals.append(jnp.sum(expo, axis=1, keepdims=True))
    mixes = []
    for expo, value, total in zip(expos, values, totals):
        mix = jnp.dot(expo, value, preferred_element_type=jnp.float32)
        mix = jnp.where(own, mix / total if final else mix, 0.0)
        folded = mix[:rows]
        for part in range(1, BUNDLE):
            folded = folded + mix[part * rows : (part + 1) * rows]
        mixes.append(folded)
    if final:
        return mixes
    lane = lax.broadcasted_iota(jnp.int32, (BUNDLE * rows, 128), 1)
    stats = jnp.zeros((BUNDLE * rows, 128), jnp.float32)
    for index, column in enumerate(tops + totals):
        stats = jnp.where(lane == index, column, stats)
    return mixes, jnp.transpose(stats)[: 2 * len(queries)]


def pages_kernel(per_req, table_ref, lens_ref, query_ref, pool_ref, mix_out, stat_out):
    me = lax.axis_index("req")
    width = query_ref.shape[1]
    pool_pages, page = pool_ref.shape[0], pool_ref.shape[1]
    requests = table_ref.shape[0] // per_req
    rows = query_ref.shape[0] // requests
    head_dim = width // HEADS
    span = BUNDLE * head_dim
    own = own_lanes(rows, head_dim)
    bundles = [slice(low, low + span) for low in range(0, width, span)]

    def rows_at(n):
        return pl.ds(pl.multiple_of(n * rows, rows), rows)

    def store(out, stat, n, result):
        mixes, stats = result
        for lanes, mix in zip(bundles, mixes):
            out[rows_at(n), lanes] = mix.astype(out.dtype)
        stat[n] = stats

    def one(n, carry):
        length = lens_ref[n]
        count = jnp.int32(0)
        slots = [jnp.int32(0)] * per_req
        starts = [jnp.int32(0)] * per_req
        for place in range(per_req):
            entry = table_ref[n * per_req + place]
            hit = (entry // pool_pages == me) & (place * page < length)
            for k in range(place + 1):
                here = hit & (count == k)
                slots[k] = jnp.where(here, entry % pool_pages, slots[k])
                starts[k] = jnp.where(here, length - place * page, starts[k])
            count = count + hit.astype(jnp.int32)

        def work(uses):
            lane = lax.broadcasted_iota(jnp.int32, (BUNDLE * rows, uses * page), 1)
            limit = jnp.zeros_like(lane)
            for k in range(uses):
                limit = jnp.where(lane // page == k, k * page + starts[k], limit)
            seen = lane < limit
            at = rows_at(n)
            store(mix_out, stat_out, n, attend(
                [query_ref[at, lanes] for lanes in bundles],
                [jnp.concatenate([pool_ref[slots[k], :, lanes] for k in range(uses)], axis=0) for lanes in bundles],
                [
                    jnp.concatenate(
                        [pool_ref[slots[k], :, width + lanes.start : width + lanes.stop] for k in range(uses)], axis=0
                    )
                    for lanes in bundles
                ],
                seen, own))

        @pl.when(count == 0)
        def _():
            mix_out[rows_at(n), :] = jnp.zeros((rows, width), mix_out.dtype)
            stat_out[n, pl.ds(0, BUNDLE), :] = jnp.full((BUNDLE, BUNDLE * rows), NEGATIVE, jnp.float32)
            stat_out[n, pl.ds(BUNDLE, BUNDLE), :] = jnp.zeros((BUNDLE, BUNDLE * rows), jnp.float32)

        pl.when(count == 1)(lambda: work(1))
        pl.when(count == 2)(lambda: work(2))
        pl.when((count > 2) & (count <= 4))(lambda: work(4))
        pl.when(count > 4)(lambda: work(per_req))
        return carry

    lax.fori_loop(0, requests, one, 0)


def page_partials(table, lens, query_all, pool):
    owners, rows_both, width = query_all.shape
    requests = lens.shape[0]
    rows = rows_both * owners // requests
    sds = jax.ShapeDtypeStruct
    return pl.pallas_call(
        functools.partial(pages_kernel, table.shape[0] // requests),
        in_specs=[SCALARS, SCALARS] + [WHOLE] * 2,
        out_specs=[WHOLE] * 2,
        out_shape=[
            sds((requests * rows, width), query_all.dtype),
            sds((requests, 2 * (HEADS // BUNDLE), BUNDLE * rows), jnp.float32),
        ],
        compiler_params=pltpu.CompilerParams(vmem_limit_bytes=60 * MIB),
    )(table, lens, query_all.reshape(requests * rows, width), pool)


def widen(weights, eye, ones):
    high = weights.astype(jnp.bfloat16)
    low = (weights - high.astype(jnp.float32)).astype(jnp.bfloat16)
    zero = jnp.zeros((), jnp.bfloat16)
    spread = jnp.concatenate(
        [jnp.where(eye, jnp.broadcast_to(part, eye.shape), zero) for part in (high, low)], axis=1
    )
    return jnp.dot(spread, ones, preferred_element_type=jnp.float32)


def merge(sources, stats, out, stat_out, last):
    per_owner, rows, span, store = out
    lanes_of = (rows, BUNDLE * rows)
    eye = lax.broadcasted_iota(jnp.int32, lanes_of, 1) % rows == lax.broadcasted_iota(jnp.int32, lanes_of, 0)
    shape = (2 * BUNDLE * rows, span)
    row_head = (lax.broadcasted_iota(jnp.int32, shape, 0) % (BUNDLE * rows)) // rows
    ones = (row_head == lax.broadcasted_iota(jnp.int32, shape, 1) // (span // BUNDLE)).astype(jnp.float32)
    ones = ones.astype(jnp.bfloat16)

    def one(n, carry):
        read = [stat(n) for stat in stats]
        tops = [value[:BUNDLE] for value in read]
        sums = [value[BUNDLE:] for value in read]
        top = functools.reduce(jnp.maximum, tops)
        scales = [jnp.exp(value - top) for value in tops]
        total = functools.reduce(jnp.add, [scale * part for scale, part in zip(scales, sums)])
        if last:
            scales = [scale / total for scale in scales]
        else:
            stat_out(n, jnp.concatenate([top, total], axis=0))
        for bundle in range(HEADS // BUNDLE):
            lanes = slice(bundle * span, (bundle + 1) * span)
            mixed = functools.reduce(
                jnp.add,
                [
                    widen(scale[bundle : bundle + 1], eye, ones) * source(n, lanes).astype(jnp.float32)
                    for scale, source in zip(scales, sources)
                ],
            )
            store(n, lanes, mixed)
        return carry

    lax.fori_loop(0, per_owner, one, 0)


GROUP_CUTS = 2


def normalise(source, out):
    rows = source.shape[0]
    step = 64
    for low in range(0, rows, step):
        out[low : low + step, :] = layer_norm(source[low : low + step, :]).astype(out.dtype)


def second_kernel(owners, parts, mix_ref, stat_ref, draft_ref, draft_stat, tokens_ref, memory_ref, wout_ref,
                  wo_ref, wcq_ref, norm_out, shared_out, m_out, wout_out,
                  own, own_stat, got, got_stat, zin, zin_stat, memory, wout, wo, wcq, self_mix, total, cross,
                  load_sems, own_sems, hold_sems, y_send, y_recv, z_send, z_recv,
                  line_send, line_recv, wout_send, wout_recv, share_send, share_recv):
    me, part = lax.axis_index("req"), lax.axis_index("grp")
    half = owners // 2
    place, side = me // 2, me % 2
    pair = flip(me, 1)
    per_owner = draft_stat.shape[0]
    width = draft_ref.shape[1]
    rows = draft_ref.shape[0] // per_owner
    span = BUNDLE * (width // HEADS)
    groups = memory_ref.shape[0]
    wide = memory_ref.shape[2] // 2
    lanes_in = wide // parts
    order = list(range(half - 1, -1, -1))

    own_loads = {}
    for mask in order:
        dest = flips(place, mask)
        own_loads[mask] = [
            pltpu.make_async_copy(mix_ref.at[dest * 2 + side], own.at[dest], own_sems.at[0, mask]),
            pltpu.make_async_copy(stat_ref.at[dest * 2 + side], own_stat.at[dest], own_sems.at[1, mask]),
        ]
        for copy in own_loads[mask]:
            copy.start()
    loads = []
    for kind in range(2):
        lanes = pl.ds(pl.multiple_of(kind * wide + part * lanes_in, 128), lanes_in)
        loads.append(pltpu.make_async_copy(memory_ref.at[:, :, lanes], memory.at[kind], load_sems.at[kind]))
    loads.append(pltpu.make_async_copy(wout_ref, wout, load_sems.at[2]))
    weights = [
        pltpu.make_async_copy(wo_ref, wo, load_sems.at[3]),
        pltpu.make_async_copy(wcq_ref, wcq, load_sems.at[4]),
    ]
    for copy in loads + weights:
        copy.start()
    meet(owners, parts)

    def to_pair(mask):
        dest = flips(place, mask)
        far = dest * 2 + flip(side, 1)
        return [
            pltpu.make_async_remote_copy(
                src_ref=source.at[far], dst_ref=target.at[dest], send_sem=y_send.at[k, mask],
                recv_sem=y_recv.at[k, mask], device_id={"req": pair}, device_id_type=MESH)
            for k, (source, target) in enumerate(((mix_ref, got), (stat_ref, got_stat)))
        ]

    def to_place(mask):
        dest = flips(place, mask)
        return [
            pltpu.make_async_remote_copy(
                src_ref=source.at[dest], dst_ref=target.at[mask], send_sem=z_send.at[k, mask],
                recv_sem=z_recv.at[k, mask], device_id={"req": dest * 2 + side}, device_id_type=MESH)
            for k, (source, target) in enumerate(((own, zin), (own_stat, zin_stat)))
        ]

    for mask in order[:2]:
        for copy in to_pair(mask):
            copy.start()

    cut = groups // GROUP_CUTS

    def slot(kind, first, owner):
        return m_out.at[owner, kind, pl.ds(first, cut)]

    items = [
        (memory.at[kind, pl.ds(index * cut, cut)], functools.partial(slot, kind, index * cut), kind + index == 0)
        for kind in range(2)
        for index in range(GROUP_CUTS)
    ]
    line = Line(owners, items, line_send, line_recv)
    square = Square(wout, wout_out, wout_send, wout_recv)
    for copy in loads:
        copy.wait()
    for item in range(len(items)):
        line.start(item)
    square.start()
    holds = [
        pltpu.make_async_copy(memory, m_out.at[me], hold_sems.at[0]),
        pltpu.make_async_copy(wout, wout_out.at[part], hold_sems.at[1]),
    ]
    for copy in holds:
        copy.start()

    def rows_at(n):
        return pl.ds(pl.multiple_of(n * rows, rows), rows)

    def take(ref, index):
        return lambda n, lanes: ref[index, rows_at(n), lanes]

    def take_stat(ref, index):
        return lambda n: ref[index, n]

    for turn, mask in enumerate(order):
        dest = flips(place, mask)
        for copy in to_pair(mask):
            copy.wait_recv()
        if turn + 2 < half:
            for copy in to_pair(order[turn + 2]):
                copy.start()
        for copy in own_loads[mask]:
            copy.wait()

        def store(n, lanes, value):
            own[dest, rows_at(n), lanes] = value.astype(own.dtype)

        def store_stat(n, value):
            own_stat[dest, n] = value

        merge([take(own, dest), take(got, dest)], [take_stat(own_stat, dest), take_stat(got_stat, dest)],
              (per_owner, rows, span, store), store_stat, False)
        if mask:
            for copy in to_place(mask):
                copy.start()
        if turn == 0:
            for item in range(len(items)):
                line.start_wide(item)
        elif turn < half - 1:
            for item in range(len(items)):
                line.step(item, turn)
        if turn == half - 2 or half == 1:
            for distance in range(turn + 1):
                for item in range(len(items)):
                    line.hand(item, distance)
    for mask in range(1, half):
        for copy in to_place(mask):
            copy.wait_recv()

    def store(n, lanes, value):
        self_mix[rows_at(n), lanes] = value.astype(self_mix.dtype)

    merge(
        [take(own, place)] + [take(zin, mask) for mask in range(1, half)] + [lambda n, lanes: draft_ref[rows_at(n), lanes]],
        [take_stat(own_stat, place)] + [take_stat(zin_stat, mask) for mask in range(1, half)] + [lambda n: draft_stat[n]],
        (per_owner, rows, span, store), None, True)
    last = half - 1
    if last > 0:
        for item in range(len(items)):
            line.step(item, last)
            line.hand(item, last)
    square.forward()

    for copy in weights:
        copy.wait()
    for low in range(0, width, 256):
        lanes = slice(low, low + 256)
        total[:, lanes] = tokens_ref[:, lanes].astype(jnp.float32) + jnp.dot(
            self_mix[...], wo[:, lanes], preferred_element_type=jnp.float32
        )
    normalise(total, norm_out)

    def share(offset):
        other = lax.rem(part + offset, parts)
        return pltpu.make_async_remote_copy(
            src_ref=cross.at[offset], dst_ref=shared_out.at[part], send_sem=share_send.at[offset],
            recv_sem=share_recv.at[offset], device_id={"grp": other}, device_id_type=MESH)

    scale = (width // HEADS) ** (-0.5)
    for offset in list(range(1, parts)) + [0]:
        other = lax.rem(part + offset, parts)
        lanes = pl.ds(pl.multiple_of(other * lanes_in, 128), lanes_in)
        value = jnp.dot(norm_out[...], wcq[:, lanes], preferred_element_type=jnp.float32) * scale
        if offset:
            cross[offset] = value.astype(cross.dtype)
            share(offset).start()
        else:
            shared_out[part] = value.astype(cross.dtype)

    for item in range(len(items)):
        line.finish(item)
    square.finish()
    for offset in range(1, parts):
        share(offset).wait()
    for mask in range(half):
        for copy in to_pair(mask):
            copy.wait_send()
        if mask:
            for copy in to_place(mask):
                copy.wait_send()
    for copy in holds:
        copy.wait()


def second_exchange(mix, stat, draft, draft_stat, tokens, memory, w_out, w_output, w_cross_query, owners, parts):
    groups, local, both = memory.shape
    half = owners // 2
    rows_both, width = draft.shape
    mix = mix.reshape(owners, rows_both, width)
    stat = stat.reshape((owners,) + draft_stat.shape)
    sds = jax.ShapeDtypeStruct
    chunk = pltpu.VMEM((half, rows_both, width), mix.dtype)
    chunk_stat = pltpu.VMEM((half,) + draft_stat.shape, stat.dtype)
    weight = pltpu.VMEM(w_output.shape, w_output.dtype)
    items = 2 * GROUP_CUTS
    share = (parts, rows_both, width // parts)
    return pl.pallas_call(
        functools.partial(second_kernel, owners, parts),
        in_specs=[ANY, ANY, WHOLE, WHOLE, WHOLE] + [ANY] * 4,
        out_specs=[WHOLE, WHOLE, ANY, ANY],
        out_shape=[
            sds(draft.shape, draft.dtype),
            sds(share, draft.dtype),
            sds((owners, 2, groups, local, both // 2 // parts), memory.dtype),
            sds((parts,) + w_out.shape, w_out.dtype),
        ],
        scratch_shapes=[
            chunk, chunk_stat, chunk, chunk_stat, chunk, chunk_stat,
            pltpu.VMEM((2, groups, local, both // 2 // parts), memory.dtype),
            pltpu.VMEM(w_out.shape, w_out.dtype),
            weight, weight,
            pltpu.VMEM(draft.shape, draft.dtype),
            pltpu.VMEM(draft.shape, jnp.float32),
            pltpu.VMEM(share, draft.dtype),
            pltpu.SemaphoreType.DMA((5,)),
            pltpu.SemaphoreType.DMA((2, half)),
            pltpu.SemaphoreType.DMA((2,)),
            pltpu.SemaphoreType.DMA((2, half)),
            pltpu.SemaphoreType.DMA((2, half)),
            pltpu.SemaphoreType.DMA((2, half)),
            pltpu.SemaphoreType.DMA((2, half)),
            *line_sems(items, owners),
            *square_sems(parts),
            pltpu.SemaphoreType.DMA((parts,)),
            pltpu.SemaphoreType.DMA((parts,)),
        ],
        compiler_params=pltpu.CompilerParams(
            collective_id=2, has_side_effects=True, vmem_limit_bytes=60 * MIB
        ),
    )(mix, stat, draft, draft_stat, tokens, memory, w_out, w_output, w_cross_query)


def gelu(values):
    return values * (1.0 + lax.erf(values * (0.5**0.5))) * 0.5


def third_kernel(owners, parts, ids_ref, counts_ref, shared_ref, norm_ref, m_ref, wco_ref, win_ref, wout_ref, out_ref,
                 memory, wco, win, wout, mixed, sent, total, second, load_sems, win_sems, wout_sems, back_send, back_recv):
    part = lax.axis_index("grp")
    loads = [
        pltpu.make_async_copy(m_ref, memory, load_sems.at[0]),
        pltpu.make_async_copy(wco_ref, wco, load_sems.at[1]),
    ]
    streams = [
        [pltpu.make_async_copy(source.at[index], target.at[index], sems.at[index]) for index in range(parts)]
        for source, target, sems in ((win_ref, win, win_sems), (wout_ref, wout, wout_sems))
    ]
    for copy in loads:
        copy.start()
    for pieces in zip(*streams):
        for copy in pieces:
            copy.start()
    barrier = pltpu.get_barrier_semaphore()
    for offset in range(1, parts):
        other = lax.rem(part + offset, parts)
        pl.semaphore_signal(barrier, inc=1, device_id={"grp": other}, device_id_type=MESH)
    pl.semaphore_wait(barrier, parts - 1)

    rows_both, span = shared_ref.shape[1:]
    width = span * parts
    per_owner = ids_ref.shape[0] // parts
    rows = rows_both // per_owner
    positions = memory.shape[0] * memory.shape[3]
    own = own_lanes(rows, span // BUNDLE)
    loads[0].wait()

    def back(offset):
        other = lax.rem(part + offset, parts)
        return pltpu.make_async_remote_copy(
            src_ref=sent.at[offset], dst_ref=mixed.at[part], send_sem=back_send.at[offset],
            recv_sem=back_recv.at[offset], device_id={"grp": other}, device_id_type=MESH)

    for offset in list(range(1, parts)) + [0]:
        other = lax.rem(part + offset, parts)
        groups = [ids_ref[other * per_owner + n] for n in range(per_owner)]
        results = attend(
            [shared_ref[other, n * rows : (n + 1) * rows, :] for n in range(per_owner)],
            [memory[:, 0, group].reshape(positions, span) for group in groups],
            [memory[:, 1, group].reshape(positions, span) for group in groups],
            None, own, True)
        for n, result in enumerate(results):
            at = slice(n * rows, (n + 1) * rows)
            if offset:
                sent[offset, at, :] = result.astype(sent.dtype)
            else:
                mixed[part, at, :] = result.astype(sent.dtype)
        if offset:
            back(offset).start()
    loads[1].wait()
    for offset in range(1, parts):
        back(offset).wait_recv()
    for low in range(0, width, 256):
        lanes = slice(low, low + 256)
        value = norm_ref[:, lanes].astype(jnp.float32)
        for index in range(parts):
            value = value + jnp.dot(
                mixed[index], wco[index * span : (index + 1) * span, lanes], preferred_element_type=jnp.float32
            )
        total[:, lanes] = value
    normalise(total, second)
    total[...] = second[...].astype(jnp.float32)
    for index in range(parts):
        streams[0][index].wait()
        streams[1][index].wait()

    def feed(index, carry):
        hidden = []
        for low in range(0, win.shape[2], 256):
            value = jnp.dot(second[...], win[index, :, low : low + 256], preferred_element_type=jnp.float32)
            hidden.append(gelu(value).astype(jnp.bfloat16))
        hidden = jnp.concatenate(hidden, axis=1)
        for low in range(0, width, 256):
            lanes = slice(low, low + 256)
            total[:, lanes] += jnp.dot(hidden, wout[index, :, lanes], preferred_element_type=jnp.float32)
        return carry

    lax.fori_loop(0, parts, feed, 0)
    position = lax.broadcasted_iota(jnp.int32, (rows, width), 0)
    for n in range(per_owner):
        at = slice(n * rows, (n + 1) * rows)
        normed = layer_norm(total[at, :])
        live = position < counts_ref[part * per_owner + n]
        out_ref[at, :] = jnp.where(live, normed, 0.0).astype(out_ref.dtype)
    for offset in range(1, parts):
        back(offset).wait_send()


def third_stage(ids, counts, shared, norm, memory, w_cross_output, w_in, w_out, owners, parts):
    any_vmem = lambda array: pltpu.VMEM(array.shape, array.dtype)
    return pl.pallas_call(
        functools.partial(third_kernel, owners, parts),
        in_specs=[SCALARS, SCALARS, WHOLE, WHOLE] + [ANY] * 4,
        out_specs=WHOLE,
        out_shape=jax.ShapeDtypeStruct(norm.shape, norm.dtype),
        scratch_shapes=[
            any_vmem(memory), any_vmem(w_cross_output), any_vmem(w_in), any_vmem(w_out),
            any_vmem(shared), any_vmem(shared),
            pltpu.VMEM(norm.shape, jnp.float32),
            any_vmem(norm),
            pltpu.SemaphoreType.DMA((2,)),
            pltpu.SemaphoreType.DMA((parts,)),
            pltpu.SemaphoreType.DMA((parts,)),
            pltpu.SemaphoreType.DMA((parts,)),
            pltpu.SemaphoreType.DMA((parts,)),
        ],
        compiler_params=pltpu.CompilerParams(
            collective_id=3, has_side_effects=True, vmem_limit_bytes=60 * MIB
        ),
    )(ids, counts, shared, norm, memory, w_cross_output, w_in, w_out)


def per_device(
    tokens,
    kv_pool,
    page_table,
    cache_lens,
    draft_lengths,
    draft_parents,
    accepted_path,
    prompt_group,
    memory_kv,
    w_query,
    w_key,
    w_value,
    w_output,
    w_cross_query,
    w_cross_output,
    w_in,
    w_out,
):
    req_count, draft_len, model_width = tokens.shape
    owners = page_table.shape[0]
    parts = lax.axis_size("grp")
    flat_rows = tokens.reshape(req_count * draft_len, model_width)
    small = jnp.pad(jnp.stack([cache_lens, prompt_group]), ((0, 6), (0, 128 - req_count)))
    query_all, w_in_all, lens_all, groups_all, accepted_kv, draft_mix, draft_stat = first_gather(
        flat_rows, w_query, w_key, w_value, draft_parents, accepted_path, w_in, small, owners, parts
    )
    lens = lens_all[:, 0, :req_count].reshape(-1)
    group_ids = groups_all[:, 1, :req_count].reshape(-1)
    mix, stat = page_partials(page_table.reshape(-1), lens, query_all, kv_pool)
    first_norm, shared, memory_all, w_out_all = second_exchange(
        mix, stat, draft_mix, draft_stat, flat_rows, memory_kv, w_out, w_output, w_cross_query, owners, parts
    )
    result = third_stage(
        group_ids, draft_lengths[0], shared, first_norm, memory_all, w_cross_output, w_in_all, w_out_all, owners, parts
    )
    return (result.reshape(req_count, draft_len, model_width), accepted_kv)


def solution(mesh):
    return jax.shard_map(
        per_device,
        mesh=mesh,
        in_specs=(
            P(("req", "grp"), None, None),
            P("req", "grp", None),
            P(None, "grp", None),
            P(("req", "grp")),
            P("req", None),
            P(("req", "grp"), None),
            P(("req", "grp"), None),
            P(("req", "grp")),
            P(None, "req", None),
            P(),
            P(),
            P(),
            P(),
            P(),
            P(),
            P(None, "grp"),
            P("grp", None),
        ),
        out_specs=(P(("req", "grp"), None, None), P(("req", "grp"), None, None)),
        check_vma=False,
    )
```

```python
import functools

import jax
import jax.numpy as jnp
from jax import lax
from jax.experimental import pallas as pl
from jax.experimental.pallas import tpu as pltpu
from jax.sharding import PartitionSpec as P

HEADS = 16
BUNDLE = 4
MESH = pl.DeviceIdType.MESH
ANY = pl.BlockSpec(memory_space=pl.ANY)
WHOLE = pl.BlockSpec(memory_space=pltpu.VMEM)
SCALARS = pl.BlockSpec(memory_space=pltpu.SMEM)
MIB = 1024 * 1024
RIGHT, LEFT, PAIR = 0, 1, 2

EPSILON = 1e-05
NEGATIVE = -1e30


def layer_norm(values):
    center = values - jnp.mean(values, axis=-1, keepdims=True)
    spread = jnp.mean(center * center, axis=-1, keepdims=True)
    return center * lax.rsqrt(spread + EPSILON)


def flip(index, bit):
    return index + bit - 2 * bit * ((index // bit) % 2)


def flips(index, mask):
    bit = 1
    while bit <= mask:
        if mask & bit:
            index = flip(index, bit)
        bit *= 2
    return index


class Line:
    def __init__(self, owners, items, send_sems, recv_sems):
        self.me = lax.axis_index("req")
        self.half = owners // 2
        self.place, self.side = self.me // 2, self.me % 2
        self.pair = flip(self.me, 1)
        self.right = lax.rem(self.place + 1, self.half) * 2 + self.side
        self.left = lax.rem(self.place + self.half - 1, self.half) * 2 + self.side
        self.items, self.send_sems, self.recv_sems = items, send_sems, recv_sems

    def copy(self, item, way, source, owner):
        target = (self.right, self.left, self.pair)[way]
        return pltpu.make_async_remote_copy(
            src_ref=source,
            dst_ref=self.items[item][1](owner),
            send_sem=self.send_sems.at[item, way, owner],
            recv_sem=self.recv_sems.at[item, owner],
            device_id={"req": target},
            device_id_type=MESH,
        )

    def arrive(self, item, owner):
        self.copy(item, PAIR, self.items[item][1](owner), owner).wait_recv()

    def both_ways(self, item, source, owner, act):
        pl.when(self.place < self.half - 1)(lambda: act(self.copy(item, RIGHT, source, owner)))
        pl.when(self.place > 0)(lambda: act(self.copy(item, LEFT, source, owner)))

    def owners_of(self, item, place):
        first = place * 2 + self.side
        return (first, flip(first, 1)) if self.items[item][2] else (first,)

    def start(self, item):
        source = self.items[item][0]
        self.both_ways(item, source, self.me, lambda copy: copy.start())
        if self.items[item][2]:
            self.copy(item, PAIR, source, self.me).start()

    def hand(self, item, distance):
        if self.items[item][2]:
            return
        if distance == 0:
            self.copy(item, PAIR, self.items[item][0], self.me).start()
            return

        def give(place):
            owner = place * 2 + self.side
            self.copy(item, PAIR, self.items[item][1](owner), owner).start()

        pl.when(self.place - distance >= 0)(lambda: give(self.place - distance))
        pl.when(self.place + distance < self.half)(lambda: give(self.place + distance))

    def start_wide(self, item):
        if self.items[item][2]:
            self.arrive(item, self.pair)
            block = self.items[item][1](self.pair)
            self.both_ways(item, block, self.pair, lambda copy: copy.start())

    def step(self, item, distance):
        def forward(place, way, more):
            for owner in self.owners_of(item, place):
                self.arrive(item, owner)
                block = self.items[item][1](owner)
                pl.when(more)(lambda: self.copy(item, way, block, owner).start())

        pl.when(self.place - distance >= 0)(
            lambda: forward(self.place - distance, RIGHT, self.place < self.half - 1)
        )
        pl.when(self.place + distance < self.half)(
            lambda: forward(self.place + distance, LEFT, self.place > 0)
        )

    def finish(self, item):
        source, target, wide = self.items[item]
        if not wide:
            for place in range(self.half):
                self.arrive(item, place * 2 + flip(self.side, 1))
        self.copy(item, PAIR, source, self.me).wait_send()
        self.both_ways(item, source, self.me, lambda copy: copy.wait_send())
        if wide:
            self.both_ways(item, source, self.pair, lambda copy: copy.wait_send())

        def sent(place, way, more):
            for owner in self.owners_of(item, place):
                pl.when(more)(lambda: self.copy(item, way, source, owner).wait_send())
                if not wide:
                    self.copy(item, PAIR, source, owner).wait_send()

        for distance in range(1, self.half):
            pl.when(self.place - distance >= 0)(
                lambda: sent(self.place - distance, RIGHT, self.place < self.half - 1)
            )
            pl.when(self.place + distance < self.half)(
                lambda: sent(self.place + distance, LEFT, self.place > 0)
            )


class Square:
    def __init__(self, source, out, send_sems, recv_sems):
        self.part = lax.axis_index("grp")
        self.near, self.far = flip(self.part, 1), flip(self.part, 2)
        self.source, self.out, self.send_sems, self.recv_sems = source, out, send_sems, recv_sems

    def copy(self, hop, source, owner):
        return pltpu.make_async_remote_copy(
            src_ref=source,
            dst_ref=self.out.at[owner],
            send_sem=self.send_sems.at[hop],
            recv_sem=self.recv_sems.at[owner],
            device_id={"grp": (self.far, self.near, self.near)[hop]},
            device_id_type=MESH,
        )

    def start(self):
        self.copy(0, self.source, self.part).start()
        self.copy(1, self.source, self.part).start()

    def forward(self):
        block = self.out.at[self.far]
        self.copy(2, block, self.far).wait_recv()
        self.copy(2, block, self.far).start()

    def finish(self):
        self.copy(1, self.source, self.near).wait_recv()
        self.copy(2, self.source, flip(self.far, 1)).wait_recv()
        self.copy(0, self.source, self.part).wait_send()
        self.copy(1, self.source, self.part).wait_send()
        self.copy(2, self.source, self.far).wait_send()


def meet(owners, parts):
    barrier = pltpu.get_barrier_semaphore()
    me, part = lax.axis_index("req"), lax.axis_index("grp")
    for offset in range(1, owners):
        other = lax.rem(me + offset, owners)
        pl.semaphore_signal(barrier, inc=1, device_id={"req": other}, device_id_type=MESH)
    for offset in range(1, parts):
        other = lax.rem(part + offset, parts)
        pl.semaphore_signal(barrier, inc=1, device_id={"grp": other}, device_id_type=MESH)
    pl.semaphore_wait(barrier, owners + parts - 2)


def line_sems(items, owners):
    return [pltpu.SemaphoreType.DMA((items, 3, owners)), pltpu.SemaphoreType.DMA((items, owners))]


def square_sems(parts):
    return [pltpu.SemaphoreType.DMA((3,)), pltpu.SemaphoreType.DMA((parts,))]


CUTS = 4


def project(rows, weight_ref, out, scale=None, tile=256):
    for low in range(0, weight_ref.shape[1], tile):
        value = jnp.dot(rows, weight_ref[:, low : low + tile], preferred_element_type=jnp.float32)
        if scale is not None:
            value = value * scale
        out[:, low : low + tile] = value.astype(out.dtype)


def first_kernel(owners, parts, tokens_ref, wq_ref, wk_ref, wv_ref, parents_ref, path_ref, win_ref, length_ref, group_ref,
                 q_out, win_out, lens_out, grps_out, accepted_out, draft_out, draft_stat,
                 tokens, wq, wk, wv, query, keys, values, win, small_ref, load_sems, hold_sems, line_send, line_recv,
                 win_send, win_recv, small_send, small_recv):
    me, part = lax.axis_index("req"), lax.axis_index("grp")
    loads = [
        pltpu.make_async_copy(source, target, load_sems.at[index])
        for index, (source, target) in enumerate(
            ((tokens_ref, tokens), (wq_ref, wq), (win_ref, win), (wk_ref, wk), (wv_ref, wv))
        )
    ]
    for copy in loads:
        copy.start()
    width = tokens.shape[1]
    per_owner, rows = parents_ref.shape
    head_dim = width // HEADS
    line_id = lax.broadcasted_iota(jnp.int32, small_ref.shape, 0)
    lane_id = lax.broadcasted_iota(jnp.int32, small_ref.shape, 1)
    filled = jnp.zeros(small_ref.shape, jnp.int32)
    for n in range(per_owner):
        for line_index, source in enumerate((length_ref, group_ref)):
            filled = jnp.where((line_id == line_index) & (lane_id == n), source[n], filled)
    small_ref[...] = filled
    loads[0].wait()
    loads[1].wait()
    project(tokens[...], wq, query, head_dim ** (-0.5))
    meet(owners, parts)
    cut_rows = query.shape[0] // CUTS

    def slot(cut, owner):
        return q_out.at[owner, pl.ds(cut * cut_rows, cut_rows)]

    items = [
        (query.at[pl.ds(cut * cut_rows, cut_rows)], functools.partial(slot, cut), cut == 0) for cut in range(CUTS)
    ]
    line = Line(owners, items, line_send, line_recv)
    square = Square(win, win_out, win_send, win_recv)
    for item in range(CUTS):
        line.start(item)
        line.hand(item, 0)
    loads[2].wait()
    square.start()
    smalls = []
    for offset in range(1, owners):
        smalls.append(pltpu.make_async_remote_copy(
            src_ref=small_ref, dst_ref=lens_out.at[me],
            send_sem=small_send.at[offset], recv_sem=small_recv.at[offset],
            device_id={"req": lax.rem(me + offset, owners)}, device_id_type=MESH))
    for offset in range(1, parts):
        smalls.append(pltpu.make_async_remote_copy(
            src_ref=small_ref, dst_ref=grps_out.at[part],
            send_sem=small_send.at[owners + offset], recv_sem=small_recv.at[owners + offset],
            device_id={"grp": lax.rem(part + offset, parts)}, device_id_type=MESH))
    for copy in smalls:
        copy.start()
    holds = [
        pltpu.make_async_copy(query, q_out.at[me], hold_sems.at[0]),
        pltpu.make_async_copy(win, win_out.at[part], hold_sems.at[1]),
        pltpu.make_async_copy(small_ref, lens_out.at[me], hold_sems.at[2]),
        pltpu.make_async_copy(small_ref, grps_out.at[part], hold_sems.at[3]),
    ]
    for copy in holds:
        copy.start()
    loads[3].wait()
    project(tokens[...], wk, keys)
    for item in range(CUTS):
        line.start_wide(item)

    def advance(distance):
        for item in range(CUTS):
            line.step(item, distance)
            line.hand(item, distance)

    loads[4].wait()
    if owners > 2:
        advance(1)
    project(tokens[...], wv, values)
    own = own_lanes(rows, head_dim)
    square_shape = (rows, rows)
    down = lax.broadcasted_iota(jnp.int32, square_shape, 0)
    eye = (down == lax.broadcasted_iota(jnp.int32, square_shape, 1)).astype(jnp.float32).astype(jnp.bfloat16)
    turn = (((1,), (1,)), ((), ()))
    span = BUNDLE * head_dim
    bundles = [slice(low, low + span) for low in range(0, width, span)]

    def drafts(n, carry):
        at = pl.ds(pl.multiple_of(n * rows, rows), rows)
        linked = (parents_ref[pl.ds(n, 1), :] == down).astype(jnp.float32).astype(jnp.bfloat16)
        closure = linked + eye
        for sweep_index in range((rows - 1).bit_length()):
            closure = jnp.minimum(jnp.dot(closure, closure, preferred_element_type=jnp.float32), 1.0)
            closure = closure.astype(jnp.bfloat16)
        reach = lax.dot_general(eye, closure, turn, preferred_element_type=jnp.float32)
        mixes, stats = attend(
            [query[at, lanes] for lanes in bundles],
            [keys[at, lanes] for lanes in bundles],
            [values[at, lanes] for lanes in bundles],
            jnp.concatenate([reach] * BUNDLE, axis=0) > 0.5, own)
        for lanes, mix in zip(bundles, mixes):
            draft_out[at, lanes] = mix.astype(draft_out.dtype)
        draft_stat[n] = stats
        chosen = (path_ref[pl.ds(n, 1), :] == down).astype(jnp.float32).astype(jnp.bfloat16)
        chosen = lax.dot_general(eye, chosen, turn, preferred_element_type=jnp.float32).astype(jnp.bfloat16)
        for low in range(0, width, 256):
            for offset, source in ((0, keys), (width, values)):
                picked = jnp.dot(chosen, source[at, low : low + 256], preferred_element_type=jnp.float32)
                accepted_out[n, :, offset + low : offset + low + 256] = picked.astype(accepted_out.dtype)
        return carry

    for distance in range(2, owners // 2):
        advance(distance)
    square.forward()
    lax.fori_loop(0, per_owner, drafts, 0)
    for item in range(CUTS):
        line.finish(item)
    square.finish()
    for copy in smalls + holds:
        copy.wait()


def first_gather(tokens, w_query, w_key, w_value, parents, path, w_in, lengths, groups, owners, parts):
    sds = jax.ShapeDtypeStruct
    per_owner, rows = parents.shape
    small = sds((8, 128), jnp.int32)
    weight = pltpu.VMEM(w_query.shape, w_query.dtype)
    block = pltpu.VMEM(tokens.shape, tokens.dtype)
    return pl.pallas_call(
        functools.partial(first_kernel, owners, parts),
        in_specs=[ANY] * 4 + [WHOLE] * 2 + [ANY] + [SCALARS] * 2,
        out_specs=[ANY] * 4 + [WHOLE] * 3,
        out_shape=[
            sds((owners,) + tokens.shape, tokens.dtype),
            sds((parts,) + w_in.shape, w_in.dtype),
            sds((owners,) + small.shape, small.dtype),
            sds((parts,) + small.shape, small.dtype),
            sds((per_owner, rows, 2 * tokens.shape[1]), tokens.dtype),
            sds(tokens.shape, tokens.dtype),
            sds((per_owner, 2 * (HEADS // BUNDLE), BUNDLE * rows), jnp.float32),
        ],
        scratch_shapes=[
            block, weight, weight, weight, block, block, block,
            pltpu.VMEM(w_in.shape, w_in.dtype),
            pltpu.VMEM(small.shape, small.dtype),
            pltpu.SemaphoreType.DMA((5,)),
            pltpu.SemaphoreType.DMA((4,)),
            *line_sems(CUTS, owners),
            *square_sems(parts),
            pltpu.SemaphoreType.DMA((owners + parts,)),
            pltpu.SemaphoreType.DMA((owners + parts,)),
        ],
        compiler_params=pltpu.CompilerParams(
            collective_id=1, has_side_effects=True, vmem_limit_bytes=60 * MIB
        ),
    )(tokens, w_query, w_key, w_value, parents, path, w_in, lengths, groups)


def own_lanes(rows, head_dim):
    shape = (BUNDLE * rows, BUNDLE * head_dim)
    row = lax.broadcasted_iota(jnp.int32, shape, 0) // rows
    lane = lax.broadcasted_iota(jnp.int32, shape, 1) // head_dim
    return row == lane


def attend(queries, keys, values, seen, own, final=False):
    rows = queries[0].shape[0]
    scores = []
    for query, key in zip(queries, keys):
        stacked = jnp.where(own, jnp.concatenate([query] * BUNDLE, axis=0), jnp.zeros((), query.dtype))
        scores.append(
            lax.dot_general(stacked, key, (((1,), (1,)), ((), ())), preferred_element_type=jnp.float32)
        )
    expos, tops, totals = [], [], []
    for score in scores:
        if seen is not None:
            score = jnp.where(seen, score, NEGATIVE)
        top = jnp.max(score, axis=1, keepdims=True)
        expo = jnp.exp(score - top)
        expos.append(expo.astype(jnp.bfloat16))
        tops.append(top)
        totals.append(jnp.sum(expo, axis=1, keepdims=True))
    mixes = []
    for expo, value, total in zip(expos, values, totals):
        mix = jnp.dot(expo, value, preferred_element_type=jnp.float32)
        mix = jnp.where(own, mix / total if final else mix, 0.0)
        folded = mix[:rows]
        for part in range(1, BUNDLE):
            folded = folded + mix[part * rows : (part + 1) * rows]
        mixes.append(folded)
    if final:
        return mixes
    lane = lax.broadcasted_iota(jnp.int32, (BUNDLE * rows, 128), 1)
    stats = jnp.zeros((BUNDLE * rows, 128), jnp.float32)
    for index, column in enumerate(tops + totals):
        stats = jnp.where(lane == index, column, stats)
    return mixes, jnp.transpose(stats)[: 2 * len(queries)]


def pages_kernel(table_ref, lens_ref, query_ref, pool_ref, accepted_ref, mix_out, stat_out, accepted_out, held, sems):
    me, owner = lax.axis_index("req"), pl.program_id(0)
    _, per_owner, per_req = table_ref.shape
    width = query_ref.shape[2]
    pool_pages, page = pool_ref.shape[0], pool_ref.shape[1]
    rows = query_ref.shape[1] // per_owner
    head_dim = width // HEADS
    span = BUNDLE * head_dim
    fetch = pltpu.make_async_copy(accepted_ref, held, sems.at[0])
    store_back = pltpu.make_async_copy(held, accepted_out, sems.at[1])
    pl.when(owner == 0)(fetch.start)

    @pl.when(owner == 1)
    def _():
        fetch.wait()
        store_back.start()

    own = own_lanes(rows, head_dim)
    bundles = [slice(low, low + span) for low in range(0, width, span)]

    def rows_at(n):
        return pl.ds(pl.multiple_of(n * rows, rows), rows)

    def store(out, stat, n, result):
        mixes, stats = result
        for lanes, mix in zip(bundles, mixes):
            out[0, rows_at(n), lanes] = mix.astype(out.dtype)
        stat[n] = stats

    def one(n, carry):
        length = lens_ref[owner, 0, n]
        count = jnp.int32(0)
        slots = [jnp.int32(0)] * per_req
        starts = [jnp.int32(0)] * per_req
        for place in range(per_req):
            entry = table_ref[owner, n, place]
            hit = (entry // pool_pages == me) & (place * page < length)
            for k in range(place + 1):
                here = hit & (count == k)
                slots[k] = jnp.where(here, entry % pool_pages, slots[k])
                starts[k] = jnp.where(here, length - place * page, starts[k])
            count = count + hit.astype(jnp.int32)

        def work(uses):
            lane = lax.broadcasted_iota(jnp.int32, (BUNDLE * rows, uses * page), 1)
            limit = jnp.zeros_like(lane)
            for k in range(uses):
                limit = jnp.where(lane // page == k, k * page + starts[k], limit)
            seen = lane < limit
            at = rows_at(n)
            store(mix_out, stat_out, n, attend(
                [query_ref[0, at, lanes] for lanes in bundles],
                [jnp.concatenate([pool_ref[slots[k], :, lanes] for k in range(uses)], axis=0) for lanes in bundles],
                [
                    jnp.concatenate(
                        [pool_ref[slots[k], :, width + lanes.start : width + lanes.stop] for k in range(uses)], axis=0
                    )
                    for lanes in bundles
                ],
                seen, own))

        @pl.when(count == 0)
        def _():
            mix_out[0, rows_at(n), :] = jnp.zeros((rows, width), mix_out.dtype)
            stat_out[n, pl.ds(0, BUNDLE), :] = jnp.full((BUNDLE, BUNDLE * rows), NEGATIVE, jnp.float32)
            stat_out[n, pl.ds(BUNDLE, BUNDLE), :] = jnp.zeros((BUNDLE, BUNDLE * rows), jnp.float32)

        pl.when(count == 1)(lambda: work(1))
        pl.when(count == 2)(lambda: work(2))
        pl.when((count > 2) & (count <= 4))(lambda: work(4))
        pl.when(count > 4)(lambda: work(per_req))
        return carry

    lax.fori_loop(0, per_owner, one, 0)
    pl.when(owner == pl.num_programs(0) - 1)(store_back.wait)


def page_partials(table, lens, query_all, pool, accepted):
    owners, rows_both, width = query_all.shape
    per_owner = table.shape[1]
    rows = rows_both // per_owner
    sds = jax.ShapeDtypeStruct
    block = pl.BlockSpec((1, rows_both, width), lambda owner: (owner, 0, 0))
    stat_shape = (2 * (HEADS // BUNDLE), BUNDLE * rows)
    return pl.pallas_call(
        pages_kernel,
        grid=(owners,),
        in_specs=[SCALARS, SCALARS, block, WHOLE, ANY],
        out_specs=[block, pl.BlockSpec((per_owner,) + stat_shape, lambda owner: (owner, 0, 0)), ANY],
        out_shape=[
            sds(query_all.shape, query_all.dtype),
            sds((owners * per_owner,) + stat_shape, jnp.float32),
            sds(accepted.shape, accepted.dtype),
        ],
        scratch_shapes=[pltpu.VMEM(accepted.shape, accepted.dtype), pltpu.SemaphoreType.DMA((2,))],
        compiler_params=pltpu.CompilerParams(vmem_limit_bytes=60 * MIB),
    )(table, lens, query_all, pool, accepted)


def merge(sources, stats, out, stat_out, last):
    per_owner, rows, span, store = out
    wide = BUNDLE * rows
    eye = lax.broadcasted_iota(jnp.int32, (rows, wide), 1) % rows == lax.broadcasted_iota(jnp.int32, (rows, wide), 0)
    shape = (2 * wide, span)
    row_head = (lax.broadcasted_iota(jnp.int32, shape, 0) % wide) // rows
    ones = (row_head == lax.broadcasted_iota(jnp.int32, shape, 1) // (span // BUNDLE)).astype(jnp.float32)
    ones = ones.astype(jnp.bfloat16)
    zero = jnp.zeros((), jnp.bfloat16)
    highs, lows = [], []
    for n in range(per_owner):
        read = [stat(n) for stat in stats]
        tops = [value[:BUNDLE] for value in read]
        sums = [value[BUNDLE:] for value in read]
        top = functools.reduce(jnp.maximum, tops)
        scales = [jnp.exp(value - top) for value in tops]
        total = functools.reduce(jnp.add, [scale * part for scale, part in zip(scales, sums)])
        if last:
            scales = [scale / total for scale in scales]
        else:
            stat_out(n, jnp.concatenate([top, total], axis=0))
        high = [scale.astype(jnp.bfloat16) for scale in scales]
        highs.append(high)
        lows.append([(scale - part.astype(jnp.float32)).astype(jnp.bfloat16) for scale, part in zip(scales, high)])
    for bundle in range(HEADS // BUNDLE):
        lanes = slice(bundle * span, (bundle + 1) * span)

        def spread(parts):
            row = parts[bundle : bundle + 1]
            return jnp.where(eye, jnp.broadcast_to(row, eye.shape), zero)

        mixed = [None] * per_owner
        for index, source in enumerate(sources):
            weights = jnp.concatenate(
                [
                    jnp.concatenate([spread(highs[n][index]), spread(lows[n][index])], axis=1)
                    for n in range(per_owner)
                ],
                axis=0,
            )
            weights = jnp.dot(weights, ones, preferred_element_type=jnp.float32)
            for n in range(per_owner):
                term = weights[n * rows : (n + 1) * rows] * source(n, lanes).astype(jnp.float32)
                mixed[n] = term if index == 0 else mixed[n] + term
        for n in range(per_owner):
            store(n, lanes, mixed[n])


GROUP_CUTS = 2
WINDOW = 2


def normalise(source, out):
    rows = source.shape[0]
    step = 64
    for low in range(0, rows, step):
        out[low : low + step, :] = layer_norm(source[low : low + step, :]).astype(out.dtype)


def second_kernel(owners, parts, mix_ref, stat_ref, draft_ref, draft_stat, tokens_ref, memory_ref, wout_ref,
                  wo_ref, wcq_ref, norm_out, shared_out, m_out, wout_out,
                  own, own_stat, got, got_stat, zin, zin_stat, memory, wout, wo, wcq, self_mix, total, cross,
                  load_sems, own_sems, hold_sems, y_send, y_recv, z_send, z_recv,
                  line_send, line_recv, wout_send, wout_recv, share_send, share_recv):
    me, part = lax.axis_index("req"), lax.axis_index("grp")
    half = owners // 2
    place, side = me // 2, me % 2
    pair = flip(me, 1)
    per_owner = draft_stat.shape[0]
    width = draft_ref.shape[1]
    rows = draft_ref.shape[0] // per_owner
    span = BUNDLE * (width // HEADS)
    groups = memory_ref.shape[0]
    wide = memory_ref.shape[2] // 2
    lanes_in = wide // parts
    order = list(range(half - 1, -1, -1))

    own_loads = {}
    for mask in order:
        dest = flips(place, mask)
        own_loads[mask] = [
            pltpu.make_async_copy(mix_ref.at[dest * 2 + side], own.at[dest], own_sems.at[0, mask]),
            pltpu.make_async_copy(stat_ref.at[dest * 2 + side], own_stat.at[dest], own_sems.at[1, mask]),
        ]
        for copy in own_loads[mask]:
            copy.start()
    loads = []
    for kind in range(2):
        lanes = pl.ds(pl.multiple_of(kind * wide + part * lanes_in, 128), lanes_in)
        loads.append(pltpu.make_async_copy(memory_ref.at[:, :, lanes], memory.at[kind], load_sems.at[kind]))
    loads.append(pltpu.make_async_copy(wout_ref, wout, load_sems.at[2]))
    weights = [
        pltpu.make_async_copy(wo_ref, wo, load_sems.at[3]),
        pltpu.make_async_copy(wcq_ref, wcq, load_sems.at[4]),
    ]
    for copy in loads + weights:
        copy.start()
    meet(owners, parts)

    def to_pair(mask):
        dest = flips(place, mask)
        far = dest * 2 + flip(side, 1)
        return [
            pltpu.make_async_remote_copy(
                src_ref=source.at[far], dst_ref=target.at[dest], send_sem=y_send.at[k, mask],
                recv_sem=y_recv.at[k, mask], device_id={"req": pair}, device_id_type=MESH)
            for k, (source, target) in enumerate(((mix_ref, got), (stat_ref, got_stat)))
        ]

    def to_place(mask):
        dest = flips(place, mask)
        low = mask & -mask
        return [
            pltpu.make_async_remote_copy(
                src_ref=source.at[dest], dst_ref=target.at[mask], send_sem=z_send.at[k, mask],
                recv_sem=z_recv.at[k, mask], device_id={"req": flip(place, low) * 2 + side}, device_id_type=MESH)
            for k, (source, target) in enumerate(((own, zin), (own_stat, zin_stat)))
        ]

    def below(mask):
        bits, bit = [], 1
        while bit < (mask & -mask if mask else half):
            bits.append(mask + bit)
            bit *= 2
        return bits

    for mask in order[:WINDOW]:
        for copy in to_pair(mask):
            copy.start()

    cut = groups // GROUP_CUTS

    def slot(kind, first, owner):
        return m_out.at[owner, kind, pl.ds(first, cut)]

    items = [
        (memory.at[kind, pl.ds(index * cut, cut)], functools.partial(slot, kind, index * cut), index == 0)
        for kind in range(2)
        for index in range(GROUP_CUTS)
    ]
    line = Line(owners, items, line_send, line_recv)
    square = Square(wout, wout_out, wout_send, wout_recv)
    for copy in loads:
        copy.wait()
    for item in range(len(items)):
        line.start(item)
    square.start()
    holds = [
        pltpu.make_async_copy(memory, m_out.at[me], hold_sems.at[0]),
        pltpu.make_async_copy(wout, wout_out.at[part], hold_sems.at[1]),
    ]
    for copy in holds:
        copy.start()

    def rows_at(n):
        return slice(n * rows, (n + 1) * rows)

    def take(ref, index):
        return lambda n, lanes: ref[index, rows_at(n), lanes]

    def take_stat(ref, index):
        return lambda n: ref[index, n]

    for turn, mask in enumerate(order):
        dest = flips(place, mask)
        for copy in to_pair(mask):
            copy.wait_recv()
        if turn + WINDOW < half:
            for copy in to_pair(order[turn + WINDOW]):
                copy.start()
        for copy in own_loads[mask]:
            copy.wait()

        senders = below(mask)
        for sender in senders:
            for copy in to_place(sender):
                copy.wait_recv()
        sources = [take(own, dest), take(got, dest)] + [take(zin, sender) for sender in senders]
        stats = [take_stat(own_stat, dest), take_stat(got_stat, dest)] + [take_stat(zin_stat, sender) for sender in senders]
        if mask:

            def store(n, lanes, value):
                own[dest, rows_at(n), lanes] = value.astype(own.dtype)

            def store_stat(n, value):
                own_stat[dest, n] = value

            merge(sources, stats, (per_owner, rows, span, store), store_stat, False)
            for copy in to_place(mask):
                copy.start()
        else:

            def store(n, lanes, value):
                self_mix[rows_at(n), lanes] = value.astype(self_mix.dtype)

            sources.append(lambda n, lanes: draft_ref[rows_at(n), lanes])
            stats.append(lambda n: draft_stat[n])
            merge(sources, stats, (per_owner, rows, span, store), None, True)
        if turn == 0:
            for item in range(len(items)):
                line.start_wide(item)
        elif turn < half - 1:
            for item in range(len(items)):
                line.step(item, turn)
        if turn == half - 2 or half == 1:
            for distance in range(turn + 1):
                for item in range(len(items)):
                    line.hand(item, distance)
    last = half - 1
    if last > 0:
        for item in range(len(items)):
            line.step(item, last)
            line.hand(item, last)
    square.forward()

    for copy in weights:
        copy.wait()
    for low in range(0, width, 256):
        lanes = slice(low, low + 256)
        total[:, lanes] = tokens_ref[:, lanes].astype(jnp.float32) + jnp.dot(
            self_mix[...], wo[:, lanes], preferred_element_type=jnp.float32
        )
    normalise(total, norm_out)

    def share(offset):
        other = lax.rem(part + offset, parts)
        return pltpu.make_async_remote_copy(
            src_ref=cross.at[offset], dst_ref=shared_out.at[part], send_sem=share_send.at[offset],
            recv_sem=share_recv.at[offset], device_id={"grp": other}, device_id_type=MESH)

    scale = (width // HEADS) ** (-0.5)
    for offset in list(range(1, parts)) + [0]:
        other = lax.rem(part + offset, parts)
        lanes = pl.ds(pl.multiple_of(other * lanes_in, 128), lanes_in)
        value = jnp.dot(norm_out[...], wcq[:, lanes], preferred_element_type=jnp.float32) * scale
        if offset:
            cross[offset] = value.astype(cross.dtype)
            share(offset).start()
        else:
            shared_out[part] = value.astype(cross.dtype)

    for item in range(len(items)):
        line.finish(item)
    square.finish()
    for offset in range(1, parts):
        share(offset).wait()
    for mask in range(half):
        for copy in to_pair(mask):
            copy.wait_send()
        if mask:
            for copy in to_place(mask):
                copy.wait_send()
    for copy in holds:
        copy.wait()


def second_exchange(mix, stat, draft, draft_stat, tokens, memory, w_out, w_output, w_cross_query, owners, parts):
    groups, local, both = memory.shape
    half = owners // 2
    rows_both, width = draft.shape
    stat = stat.reshape((owners,) + draft_stat.shape)
    sds = jax.ShapeDtypeStruct
    chunk = pltpu.VMEM((half, rows_both, width), mix.dtype)
    chunk_stat = pltpu.VMEM((half,) + draft_stat.shape, stat.dtype)
    weight = pltpu.VMEM(w_output.shape, w_output.dtype)
    items = 2 * GROUP_CUTS
    share = (parts, rows_both, width // parts)
    return pl.pallas_call(
        functools.partial(second_kernel, owners, parts),
        in_specs=[ANY, ANY, WHOLE, WHOLE, WHOLE] + [ANY] * 4,
        out_specs=[WHOLE, WHOLE, ANY, ANY],
        out_shape=[
            sds(draft.shape, draft.dtype),
            sds(share, draft.dtype),
            sds((owners, 2, groups, local, both // 2 // parts), memory.dtype),
            sds((parts,) + w_out.shape, w_out.dtype),
        ],
        scratch_shapes=[
            chunk, chunk_stat, chunk, chunk_stat, chunk, chunk_stat,
            pltpu.VMEM((2, groups, local, both // 2 // parts), memory.dtype),
            pltpu.VMEM(w_out.shape, w_out.dtype),
            weight, weight,
            pltpu.VMEM(draft.shape, draft.dtype),
            pltpu.VMEM(draft.shape, jnp.float32),
            pltpu.VMEM(share, draft.dtype),
            pltpu.SemaphoreType.DMA((5,)),
            pltpu.SemaphoreType.DMA((2, half)),
            pltpu.SemaphoreType.DMA((2,)),
            pltpu.SemaphoreType.DMA((2, half)),
            pltpu.SemaphoreType.DMA((2, half)),
            pltpu.SemaphoreType.DMA((2, half)),
            pltpu.SemaphoreType.DMA((2, half)),
            *line_sems(items, owners),
            *square_sems(parts),
            pltpu.SemaphoreType.DMA((parts,)),
            pltpu.SemaphoreType.DMA((parts,)),
        ],
        compiler_params=pltpu.CompilerParams(
            collective_id=2, has_side_effects=True, vmem_limit_bytes=60 * MIB
        ),
    )(mix, stat, draft, draft_stat, tokens, memory, w_out, w_output, w_cross_query)


def gelu(values):
    return values * (1.0 + lax.erf(values * (0.5**0.5))) * 0.5


def third_kernel(owners, parts, ids_ref, counts_ref, shared_ref, norm_ref, m_ref, wco_ref, win_ref, wout_ref, out_ref,
                 memory, wco, win, wout, mixed, sent, total, second, load_sems, win_sems, wout_sems, back_send, back_recv):
    part = lax.axis_index("grp")
    loads = [
        pltpu.make_async_copy(m_ref, memory, load_sems.at[0]),
        pltpu.make_async_copy(wco_ref, wco, load_sems.at[1]),
    ]
    streams = [
        [pltpu.make_async_copy(source.at[index], target.at[index], sems.at[index]) for index in range(parts)]
        for source, target, sems in ((win_ref, win, win_sems), (wout_ref, wout, wout_sems))
    ]
    for copy in loads:
        copy.start()
    for pieces in zip(*streams):
        for copy in pieces:
            copy.start()
    barrier = pltpu.get_barrier_semaphore()
    for offset in range(1, parts):
        other = lax.rem(part + offset, parts)
        pl.semaphore_signal(barrier, inc=1, device_id={"grp": other}, device_id_type=MESH)
    pl.semaphore_wait(barrier, parts - 1)

    rows_both, span = shared_ref.shape[1:]
    width = span * parts
    per_owner = counts_ref.shape[1] // parts
    rows = rows_both // per_owner
    positions = memory.shape[0] * memory.shape[3]
    own = own_lanes(rows, span // BUNDLE)
    loads[0].wait()

    def back(offset):
        other = lax.rem(part + offset, parts)
        return pltpu.make_async_remote_copy(
            src_ref=sent.at[offset], dst_ref=mixed.at[part], send_sem=back_send.at[offset],
            recv_sem=back_recv.at[offset], device_id={"grp": other}, device_id_type=MESH)

    for offset in list(range(1, parts)) + [0]:
        other = lax.rem(part + offset, parts)
        groups = [ids_ref[other, 1, n] for n in range(per_owner)]
        results = attend(
            [shared_ref[other, n * rows : (n + 1) * rows, :] for n in range(per_owner)],
            [memory[:, 0, group].reshape(positions, span) for group in groups],
            [memory[:, 1, group].reshape(positions, span) for group in groups],
            None, own, True)
        for n, result in enumerate(results):
            at = slice(n * rows, (n + 1) * rows)
            if offset:
                sent[offset, at, :] = result.astype(sent.dtype)
            else:
                mixed[part, at, :] = result.astype(sent.dtype)
        if offset:
            back(offset).start()
    loads[1].wait()
    for offset in range(1, parts):
        back(offset).wait_recv()
    for low in range(0, width, 256):
        lanes = slice(low, low + 256)
        value = norm_ref[:, lanes].astype(jnp.float32)
        for index in range(parts):
            value = value + jnp.dot(
                mixed[index], wco[index * span : (index + 1) * span, lanes], preferred_element_type=jnp.float32
            )
        total[:, lanes] = value
    normalise(total, second)
    total[...] = second[...].astype(jnp.float32)
    for index in range(parts):
        streams[0][index].wait()
        streams[1][index].wait()

    def feed(index, carry):
        hidden = []
        for low in range(0, win.shape[2], 256):
            value = jnp.dot(second[...], win[index, :, low : low + 256], preferred_element_type=jnp.float32)
            hidden.append(gelu(value).astype(jnp.bfloat16))
        hidden = jnp.concatenate(hidden, axis=1)
        for low in range(0, width, 256):
            lanes = slice(low, low + 256)
            total[:, lanes] += jnp.dot(hidden, wout[index, :, lanes], preferred_element_type=jnp.float32)
        return carry

    lax.fori_loop(0, parts, feed, 0)
    position = lax.broadcasted_iota(jnp.int32, (rows, width), 0)
    for n in range(per_owner):
        at = slice(n * rows, (n + 1) * rows)
        normed = layer_norm(total[at, :])
        live = position < counts_ref[0, part * per_owner + n]
        out_ref[at, :] = jnp.where(live, normed, 0.0).astype(out_ref.dtype)
    for offset in range(1, parts):
        back(offset).wait_send()


def third_stage(ids, counts, shared, norm, memory, w_cross_output, w_in, w_out, owners, parts):
    any_vmem = lambda array: pltpu.VMEM(array.shape, array.dtype)
    return pl.pallas_call(
        functools.partial(third_kernel, owners, parts),
        in_specs=[SCALARS, SCALARS, WHOLE, WHOLE] + [ANY] * 4,
        out_specs=WHOLE,
        out_shape=jax.ShapeDtypeStruct(norm.shape, norm.dtype),
        scratch_shapes=[
            any_vmem(memory), any_vmem(w_cross_output), any_vmem(w_in), any_vmem(w_out),
            any_vmem(shared), any_vmem(shared),
            pltpu.VMEM(norm.shape, jnp.float32),
            any_vmem(norm),
            pltpu.SemaphoreType.DMA((2,)),
            pltpu.SemaphoreType.DMA((parts,)),
            pltpu.SemaphoreType.DMA((parts,)),
            pltpu.SemaphoreType.DMA((parts,)),
            pltpu.SemaphoreType.DMA((parts,)),
        ],
        compiler_params=pltpu.CompilerParams(
            collective_id=3, has_side_effects=True, vmem_limit_bytes=60 * MIB
        ),
    )(ids, counts, shared, norm, memory, w_cross_output, w_in, w_out)


def per_device(
    tokens,
    kv_pool,
    page_table,
    cache_lens,
    draft_lengths,
    draft_parents,
    accepted_path,
    prompt_group,
    memory_kv,
    w_query,
    w_key,
    w_value,
    w_output,
    w_cross_query,
    w_cross_output,
    w_in,
    w_out,
):
    req_count, draft_len, model_width = tokens.shape
    owners = page_table.shape[0]
    parts = lax.axis_size("grp")
    flat_rows = tokens.reshape(req_count * draft_len, model_width)
    query_all, w_in_all, lens, group_ids, accepted_kv, draft_mix, draft_stat = first_gather(
        flat_rows, w_query, w_key, w_value, draft_parents, accepted_path, w_in, cache_lens, prompt_group, owners, parts
    )
    mix, stat, accepted_kv = page_partials(page_table, lens, query_all, kv_pool, accepted_kv)
    first_norm, shared, memory_all, w_out_all = second_exchange(
        mix, stat, draft_mix, draft_stat, flat_rows, memory_kv, w_out, w_output, w_cross_query, owners, parts
    )
    result = third_stage(
        group_ids, draft_lengths, shared, first_norm, memory_all, w_cross_output, w_in_all, w_out_all, owners, parts
    )
    return (result.reshape(req_count, draft_len, model_width), accepted_kv)


def solution(mesh):
    return jax.shard_map(
        per_device,
        mesh=mesh,
        in_specs=(
            P(("req", "grp"), None, None),
            P("req", "grp", None),
            P(None, "grp", None),
            P(("req", "grp")),
            P("req", None),
            P(("req", "grp"), None),
            P(("req", "grp"), None),
            P(("req", "grp")),
            P(None, "req", None),
            P(),
            P(),
            P(),
            P(),
            P(),
            P(),
            P(None, "grp"),
            P("grp", None),
        ),
        out_specs=(P(("req", "grp"), None, None), P(("req", "grp"), None, None)),
        check_vma=False,
    )
```

```python
import functools

import jax
import jax.numpy as jnp
from jax import lax
from jax.experimental import pallas as pl
from jax.experimental.pallas import tpu as pltpu
from jax.sharding import PartitionSpec as P

HEADS = 16
BUNDLE = 4
MESH = pl.DeviceIdType.MESH
ANY = pl.BlockSpec(memory_space=pl.ANY)
WHOLE = pl.BlockSpec(memory_space=pltpu.VMEM)
SCALARS = pl.BlockSpec(memory_space=pltpu.SMEM)
MIB = 1024 * 1024
RIGHT, LEFT, PAIR = 0, 1, 2

EPSILON = 1e-05
NEGATIVE = -1e30


def layer_norm(values):
    center = values - jnp.mean(values, axis=-1, keepdims=True)
    spread = jnp.mean(center * center, axis=-1, keepdims=True)
    return center * lax.rsqrt(spread + EPSILON)


def flip(index, bit):
    return index + bit - 2 * bit * ((index // bit) % 2)


def flips(index, mask):
    bit = 1
    while bit <= mask:
        if mask & bit:
            index = flip(index, bit)
        bit *= 2
    return index


class Line:
    def __init__(self, owners, items, send_sems, recv_sems):
        self.me = lax.axis_index("req")
        self.half = owners // 2
        self.place, self.side = self.me // 2, self.me % 2
        self.pair = flip(self.me, 1)
        self.right = lax.rem(self.place + 1, self.half) * 2 + self.side
        self.left = lax.rem(self.place + self.half - 1, self.half) * 2 + self.side
        self.items, self.send_sems, self.recv_sems = items, send_sems, recv_sems

    def copy(self, item, way, source, owner):
        target = (self.right, self.left, self.pair)[way]
        return pltpu.make_async_remote_copy(
            src_ref=source,
            dst_ref=self.items[item][1](owner),
            send_sem=self.send_sems.at[item, way, owner],
            recv_sem=self.recv_sems.at[item, owner],
            device_id={"req": target},
            device_id_type=MESH,
        )

    def arrive(self, item, owner):
        self.copy(item, PAIR, self.items[item][1](owner), owner).wait_recv()

    def both_ways(self, item, source, owner, act):
        pl.when(self.place < self.half - 1)(lambda: act(self.copy(item, RIGHT, source, owner)))
        pl.when(self.place > 0)(lambda: act(self.copy(item, LEFT, source, owner)))

    def owners_of(self, item, place):
        first = place * 2 + self.side
        return (first, flip(first, 1)) if self.items[item][2] else (first,)

    def start(self, item):
        source = self.items[item][0]
        self.both_ways(item, source, self.me, lambda copy: copy.start())
        if self.items[item][2]:
            self.copy(item, PAIR, source, self.me).start()

    def hand(self, item, distance):
        if self.items[item][2]:
            return
        if distance == 0:
            self.copy(item, PAIR, self.items[item][0], self.me).start()
            return

        def give(place):
            owner = place * 2 + self.side
            self.copy(item, PAIR, self.items[item][1](owner), owner).start()

        pl.when(self.place - distance >= 0)(lambda: give(self.place - distance))
        pl.when(self.place + distance < self.half)(lambda: give(self.place + distance))

    def start_wide(self, item):
        if self.items[item][2]:
            self.arrive(item, self.pair)
            block = self.items[item][1](self.pair)
            self.both_ways(item, block, self.pair, lambda copy: copy.start())

    def step(self, item, distance):
        def forward(place, way, more):
            for owner in self.owners_of(item, place):
                self.arrive(item, owner)
                block = self.items[item][1](owner)
                pl.when(more)(lambda: self.copy(item, way, block, owner).start())

        pl.when(self.place - distance >= 0)(
            lambda: forward(self.place - distance, RIGHT, self.place < self.half - 1)
        )
        pl.when(self.place + distance < self.half)(
            lambda: forward(self.place + distance, LEFT, self.place > 0)
        )

    def finish(self, item):
        source, target, wide = self.items[item]
        if not wide:
            for place in range(self.half):
                self.arrive(item, place * 2 + flip(self.side, 1))
        self.copy(item, PAIR, source, self.me).wait_send()
        self.both_ways(item, source, self.me, lambda copy: copy.wait_send())
        if wide:
            self.both_ways(item, source, self.pair, lambda copy: copy.wait_send())

        def sent(place, way, more):
            for owner in self.owners_of(item, place):
                pl.when(more)(lambda: self.copy(item, way, source, owner).wait_send())
                if not wide:
                    self.copy(item, PAIR, source, owner).wait_send()

        for distance in range(1, self.half):
            pl.when(self.place - distance >= 0)(
                lambda: sent(self.place - distance, RIGHT, self.place < self.half - 1)
            )
            pl.when(self.place + distance < self.half)(
                lambda: sent(self.place + distance, LEFT, self.place > 0)
            )


class Square:
    def __init__(self, source, out, send_sems, recv_sems):
        self.part = lax.axis_index("grp")
        self.near, self.far = flip(self.part, 1), flip(self.part, 2)
        self.source, self.out, self.send_sems, self.recv_sems = source, out, send_sems, recv_sems

    def copy(self, hop, source, owner):
        return pltpu.make_async_remote_copy(
            src_ref=source,
            dst_ref=self.out.at[owner],
            send_sem=self.send_sems.at[hop],
            recv_sem=self.recv_sems.at[owner],
            device_id={"grp": (self.far, self.near, self.near)[hop]},
            device_id_type=MESH,
        )

    def start(self):
        self.copy(0, self.source, self.part).start()
        self.copy(1, self.source, self.part).start()

    def forward(self):
        block = self.out.at[self.far]
        self.copy(2, block, self.far).wait_recv()
        self.copy(2, block, self.far).start()

    def finish(self):
        self.copy(1, self.source, self.near).wait_recv()
        self.copy(2, self.source, flip(self.far, 1)).wait_recv()
        self.copy(0, self.source, self.part).wait_send()
        self.copy(1, self.source, self.part).wait_send()
        self.copy(2, self.source, self.far).wait_send()


def meet(owners, parts):
    barrier = pltpu.get_barrier_semaphore()
    me, part = lax.axis_index("req"), lax.axis_index("grp")
    for offset in range(1, owners):
        other = lax.rem(me + offset, owners)
        pl.semaphore_signal(barrier, inc=1, device_id={"req": other}, device_id_type=MESH)
    for offset in range(1, parts):
        other = lax.rem(part + offset, parts)
        pl.semaphore_signal(barrier, inc=1, device_id={"grp": other}, device_id_type=MESH)
    pl.semaphore_wait(barrier, owners + parts - 2)


def line_sems(items, owners):
    return [pltpu.SemaphoreType.DMA((items, 3, owners)), pltpu.SemaphoreType.DMA((items, owners))]


def square_sems(parts):
    return [pltpu.SemaphoreType.DMA((3,)), pltpu.SemaphoreType.DMA((parts,))]


CUTS = 4


def project(rows, weight_ref, out, scale=None, tile=256):
    for low in range(0, weight_ref.shape[1], tile):
        value = jnp.dot(rows, weight_ref[:, low : low + tile], preferred_element_type=jnp.float32)
        if scale is not None:
            value = value * scale
        out[:, low : low + tile] = value.astype(out.dtype)


def first_kernel(owners, parts, tokens_ref, wq_ref, wk_ref, wv_ref, parents_ref, path_ref, length_ref, group_ref,
                 q_out, lens_out, grps_out, accepted_out, draft_out, draft_stat,
                 tokens, wq, wk, wv, query, keys, values, small_ref, load_sems, hold_sems, line_send, line_recv,
                 small_send, small_recv):
    me, part = lax.axis_index("req"), lax.axis_index("grp")
    loads = [
        pltpu.make_async_copy(source, target, load_sems.at[index])
        for index, (source, target) in enumerate(
            ((tokens_ref, tokens), (wq_ref, wq), (wk_ref, wk), (wv_ref, wv))
        )
    ]
    for copy in loads:
        copy.start()
    width = tokens.shape[1]
    per_owner, rows = parents_ref.shape
    head_dim = width // HEADS
    line_id = lax.broadcasted_iota(jnp.int32, small_ref.shape, 0)
    lane_id = lax.broadcasted_iota(jnp.int32, small_ref.shape, 1)
    filled = jnp.zeros(small_ref.shape, jnp.int32)
    for n in range(per_owner):
        for line_index, source in enumerate((length_ref, group_ref)):
            filled = jnp.where((line_id == line_index) & (lane_id == n), source[n], filled)
    small_ref[...] = filled
    loads[0].wait()
    loads[1].wait()
    project(tokens[...], wq, query, head_dim ** (-0.5))
    meet(owners, parts)
    cut_rows = query.shape[0] // CUTS

    def slot(cut, owner):
        return q_out.at[owner, pl.ds(cut * cut_rows, cut_rows)]

    items = [
        (query.at[pl.ds(cut * cut_rows, cut_rows)], functools.partial(slot, cut), cut == 0) for cut in range(CUTS)
    ]
    line = Line(owners, items, line_send, line_recv)
    for item in range(CUTS):
        line.start(item)
        line.hand(item, 0)
    smalls = []
    for offset in range(1, owners):
        smalls.append(pltpu.make_async_remote_copy(
            src_ref=small_ref, dst_ref=lens_out.at[me],
            send_sem=small_send.at[offset], recv_sem=small_recv.at[offset],
            device_id={"req": lax.rem(me + offset, owners)}, device_id_type=MESH))
    for offset in range(1, parts):
        smalls.append(pltpu.make_async_remote_copy(
            src_ref=small_ref, dst_ref=grps_out.at[part],
            send_sem=small_send.at[owners + offset], recv_sem=small_recv.at[owners + offset],
            device_id={"grp": lax.rem(part + offset, parts)}, device_id_type=MESH))
    for copy in smalls:
        copy.start()
    holds = [
        pltpu.make_async_copy(query, q_out.at[me], hold_sems.at[0]),
        pltpu.make_async_copy(small_ref, lens_out.at[me], hold_sems.at[1]),
        pltpu.make_async_copy(small_ref, grps_out.at[part], hold_sems.at[2]),
    ]
    for copy in holds:
        copy.start()
    loads[2].wait()
    project(tokens[...], wk, keys)
    for item in range(CUTS):
        line.start_wide(item)

    def advance(distance):
        for item in range(CUTS):
            line.step(item, distance)
            line.hand(item, distance)

    loads[3].wait()
    if owners > 2:
        advance(1)
    project(tokens[...], wv, values)
    own = own_lanes(rows, head_dim)
    square_shape = (rows, rows)
    down = lax.broadcasted_iota(jnp.int32, square_shape, 0)
    eye = (down == lax.broadcasted_iota(jnp.int32, square_shape, 1)).astype(jnp.float32).astype(jnp.bfloat16)
    turn = (((1,), (1,)), ((), ()))
    span = BUNDLE * head_dim
    bundles = [slice(low, low + span) for low in range(0, width, span)]

    def drafts(n, carry):
        at = pl.ds(pl.multiple_of(n * rows, rows), rows)
        linked = (parents_ref[pl.ds(n, 1), :] == down).astype(jnp.float32).astype(jnp.bfloat16)
        closure = linked + eye
        for sweep_index in range((rows - 1).bit_length()):
            closure = jnp.minimum(jnp.dot(closure, closure, preferred_element_type=jnp.float32), 1.0)
            closure = closure.astype(jnp.bfloat16)
        reach = lax.dot_general(eye, closure, turn, preferred_element_type=jnp.float32)
        mixes, stats = attend(
            [query[at, lanes] for lanes in bundles],
            [keys[at, lanes] for lanes in bundles],
            [values[at, lanes] for lanes in bundles],
            jnp.concatenate([reach] * BUNDLE, axis=0) > 0.5, own)
        for lanes, mix in zip(bundles, mixes):
            draft_out[at, lanes] = mix.astype(draft_out.dtype)
        draft_stat[n] = stats
        chosen = (path_ref[pl.ds(n, 1), :] == down).astype(jnp.float32).astype(jnp.bfloat16)
        chosen = lax.dot_general(eye, chosen, turn, preferred_element_type=jnp.float32).astype(jnp.bfloat16)
        for low in range(0, width, 256):
            for offset, source in ((0, keys), (width, values)):
                picked = jnp.dot(chosen, source[at, low : low + 256], preferred_element_type=jnp.float32)
                accepted_out[n, :, offset + low : offset + low + 256] = picked.astype(accepted_out.dtype)
        return carry

    for distance in range(2, owners // 2):
        advance(distance)
    lax.fori_loop(0, per_owner, drafts, 0)
    for item in range(CUTS):
        line.finish(item)
    for copy in smalls + holds:
        copy.wait()


def first_gather(tokens, w_query, w_key, w_value, parents, path, lengths, groups, owners, parts):
    sds = jax.ShapeDtypeStruct
    per_owner, rows = parents.shape
    small = sds((8, 128), jnp.int32)
    weight = pltpu.VMEM(w_query.shape, w_query.dtype)
    block = pltpu.VMEM(tokens.shape, tokens.dtype)
    return pl.pallas_call(
        functools.partial(first_kernel, owners, parts),
        in_specs=[ANY] * 4 + [WHOLE] * 2 + [SCALARS] * 2,
        out_specs=[ANY] * 3 + [WHOLE] * 3,
        out_shape=[
            sds((owners,) + tokens.shape, tokens.dtype),
            sds((owners,) + small.shape, small.dtype),
            sds((parts,) + small.shape, small.dtype),
            sds((per_owner, rows, 2 * tokens.shape[1]), tokens.dtype),
            sds(tokens.shape, tokens.dtype),
            sds((per_owner, 2 * (HEADS // BUNDLE), BUNDLE * rows), jnp.float32),
        ],
        scratch_shapes=[
            block, weight, weight, weight, block, block, block,
            pltpu.VMEM(small.shape, small.dtype),
            pltpu.SemaphoreType.DMA((4,)),
            pltpu.SemaphoreType.DMA((3,)),
            *line_sems(CUTS, owners),
            pltpu.SemaphoreType.DMA((owners + parts,)),
            pltpu.SemaphoreType.DMA((owners + parts,)),
        ],
        compiler_params=pltpu.CompilerParams(
            collective_id=1, has_side_effects=True, vmem_limit_bytes=60 * MIB
        ),
    )(tokens, w_query, w_key, w_value, parents, path, lengths, groups)


def own_lanes(rows, head_dim):
    shape = (BUNDLE * rows, BUNDLE * head_dim)
    row = lax.broadcasted_iota(jnp.int32, shape, 0) // rows
    lane = lax.broadcasted_iota(jnp.int32, shape, 1) // head_dim
    return row == lane


def attend(queries, keys, values, seen, own, final=False):
    rows = queries[0].shape[0]
    scores = []
    for query, key in zip(queries, keys):
        stacked = jnp.where(own, jnp.concatenate([query] * BUNDLE, axis=0), jnp.zeros((), query.dtype))
        scores.append(
            lax.dot_general(stacked, key, (((1,), (1,)), ((), ())), preferred_element_type=jnp.float32)
        )
    expos, tops, totals = [], [], []
    for score in scores:
        if seen is not None:
            score = jnp.where(seen, score, NEGATIVE)
        top = jnp.max(score, axis=1, keepdims=True)
        expo = jnp.exp(score - top)
        expos.append(expo.astype(jnp.bfloat16))
        tops.append(top)
        totals.append(jnp.sum(expo, axis=1, keepdims=True))
    mixes = []
    for expo, value, total in zip(expos, values, totals):
        mix = jnp.dot(expo, value, preferred_element_type=jnp.float32)
        mix = jnp.where(own, mix / total if final else mix, 0.0)
        folded = mix[:rows]
        for part in range(1, BUNDLE):
            folded = folded + mix[part * rows : (part + 1) * rows]
        mixes.append(folded)
    if final:
        return mixes
    lane = lax.broadcasted_iota(jnp.int32, (BUNDLE * rows, 128), 1)
    stats = jnp.zeros((BUNDLE * rows, 128), jnp.float32)
    for index, column in enumerate(tops + totals):
        stats = jnp.where(lane == index, column, stats)
    return mixes, jnp.transpose(stats)[: 2 * len(queries)]


def pages_kernel(table_ref, lens_ref, query_ref, pool_ref, accepted_ref, mix_out, stat_out, accepted_out, held, sems):
    me, owner = lax.axis_index("req"), pl.program_id(0)
    _, per_owner, per_req = table_ref.shape
    width = query_ref.shape[2]
    pool_pages, page = pool_ref.shape[0], pool_ref.shape[1]
    rows = query_ref.shape[1] // per_owner
    head_dim = width // HEADS
    span = BUNDLE * head_dim
    fetch = pltpu.make_async_copy(accepted_ref, held, sems.at[0])
    store_back = pltpu.make_async_copy(held, accepted_out, sems.at[1])
    pl.when(owner == 0)(fetch.start)

    @pl.when(owner == 1)
    def _():
        fetch.wait()
        store_back.start()

    own = own_lanes(rows, head_dim)
    bundles = [slice(low, low + span) for low in range(0, width, span)]

    def rows_at(n):
        return pl.ds(pl.multiple_of(n * rows, rows), rows)

    def store(out, stat, n, result):
        mixes, stats = result
        for lanes, mix in zip(bundles, mixes):
            out[0, rows_at(n), lanes] = mix.astype(out.dtype)
        stat[n] = stats

    def one(n, carry):
        length = lens_ref[owner, 0, n]
        count = jnp.int32(0)
        slots = [jnp.int32(0)] * per_req
        starts = [jnp.int32(0)] * per_req
        for place in range(per_req):
            entry = table_ref[owner, n, place]
            hit = (entry // pool_pages == me) & (place * page < length)
            for k in range(place + 1):
                here = hit & (count == k)
                slots[k] = jnp.where(here, entry % pool_pages, slots[k])
                starts[k] = jnp.where(here, length - place * page, starts[k])
            count = count + hit.astype(jnp.int32)

        def work(uses):
            lane = lax.broadcasted_iota(jnp.int32, (BUNDLE * rows, uses * page), 1)
            limit = jnp.zeros_like(lane)
            for k in range(uses):
                limit = jnp.where(lane // page == k, k * page + starts[k], limit)
            seen = lane < limit
            at = rows_at(n)
            store(mix_out, stat_out, n, attend(
                [query_ref[0, at, lanes] for lanes in bundles],
                [jnp.concatenate([pool_ref[slots[k], :, lanes] for k in range(uses)], axis=0) for lanes in bundles],
                [
                    jnp.concatenate(
                        [pool_ref[slots[k], :, width + lanes.start : width + lanes.stop] for k in range(uses)], axis=0
                    )
                    for lanes in bundles
                ],
                seen, own))

        @pl.when(count == 0)
        def _():
            mix_out[0, rows_at(n), :] = jnp.zeros((rows, width), mix_out.dtype)
            stat_out[n, pl.ds(0, BUNDLE), :] = jnp.full((BUNDLE, BUNDLE * rows), NEGATIVE, jnp.float32)
            stat_out[n, pl.ds(BUNDLE, BUNDLE), :] = jnp.zeros((BUNDLE, BUNDLE * rows), jnp.float32)

        pl.when(count == 1)(lambda: work(1))
        pl.when(count == 2)(lambda: work(2))
        pl.when((count > 2) & (count <= 4))(lambda: work(4))
        pl.when(count > 4)(lambda: work(per_req))
        return carry

    lax.fori_loop(0, per_owner, one, 0)
    pl.when(owner == pl.num_programs(0) - 1)(store_back.wait)


def page_partials(table, lens, query_all, pool, accepted):
    owners, rows_both, width = query_all.shape
    per_owner = table.shape[1]
    rows = rows_both // per_owner
    sds = jax.ShapeDtypeStruct
    block = pl.BlockSpec((1, rows_both, width), lambda owner: (owner, 0, 0))
    stat_shape = (2 * (HEADS // BUNDLE), BUNDLE * rows)
    return pl.pallas_call(
        pages_kernel,
        grid=(owners,),
        in_specs=[SCALARS, SCALARS, block, WHOLE, ANY],
        out_specs=[block, pl.BlockSpec((per_owner,) + stat_shape, lambda owner: (owner, 0, 0)), ANY],
        out_shape=[
            sds(query_all.shape, query_all.dtype),
            sds((owners * per_owner,) + stat_shape, jnp.float32),
            sds(accepted.shape, accepted.dtype),
        ],
        scratch_shapes=[pltpu.VMEM(accepted.shape, accepted.dtype), pltpu.SemaphoreType.DMA((2,))],
        compiler_params=pltpu.CompilerParams(vmem_limit_bytes=60 * MIB),
    )(table, lens, query_all, pool, accepted)


def merge(sources, stats, out, stat_out, last):
    per_owner, rows, span, store = out
    wide = BUNDLE * rows
    eye = lax.broadcasted_iota(jnp.int32, (rows, wide), 1) % rows == lax.broadcasted_iota(jnp.int32, (rows, wide), 0)
    shape = (2 * wide, span)
    row_head = (lax.broadcasted_iota(jnp.int32, shape, 0) % wide) // rows
    ones = (row_head == lax.broadcasted_iota(jnp.int32, shape, 1) // (span // BUNDLE)).astype(jnp.float32)
    ones = ones.astype(jnp.bfloat16)
    zero = jnp.zeros((), jnp.bfloat16)
    highs, lows = [], []
    for n in range(per_owner):
        read = [stat(n) for stat in stats]
        tops = [value[:BUNDLE] for value in read]
        sums = [value[BUNDLE:] for value in read]
        top = functools.reduce(jnp.maximum, tops)
        scales = [jnp.exp(value - top) for value in tops]
        total = functools.reduce(jnp.add, [scale * part for scale, part in zip(scales, sums)])
        if last:
            scales = [scale / total for scale in scales]
        else:
            stat_out(n, jnp.concatenate([top, total], axis=0))
        high = [scale.astype(jnp.bfloat16) for scale in scales]
        highs.append(high)
        lows.append([(scale - part.astype(jnp.float32)).astype(jnp.bfloat16) for scale, part in zip(scales, high)])
    for bundle in range(HEADS // BUNDLE):
        lanes = slice(bundle * span, (bundle + 1) * span)

        def spread(parts):
            row = parts[bundle : bundle + 1]
            return jnp.where(eye, jnp.broadcast_to(row, eye.shape), zero)

        mixed = [None] * per_owner
        for index, source in enumerate(sources):
            weights = jnp.concatenate(
                [
                    jnp.concatenate([spread(highs[n][index]), spread(lows[n][index])], axis=1)
                    for n in range(per_owner)
                ],
                axis=0,
            )
            weights = jnp.dot(weights, ones, preferred_element_type=jnp.float32)
            for n in range(per_owner):
                term = weights[n * rows : (n + 1) * rows] * source(n, lanes).astype(jnp.float32)
                mixed[n] = term if index == 0 else mixed[n] + term
        for n in range(per_owner):
            store(n, lanes, mixed[n])


GROUP_CUTS = 2
WINDOW = 2


def normalise(source, out):
    rows = source.shape[0]
    step = 64
    for low in range(0, rows, step):
        out[low : low + step, :] = layer_norm(source[low : low + step, :]).astype(out.dtype)


def second_kernel(owners, parts, mix_ref, stat_ref, draft_ref, draft_stat, tokens_ref, memory_ref, wout_ref,
                  wo_ref, wcq_ref, win_ref, norm_out, shared_out, m_out, wout_out, win_out,
                  own, own_stat, got, got_stat, zin, zin_stat, memory, wout, wo, wcq, win, self_mix, total, cross,
                  load_sems, own_sems, hold_sems, y_send, y_recv, z_send, z_recv,
                  line_send, line_recv, wout_send, wout_recv, share_send, share_recv, win_send, win_recv):
    me, part = lax.axis_index("req"), lax.axis_index("grp")
    half = owners // 2
    place, side = me // 2, me % 2
    pair = flip(me, 1)
    per_owner = draft_stat.shape[0]
    width = draft_ref.shape[1]
    rows = draft_ref.shape[0] // per_owner
    span = BUNDLE * (width // HEADS)
    groups = memory_ref.shape[0]
    wide = memory_ref.shape[2] // 2
    lanes_in = wide // parts
    order = list(range(half - 1, -1, -1))

    own_loads = {}
    for mask in order:
        dest = flips(place, mask)
        own_loads[mask] = [
            pltpu.make_async_copy(mix_ref.at[dest * 2 + side], own.at[dest], own_sems.at[0, mask]),
            pltpu.make_async_copy(stat_ref.at[dest * 2 + side], own_stat.at[dest], own_sems.at[1, mask]),
        ]
        for copy in own_loads[mask]:
            copy.start()
    loads = []
    for kind in range(2):
        lanes = pl.ds(pl.multiple_of(kind * wide + part * lanes_in, 128), lanes_in)
        loads.append(pltpu.make_async_copy(memory_ref.at[:, :, lanes], memory.at[kind], load_sems.at[kind]))
    loads.append(pltpu.make_async_copy(wout_ref, wout, load_sems.at[2]))
    loads.append(pltpu.make_async_copy(win_ref, win, load_sems.at[5]))
    weights = [
        pltpu.make_async_copy(wo_ref, wo, load_sems.at[3]),
        pltpu.make_async_copy(wcq_ref, wcq, load_sems.at[4]),
    ]
    for copy in loads + weights:
        copy.start()
    meet(owners, parts)

    def to_pair(mask):
        dest = flips(place, mask)
        far = dest * 2 + flip(side, 1)
        return [
            pltpu.make_async_remote_copy(
                src_ref=source.at[far], dst_ref=target.at[dest], send_sem=y_send.at[k, mask],
                recv_sem=y_recv.at[k, mask], device_id={"req": pair}, device_id_type=MESH)
            for k, (source, target) in enumerate(((mix_ref, got), (stat_ref, got_stat)))
        ]

    def to_place(mask):
        dest = flips(place, mask)
        low = mask & -mask
        return [
            pltpu.make_async_remote_copy(
                src_ref=source.at[dest], dst_ref=target.at[mask], send_sem=z_send.at[k, mask],
                recv_sem=z_recv.at[k, mask], device_id={"req": flip(place, low) * 2 + side}, device_id_type=MESH)
            for k, (source, target) in enumerate(((own, zin), (own_stat, zin_stat)))
        ]

    def below(mask):
        bits, bit = [], 1
        while bit < (mask & -mask if mask else half):
            bits.append(mask + bit)
            bit *= 2
        return bits

    for mask in order[:WINDOW]:
        for copy in to_pair(mask):
            copy.start()

    cut = groups // GROUP_CUTS

    def slot(kind, first, owner):
        return m_out.at[owner, kind, pl.ds(first, cut)]

    items = [
        (memory.at[kind, pl.ds(index * cut, cut)], functools.partial(slot, kind, index * cut), index == 0)
        for kind in range(2)
        for index in range(GROUP_CUTS)
    ]
    line = Line(owners, items, line_send, line_recv)
    squares = [Square(win, win_out, win_send, win_recv), Square(wout, wout_out, wout_send, wout_recv)]
    for copy in loads:
        copy.wait()
    for item in range(len(items)):
        line.start(item)
    for square in squares:
        square.start()
    holds = [
        pltpu.make_async_copy(win, win_out.at[part], hold_sems.at[2]),
        pltpu.make_async_copy(memory, m_out.at[me], hold_sems.at[0]),
        pltpu.make_async_copy(wout, wout_out.at[part], hold_sems.at[1]),
    ]
    for copy in holds:
        copy.start()

    def rows_at(n):
        return slice(n * rows, (n + 1) * rows)

    def take(ref, index):
        return lambda n, lanes: ref[index, rows_at(n), lanes]

    def take_stat(ref, index):
        return lambda n: ref[index, n]

    for turn, mask in enumerate(order):
        dest = flips(place, mask)
        for copy in to_pair(mask):
            copy.wait_recv()
        if turn + WINDOW < half:
            for copy in to_pair(order[turn + WINDOW]):
                copy.start()
        for copy in own_loads[mask]:
            copy.wait()

        senders = below(mask)
        for sender in senders:
            for copy in to_place(sender):
                copy.wait_recv()
        sources = [take(own, dest), take(got, dest)] + [take(zin, sender) for sender in senders]
        stats = [take_stat(own_stat, dest), take_stat(got_stat, dest)] + [take_stat(zin_stat, sender) for sender in senders]
        if mask:

            def store(n, lanes, value):
                own[dest, rows_at(n), lanes] = value.astype(own.dtype)

            def store_stat(n, value):
                own_stat[dest, n] = value

            merge(sources, stats, (per_owner, rows, span, store), store_stat, False)
            for copy in to_place(mask):
                copy.start()
        else:

            def store(n, lanes, value):
                self_mix[rows_at(n), lanes] = value.astype(self_mix.dtype)

            sources.append(lambda n, lanes: draft_ref[rows_at(n), lanes])
            stats.append(lambda n: draft_stat[n])
            merge(sources, stats, (per_owner, rows, span, store), None, True)
            for item in range(len(items)) if turn else ():
                line.step(item, turn)
                line.hand(item, turn)
        if turn == 0:
            for item in range(len(items)):
                line.start_wide(item)
        elif turn < half - 1:
            for item in range(len(items)):
                line.step(item, turn)
        if turn == half - 2 or half == 1:
            for distance in range(turn + 1):
                for item in range(len(items)):
                    line.hand(item, distance)
    for square in squares:
        square.forward()

    for copy in weights:
        copy.wait()
    for low in range(0, width, 256):
        lanes = slice(low, low + 256)
        total[:, lanes] = tokens_ref[:, lanes].astype(jnp.float32) + jnp.dot(
            self_mix[...], wo[:, lanes], preferred_element_type=jnp.float32
        )
    normalise(total, norm_out)

    def share(offset):
        other = lax.rem(part + offset, parts)
        return pltpu.make_async_remote_copy(
            src_ref=cross.at[offset], dst_ref=shared_out.at[part], send_sem=share_send.at[offset],
            recv_sem=share_recv.at[offset], device_id={"grp": other}, device_id_type=MESH)

    scale = (width // HEADS) ** (-0.5)
    for offset in list(range(1, parts)) + [0]:
        other = lax.rem(part + offset, parts)
        lanes = pl.ds(pl.multiple_of(other * lanes_in, 128), lanes_in)
        value = jnp.dot(norm_out[...], wcq[:, lanes], preferred_element_type=jnp.float32) * scale
        if offset:
            cross[offset] = value.astype(cross.dtype)
            share(offset).start()
        else:
            shared_out[part] = value.astype(cross.dtype)

    for item in range(len(items)):
        line.finish(item)
    for square in squares:
        square.finish()
    for offset in range(1, parts):
        share(offset).wait()
    for mask in range(half):
        for copy in to_pair(mask):
            copy.wait_send()
        if mask:
            for copy in to_place(mask):
                copy.wait_send()
    for copy in holds:
        copy.wait()


def second_exchange(mix, stat, draft, draft_stat, tokens, memory, w_out, w_output, w_cross_query, w_in, owners, parts):
    groups, local, both = memory.shape
    half = owners // 2
    rows_both, width = draft.shape
    stat = stat.reshape((owners,) + draft_stat.shape)
    sds = jax.ShapeDtypeStruct
    chunk = pltpu.VMEM((half, rows_both, width), mix.dtype)
    chunk_stat = pltpu.VMEM((half,) + draft_stat.shape, stat.dtype)
    weight = pltpu.VMEM(w_output.shape, w_output.dtype)
    items = 2 * GROUP_CUTS
    share = (parts, rows_both, width // parts)
    return pl.pallas_call(
        functools.partial(second_kernel, owners, parts),
        in_specs=[ANY, ANY, WHOLE, WHOLE, WHOLE] + [ANY] * 5,
        out_specs=[WHOLE, WHOLE] + [ANY] * 3,
        out_shape=[
            sds(draft.shape, draft.dtype),
            sds(share, draft.dtype),
            sds((owners, 2, groups, local, both // 2 // parts), memory.dtype),
            sds((parts,) + w_out.shape, w_out.dtype),
            sds((parts,) + w_in.shape, w_in.dtype),
        ],
        scratch_shapes=[
            chunk, chunk_stat, chunk, chunk_stat, chunk, chunk_stat,
            pltpu.VMEM((2, groups, local, both // 2 // parts), memory.dtype),
            pltpu.VMEM(w_out.shape, w_out.dtype),
            weight, weight,
            pltpu.VMEM(w_in.shape, w_in.dtype),
            pltpu.VMEM(draft.shape, draft.dtype),
            pltpu.VMEM(draft.shape, jnp.float32),
            pltpu.VMEM(share, draft.dtype),
            pltpu.SemaphoreType.DMA((6,)),
            pltpu.SemaphoreType.DMA((2, half)),
            pltpu.SemaphoreType.DMA((3,)),
            pltpu.SemaphoreType.DMA((2, half)),
            pltpu.SemaphoreType.DMA((2, half)),
            pltpu.SemaphoreType.DMA((2, half)),
            pltpu.SemaphoreType.DMA((2, half)),
            *line_sems(items, owners),
            *square_sems(parts),
            pltpu.SemaphoreType.DMA((parts,)),
            pltpu.SemaphoreType.DMA((parts,)),
            *square_sems(parts),
        ],
        compiler_params=pltpu.CompilerParams(
            collective_id=2, has_side_effects=True, vmem_limit_bytes=60 * MIB
        ),
    )(mix, stat, draft, draft_stat, tokens, memory, w_out, w_output, w_cross_query, w_in)


def gelu(values):
    return values * (1.0 + lax.erf(values * (0.5**0.5))) * 0.5


def third_kernel(owners, parts, ids_ref, counts_ref, shared_ref, norm_ref, m_ref, wco_ref, win_ref, wout_ref, out_ref,
                 memory, wco, win, wout, mixed, sent, total, second, load_sems, win_sems, wout_sems, back_send, back_recv):
    part = lax.axis_index("grp")
    loads = [
        pltpu.make_async_copy(m_ref, memory, load_sems.at[0]),
        pltpu.make_async_copy(wco_ref, wco, load_sems.at[1]),
    ]
    streams = [
        [pltpu.make_async_copy(source.at[index], target.at[index], sems.at[index]) for index in range(parts)]
        for source, target, sems in ((win_ref, win, win_sems), (wout_ref, wout, wout_sems))
    ]
    loads[0].start()
    barrier = pltpu.get_barrier_semaphore()
    for offset in range(1, parts):
        other = lax.rem(part + offset, parts)
        pl.semaphore_signal(barrier, inc=1, device_id={"grp": other}, device_id_type=MESH)
    pl.semaphore_wait(barrier, parts - 1)

    rows_both, span = shared_ref.shape[1:]
    width = span * parts
    per_owner = counts_ref.shape[1] // parts
    rows = rows_both // per_owner
    positions = memory.shape[0] * memory.shape[3]
    own = own_lanes(rows, span // BUNDLE)
    loads[0].wait()
    loads[1].start()
    for pieces in zip(*streams):
        for copy in pieces:
            copy.start()

    def back(offset):
        other = lax.rem(part + offset, parts)
        return pltpu.make_async_remote_copy(
            src_ref=sent.at[offset], dst_ref=mixed.at[part], send_sem=back_send.at[offset],
            recv_sem=back_recv.at[offset], device_id={"grp": other}, device_id_type=MESH)

    for offset in list(range(1, parts)) + [0]:
        other = lax.rem(part + offset, parts)
        groups = [ids_ref[other, 1, n] for n in range(per_owner)]
        results = attend(
            [shared_ref[other, n * rows : (n + 1) * rows, :] for n in range(per_owner)],
            [memory[:, 0, group].reshape(positions, span) for group in groups],
            [memory[:, 1, group].reshape(positions, span) for group in groups],
            None, own, True)
        for n, result in enumerate(results):
            at = slice(n * rows, (n + 1) * rows)
            if offset:
                sent[offset, at, :] = result.astype(sent.dtype)
            else:
                mixed[part, at, :] = result.astype(sent.dtype)
        if offset:
            back(offset).start()
    loads[1].wait()
    for offset in range(1, parts):
        back(offset).wait_recv()
    for low in range(0, width, 256):
        lanes = slice(low, low + 256)
        value = norm_ref[:, lanes].astype(jnp.float32)
        for index in range(parts):
            value = value + jnp.dot(
                mixed[index], wco[index * span : (index + 1) * span, lanes], preferred_element_type=jnp.float32
            )
        total[:, lanes] = value
    normalise(total, second)
    total[...] = second[...].astype(jnp.float32)
    for index in range(parts):
        streams[0][index].wait()
        streams[1][index].wait()

    def feed(index, carry):
        hidden = []
        for low in range(0, win.shape[2], 256):
            value = jnp.dot(second[...], win[index, :, low : low + 256], preferred_element_type=jnp.float32)
            hidden.append(gelu(value).astype(jnp.bfloat16))
        hidden = jnp.concatenate(hidden, axis=1)
        for low in range(0, width, 256):
            lanes = slice(low, low + 256)
            total[:, lanes] += jnp.dot(hidden, wout[index, :, lanes], preferred_element_type=jnp.float32)
        return carry

    lax.fori_loop(0, parts, feed, 0)
    position = lax.broadcasted_iota(jnp.int32, (rows, width), 0)
    for n in range(per_owner):
        at = slice(n * rows, (n + 1) * rows)
        normed = layer_norm(total[at, :])
        live = position < counts_ref[0, part * per_owner + n]
        out_ref[at, :] = jnp.where(live, normed, 0.0).astype(out_ref.dtype)
    for offset in range(1, parts):
        back(offset).wait_send()


def third_stage(ids, counts, shared, norm, memory, w_cross_output, w_in, w_out, owners, parts):
    any_vmem = lambda array: pltpu.VMEM(array.shape, array.dtype)
    return pl.pallas_call(
        functools.partial(third_kernel, owners, parts),
        in_specs=[SCALARS, SCALARS, WHOLE, WHOLE] + [ANY] * 4,
        out_specs=WHOLE,
        out_shape=jax.ShapeDtypeStruct(norm.shape, norm.dtype),
        scratch_shapes=[
            any_vmem(memory), any_vmem(w_cross_output), any_vmem(w_in), any_vmem(w_out),
            any_vmem(shared), any_vmem(shared),
            pltpu.VMEM(norm.shape, jnp.float32),
            any_vmem(norm),
            pltpu.SemaphoreType.DMA((2,)),
            pltpu.SemaphoreType.DMA((parts,)),
            pltpu.SemaphoreType.DMA((parts,)),
            pltpu.SemaphoreType.DMA((parts,)),
            pltpu.SemaphoreType.DMA((parts,)),
        ],
        compiler_params=pltpu.CompilerParams(
            collective_id=3, has_side_effects=True, vmem_limit_bytes=60 * MIB
        ),
    )(ids, counts, shared, norm, memory, w_cross_output, w_in, w_out)


def per_device(
    tokens,
    kv_pool,
    page_table,
    cache_lens,
    draft_lengths,
    draft_parents,
    accepted_path,
    prompt_group,
    memory_kv,
    w_query,
    w_key,
    w_value,
    w_output,
    w_cross_query,
    w_cross_output,
    w_in,
    w_out,
):
    req_count, draft_len, model_width = tokens.shape
    owners = page_table.shape[0]
    parts = lax.axis_size("grp")
    flat_rows = tokens.reshape(req_count * draft_len, model_width)
    query_all, lens, group_ids, accepted_kv, draft_mix, draft_stat = first_gather(
        flat_rows, w_query, w_key, w_value, draft_parents, accepted_path, cache_lens, prompt_group, owners, parts
    )
    mix, stat, accepted_kv = page_partials(page_table, lens, query_all, kv_pool, accepted_kv)
    first_norm, shared, memory_all, w_out_all, w_in_all = second_exchange(
        mix, stat, draft_mix, draft_stat, flat_rows, memory_kv, w_out, w_output, w_cross_query, w_in, owners, parts
    )
    result = third_stage(
        group_ids, draft_lengths, shared, first_norm, memory_all, w_cross_output, w_in_all, w_out_all, owners, parts
    )
    return (result.reshape(req_count, draft_len, model_width), accepted_kv)


def solution(mesh):
    return jax.shard_map(
        per_device,
        mesh=mesh,
        in_specs=(
            P(("req", "grp"), None, None),
            P("req", "grp", None),
            P(None, "grp", None),
            P(("req", "grp")),
            P("req", None),
            P(("req", "grp"), None),
            P(("req", "grp"), None),
            P(("req", "grp")),
            P(None, "req", None),
            P(),
            P(),
            P(),
            P(),
            P(),
            P(),
            P(None, "grp"),
            P("grp", None),
        ),
        out_specs=(P(("req", "grp"), None, None), P(("req", "grp"), None, None)),
        check_vma=False,
    )
```

```python
import functools

import jax
import jax.numpy as jnp
from jax import lax
from jax.experimental import pallas as pl
from jax.experimental.pallas import tpu as pltpu
from jax.sharding import PartitionSpec as P

HEADS = 16
BUNDLE = 4
MESH = pl.DeviceIdType.MESH
ANY = pl.BlockSpec(memory_space=pl.ANY)
WHOLE = pl.BlockSpec(memory_space=pltpu.VMEM)
SCALARS = pl.BlockSpec(memory_space=pltpu.SMEM)
MIB = 1024 * 1024
RIGHT, LEFT, PAIR = 0, 1, 2

EPSILON = 1e-05
NEGATIVE = -1e30


def layer_norm(values):
    center = values - jnp.mean(values, axis=-1, keepdims=True)
    spread = jnp.mean(center * center, axis=-1, keepdims=True)
    return center * lax.rsqrt(spread + EPSILON)


def flip(index, bit):
    return index + bit - 2 * bit * ((index // bit) % 2)


def flips(index, mask):
    bit = 1
    while bit <= mask:
        if mask & bit:
            index = flip(index, bit)
        bit *= 2
    return index


class Line:
    def __init__(self, owners, items, send_sems, recv_sems):
        self.me = lax.axis_index("req")
        self.half = owners // 2
        self.place, self.side = self.me // 2, self.me % 2
        self.pair = flip(self.me, 1)
        self.right = lax.rem(self.place + 1, self.half) * 2 + self.side
        self.left = lax.rem(self.place + self.half - 1, self.half) * 2 + self.side
        self.items, self.send_sems, self.recv_sems = items, send_sems, recv_sems

    def copy(self, item, way, source, owner):
        target = (self.right, self.left, self.pair)[way]
        return pltpu.make_async_remote_copy(
            src_ref=source,
            dst_ref=self.items[item][1](owner),
            send_sem=self.send_sems.at[item, way, owner],
            recv_sem=self.recv_sems.at[item, owner],
            device_id={"req": target},
            device_id_type=MESH,
        )

    def arrive(self, item, owner):
        self.copy(item, PAIR, self.items[item][1](owner), owner).wait_recv()

    def both_ways(self, item, source, owner, act):
        pl.when(self.place < self.half - 1)(lambda: act(self.copy(item, RIGHT, source, owner)))
        pl.when(self.place > 0)(lambda: act(self.copy(item, LEFT, source, owner)))

    def owners_of(self, item, place):
        first = place * 2 + self.side
        return (first, flip(first, 1)) if self.items[item][2] else (first,)

    def start(self, item):
        source = self.items[item][0]
        self.both_ways(item, source, self.me, lambda copy: copy.start())
        if self.items[item][2]:
            self.copy(item, PAIR, source, self.me).start()

    def hand(self, item, distance):
        if self.items[item][2]:
            return
        if distance == 0:
            self.copy(item, PAIR, self.items[item][0], self.me).start()
            return

        def give(place):
            owner = place * 2 + self.side
            self.copy(item, PAIR, self.items[item][1](owner), owner).start()

        pl.when(self.place - distance >= 0)(lambda: give(self.place - distance))
        pl.when(self.place + distance < self.half)(lambda: give(self.place + distance))

    def start_wide(self, item):
        if self.items[item][2]:
            self.arrive(item, self.pair)
            block = self.items[item][1](self.pair)
            self.both_ways(item, block, self.pair, lambda copy: copy.start())

    def step(self, item, distance):
        def forward(place, way, more):
            for owner in self.owners_of(item, place):
                self.arrive(item, owner)
                block = self.items[item][1](owner)
                pl.when(more)(lambda: self.copy(item, way, block, owner).start())

        pl.when(self.place - distance >= 0)(
            lambda: forward(self.place - distance, RIGHT, self.place < self.half - 1)
        )
        pl.when(self.place + distance < self.half)(
            lambda: forward(self.place + distance, LEFT, self.place > 0)
        )

    def finish(self, item):
        source, target, wide = self.items[item]
        if not wide:
            for place in range(self.half):
                self.arrive(item, place * 2 + flip(self.side, 1))
        self.copy(item, PAIR, source, self.me).wait_send()
        self.both_ways(item, source, self.me, lambda copy: copy.wait_send())
        if wide:
            self.both_ways(item, source, self.pair, lambda copy: copy.wait_send())

        def sent(place, way, more):
            for owner in self.owners_of(item, place):
                pl.when(more)(lambda: self.copy(item, way, source, owner).wait_send())
                if not wide:
                    self.copy(item, PAIR, source, owner).wait_send()

        for distance in range(1, self.half):
            pl.when(self.place - distance >= 0)(
                lambda: sent(self.place - distance, RIGHT, self.place < self.half - 1)
            )
            pl.when(self.place + distance < self.half)(
                lambda: sent(self.place + distance, LEFT, self.place > 0)
            )


class Square:
    def __init__(self, source, out, send_sems, recv_sems):
        self.part = lax.axis_index("grp")
        self.near, self.far = flip(self.part, 1), flip(self.part, 2)
        self.source, self.out, self.send_sems, self.recv_sems = source, out, send_sems, recv_sems

    def copy(self, hop, source, owner):
        return pltpu.make_async_remote_copy(
            src_ref=source,
            dst_ref=self.out.at[owner],
            send_sem=self.send_sems.at[hop],
            recv_sem=self.recv_sems.at[owner],
            device_id={"grp": (self.far, self.near, self.near)[hop]},
            device_id_type=MESH,
        )

    def start(self):
        self.copy(0, self.source, self.part).start()
        self.copy(1, self.source, self.part).start()

    def forward(self):
        block = self.out.at[self.far]
        self.copy(2, block, self.far).wait_recv()
        self.copy(2, block, self.far).start()

    def finish(self):
        self.copy(1, self.source, self.near).wait_recv()
        self.copy(2, self.source, flip(self.far, 1)).wait_recv()
        self.copy(0, self.source, self.part).wait_send()
        self.copy(1, self.source, self.part).wait_send()
        self.copy(2, self.source, self.far).wait_send()


def meet(owners, parts):
    barrier = pltpu.get_barrier_semaphore()
    me, part = lax.axis_index("req"), lax.axis_index("grp")
    for offset in range(1, owners):
        other = lax.rem(me + offset, owners)
        pl.semaphore_signal(barrier, inc=1, device_id={"req": other}, device_id_type=MESH)
    for offset in range(1, parts):
        other = lax.rem(part + offset, parts)
        pl.semaphore_signal(barrier, inc=1, device_id={"grp": other}, device_id_type=MESH)
    pl.semaphore_wait(barrier, owners + parts - 2)


def line_sems(items, owners):
    return [pltpu.SemaphoreType.DMA((items, 3, owners)), pltpu.SemaphoreType.DMA((items, owners))]


def square_sems(parts):
    return [pltpu.SemaphoreType.DMA((3,)), pltpu.SemaphoreType.DMA((parts,))]


CUTS = 4


def project(rows, weight_ref, out, scale=None, tile=256):
    for low in range(0, weight_ref.shape[1], tile):
        value = jnp.dot(rows, weight_ref[:, low : low + tile], preferred_element_type=jnp.float32)
        if scale is not None:
            value = value * scale
        out[:, low : low + tile] = value.astype(out.dtype)


def first_kernel(owners, parts, tokens_ref, wq_ref, wk_ref, wv_ref, parents_ref, path_ref, length_ref, group_ref,
                 q_out, lens_out, grps_out, accepted_out, draft_out, draft_stat,
                 tokens, wq, wk, wv, query, keys, values, small_ref, load_sems, hold_sems, line_send, line_recv,
                 small_send, small_recv):
    me, part = lax.axis_index("req"), lax.axis_index("grp")
    loads = [
        pltpu.make_async_copy(source, target, load_sems.at[index])
        for index, (source, target) in enumerate(
            ((tokens_ref, tokens), (wq_ref, wq), (wk_ref, wk), (wv_ref, wv))
        )
    ]
    for copy in loads:
        copy.start()
    width = tokens.shape[1]
    per_owner, rows = parents_ref.shape
    head_dim = width // HEADS
    line_id = lax.broadcasted_iota(jnp.int32, small_ref.shape, 0)
    lane_id = lax.broadcasted_iota(jnp.int32, small_ref.shape, 1)
    filled = jnp.zeros(small_ref.shape, jnp.int32)
    for n in range(per_owner):
        for line_index, source in enumerate((length_ref, group_ref)):
            filled = jnp.where((line_id == line_index) & (lane_id == n), source[n], filled)
    small_ref[...] = filled
    loads[0].wait()
    loads[1].wait()
    project(tokens[...], wq, query, head_dim ** (-0.5))
    meet(owners, parts)
    cut_rows = query.shape[0] // CUTS

    def slot(cut, owner):
        return q_out.at[owner, pl.ds(cut * cut_rows, cut_rows)]

    items = [
        (query.at[pl.ds(cut * cut_rows, cut_rows)], functools.partial(slot, cut), cut == 0) for cut in range(CUTS)
    ]
    line = Line(owners, items, line_send, line_recv)
    for item in range(CUTS):
        line.start(item)
        line.hand(item, 0)
    smalls = []
    for offset in range(1, owners):
        smalls.append(pltpu.make_async_remote_copy(
            src_ref=small_ref, dst_ref=lens_out.at[me],
            send_sem=small_send.at[offset], recv_sem=small_recv.at[offset],
            device_id={"req": lax.rem(me + offset, owners)}, device_id_type=MESH))
    for offset in range(1, parts):
        smalls.append(pltpu.make_async_remote_copy(
            src_ref=small_ref, dst_ref=grps_out.at[part],
            send_sem=small_send.at[owners + offset], recv_sem=small_recv.at[owners + offset],
            device_id={"grp": lax.rem(part + offset, parts)}, device_id_type=MESH))
    for copy in smalls:
        copy.start()
    holds = [
        pltpu.make_async_copy(query, q_out.at[me], hold_sems.at[0]),
        pltpu.make_async_copy(small_ref, lens_out.at[me], hold_sems.at[1]),
        pltpu.make_async_copy(small_ref, grps_out.at[part], hold_sems.at[2]),
    ]
    for copy in holds:
        copy.start()
    loads[2].wait()
    project(tokens[...], wk, keys)
    for item in range(CUTS):
        line.start_wide(item)

    def advance(distance):
        for item in range(CUTS):
            line.step(item, distance)
            line.hand(item, distance)

    loads[3].wait()
    if owners > 2:
        advance(1)
    project(tokens[...], wv, values)
    own = own_lanes(rows, head_dim)
    square_shape = (rows, rows)
    down = lax.broadcasted_iota(jnp.int32, square_shape, 0)
    eye = (down == lax.broadcasted_iota(jnp.int32, square_shape, 1)).astype(jnp.float32).astype(jnp.bfloat16)
    turn = (((1,), (1,)), ((), ()))
    span = BUNDLE * head_dim
    bundles = [slice(low, low + span) for low in range(0, width, span)]

    def drafts(n, carry):
        at = pl.ds(pl.multiple_of(n * rows, rows), rows)
        linked = (parents_ref[pl.ds(n, 1), :] == down).astype(jnp.float32).astype(jnp.bfloat16)
        closure = linked + eye
        for sweep_index in range((rows - 1).bit_length()):
            closure = jnp.minimum(jnp.dot(closure, closure, preferred_element_type=jnp.float32), 1.0)
            closure = closure.astype(jnp.bfloat16)
        reach = lax.dot_general(eye, closure, turn, preferred_element_type=jnp.float32)
        mixes, stats = attend(
            [query[at, lanes] for lanes in bundles],
            [keys[at, lanes] for lanes in bundles],
            [values[at, lanes] for lanes in bundles],
            jnp.concatenate([reach] * BUNDLE, axis=0) > 0.5, own)
        for lanes, mix in zip(bundles, mixes):
            draft_out[at, lanes] = mix.astype(draft_out.dtype)
        draft_stat[n] = stats
        chosen = (path_ref[pl.ds(n, 1), :] == down).astype(jnp.float32).astype(jnp.bfloat16)
        chosen = lax.dot_general(eye, chosen, turn, preferred_element_type=jnp.float32).astype(jnp.bfloat16)
        for low in range(0, width, 256):
            for offset, source in ((0, keys), (width, values)):
                picked = jnp.dot(chosen, source[at, low : low + 256], preferred_element_type=jnp.float32)
                accepted_out[n, :, offset + low : offset + low + 256] = picked.astype(accepted_out.dtype)
        return carry

    for distance in range(2, owners // 2):
        advance(distance)
    lax.fori_loop(0, per_owner, drafts, 0)
    for item in range(CUTS):
        line.finish(item)
    for copy in smalls + holds:
        copy.wait()


def first_gather(tokens, w_query, w_key, w_value, parents, path, lengths, groups, owners, parts):
    sds = jax.ShapeDtypeStruct
    per_owner, rows = parents.shape
    small = sds((8, 128), jnp.int32)
    weight = pltpu.VMEM(w_query.shape, w_query.dtype)
    block = pltpu.VMEM(tokens.shape, tokens.dtype)
    return pl.pallas_call(
        functools.partial(first_kernel, owners, parts),
        in_specs=[ANY] * 4 + [WHOLE] * 2 + [SCALARS] * 2,
        out_specs=[ANY] * 3 + [WHOLE] * 3,
        out_shape=[
            sds((owners,) + tokens.shape, tokens.dtype),
            sds((owners,) + small.shape, small.dtype),
            sds((parts,) + small.shape, small.dtype),
            sds((per_owner, rows, 2 * tokens.shape[1]), tokens.dtype),
            sds(tokens.shape, tokens.dtype),
            sds((per_owner, 2 * (HEADS // BUNDLE), BUNDLE * rows), jnp.float32),
        ],
        scratch_shapes=[
            block, weight, weight, weight, block, block, block,
            pltpu.VMEM(small.shape, small.dtype),
            pltpu.SemaphoreType.DMA((4,)),
            pltpu.SemaphoreType.DMA((3,)),
            *line_sems(CUTS, owners),
            pltpu.SemaphoreType.DMA((owners + parts,)),
            pltpu.SemaphoreType.DMA((owners + parts,)),
        ],
        compiler_params=pltpu.CompilerParams(
            collective_id=1, has_side_effects=True, vmem_limit_bytes=60 * MIB
        ),
    )(tokens, w_query, w_key, w_value, parents, path, lengths, groups)


def own_lanes(rows, head_dim):
    shape = (BUNDLE * rows, BUNDLE * head_dim)
    row = lax.broadcasted_iota(jnp.int32, shape, 0) // rows
    lane = lax.broadcasted_iota(jnp.int32, shape, 1) // head_dim
    return row == lane


def attend(queries, keys, values, seen, own, final=False):
    rows = queries[0].shape[0]
    scores = []
    for query, key in zip(queries, keys):
        stacked = jnp.where(own, jnp.concatenate([query] * BUNDLE, axis=0), jnp.zeros((), query.dtype))
        scores.append(
            lax.dot_general(stacked, key, (((1,), (1,)), ((), ())), preferred_element_type=jnp.float32)
        )
    expos, tops, totals = [], [], []
    for score in scores:
        if seen is not None:
            score = jnp.where(seen, score, NEGATIVE)
        top = jnp.max(score, axis=1, keepdims=True)
        expo = jnp.exp(score - top)
        expos.append(expo.astype(jnp.bfloat16))
        tops.append(top)
        totals.append(jnp.sum(expo, axis=1, keepdims=True))
    mixes = []
    for expo, value, total in zip(expos, values, totals):
        mix = jnp.dot(expo, value, preferred_element_type=jnp.float32)
        mix = jnp.where(own, mix / total if final else mix, 0.0)
        folded = mix[:rows]
        for part in range(1, BUNDLE):
            folded = folded + mix[part * rows : (part + 1) * rows]
        mixes.append(folded)
    if final:
        return mixes
    lane = lax.broadcasted_iota(jnp.int32, (BUNDLE * rows, 128), 1)
    stats = jnp.zeros((BUNDLE * rows, 128), jnp.float32)
    for index, column in enumerate(tops + totals):
        stats = jnp.where(lane == index, column, stats)
    return mixes, jnp.transpose(stats)[: 2 * len(queries)]


def pages_kernel(table_ref, lens_ref, query_ref, pool_ref, accepted_ref, mix_out, stat_out, accepted_out, held, sems):
    me, owner = lax.axis_index("req"), pl.program_id(0)
    _, per_owner, per_req = table_ref.shape
    width = query_ref.shape[2]
    pool_pages, page = pool_ref.shape[0], pool_ref.shape[1]
    rows = query_ref.shape[1] // per_owner
    head_dim = width // HEADS
    span = BUNDLE * head_dim
    fetch = pltpu.make_async_copy(accepted_ref, held, sems.at[0])
    store_back = pltpu.make_async_copy(held, accepted_out, sems.at[1])
    pl.when(owner == 0)(fetch.start)

    @pl.when(owner == 1)
    def _():
        fetch.wait()
        store_back.start()

    own = own_lanes(rows, head_dim)
    bundles = [slice(low, low + span) for low in range(0, width, span)]

    def rows_at(n):
        return pl.ds(pl.multiple_of(n * rows, rows), rows)

    def store(out, stat, n, result):
        mixes, stats = result
        for lanes, mix in zip(bundles, mixes):
            out[0, rows_at(n), lanes] = mix.astype(out.dtype)
        stat[n] = stats

    def one(n, carry):
        length = lens_ref[owner, 0, n]
        count = jnp.int32(0)
        slots = [jnp.int32(0)] * per_req
        starts = [jnp.int32(0)] * per_req
        for place in range(per_req):
            entry = table_ref[owner, n, place]
            hit = (entry // pool_pages == me) & (place * page < length)
            for k in range(place + 1):
                here = hit & (count == k)
                slots[k] = jnp.where(here, entry % pool_pages, slots[k])
                starts[k] = jnp.where(here, length - place * page, starts[k])
            count = count + hit.astype(jnp.int32)

        def work(uses):
            lane = lax.broadcasted_iota(jnp.int32, (BUNDLE * rows, uses * page), 1)
            limit = jnp.zeros_like(lane)
            for k in range(uses):
                limit = jnp.where(lane // page == k, k * page + starts[k], limit)
            seen = lane < limit
            at = rows_at(n)
            store(mix_out, stat_out, n, attend(
                [query_ref[0, at, lanes] for lanes in bundles],
                [jnp.concatenate([pool_ref[slots[k], :, lanes] for k in range(uses)], axis=0) for lanes in bundles],
                [
                    jnp.concatenate(
                        [pool_ref[slots[k], :, width + lanes.start : width + lanes.stop] for k in range(uses)], axis=0
                    )
                    for lanes in bundles
                ],
                seen, own))

        @pl.when(count == 0)
        def _():
            mix_out[0, rows_at(n), :] = jnp.zeros((rows, width), mix_out.dtype)
            stat_out[n, pl.ds(0, BUNDLE), :] = jnp.full((BUNDLE, BUNDLE * rows), NEGATIVE, jnp.float32)
            stat_out[n, pl.ds(BUNDLE, BUNDLE), :] = jnp.zeros((BUNDLE, BUNDLE * rows), jnp.float32)

        pl.when(count == 1)(lambda: work(1))
        pl.when(count == 2)(lambda: work(2))
        pl.when((count > 2) & (count <= 4))(lambda: work(4))
        pl.when(count > 4)(lambda: work(per_req))
        return carry

    lax.fori_loop(0, per_owner, one, 0)
    pl.when(owner == pl.num_programs(0) - 1)(store_back.wait)


def page_partials(table, lens, query_all, pool, accepted):
    owners, rows_both, width = query_all.shape
    per_owner = table.shape[1]
    rows = rows_both // per_owner
    sds = jax.ShapeDtypeStruct
    block = pl.BlockSpec((1, rows_both, width), lambda owner: (owner, 0, 0))
    stat_shape = (2 * (HEADS // BUNDLE), BUNDLE * rows)
    return pl.pallas_call(
        pages_kernel,
        grid=(owners,),
        in_specs=[SCALARS, SCALARS, block, WHOLE, ANY],
        out_specs=[block, pl.BlockSpec((per_owner,) + stat_shape, lambda owner: (owner, 0, 0)), ANY],
        out_shape=[
            sds(query_all.shape, query_all.dtype),
            sds((owners * per_owner,) + stat_shape, jnp.float32),
            sds(accepted.shape, accepted.dtype),
        ],
        scratch_shapes=[pltpu.VMEM(accepted.shape, accepted.dtype), pltpu.SemaphoreType.DMA((2,))],
        compiler_params=pltpu.CompilerParams(vmem_limit_bytes=60 * MIB),
    )(table, lens, query_all, pool, accepted)


def merge(sources, stats, out, stat_out, last):
    per_owner, rows, span, store = out
    wide = BUNDLE * rows
    eye = lax.broadcasted_iota(jnp.int32, (rows, wide), 1) % rows == lax.broadcasted_iota(jnp.int32, (rows, wide), 0)
    shape = (2 * wide, span)
    row_head = (lax.broadcasted_iota(jnp.int32, shape, 0) % wide) // rows
    ones = (row_head == lax.broadcasted_iota(jnp.int32, shape, 1) // (span // BUNDLE)).astype(jnp.float32)
    ones = ones.astype(jnp.bfloat16)
    zero = jnp.zeros((), jnp.bfloat16)
    highs, lows = [], []
    for n in range(per_owner):
        read = [stat(n) for stat in stats]
        tops = [value[:BUNDLE] for value in read]
        sums = [value[BUNDLE:] for value in read]
        top = functools.reduce(jnp.maximum, tops)
        scales = [jnp.exp(value - top) for value in tops]
        total = functools.reduce(jnp.add, [scale * part for scale, part in zip(scales, sums)])
        if last:
            scales = [scale / total for scale in scales]
        else:
            stat_out(n, jnp.concatenate([top, total], axis=0))
        high = [scale.astype(jnp.bfloat16) for scale in scales]
        highs.append(high)
        lows.append([(scale - part.astype(jnp.float32)).astype(jnp.bfloat16) for scale, part in zip(scales, high)])
    for bundle in range(HEADS // BUNDLE):
        lanes = slice(bundle * span, (bundle + 1) * span)

        def spread(parts):
            row = parts[bundle : bundle + 1]
            return jnp.where(eye, jnp.broadcast_to(row, eye.shape), zero)

        mixed = [None] * per_owner
        for index, source in enumerate(sources):
            weights = jnp.concatenate(
                [
                    jnp.concatenate([spread(highs[n][index]), spread(lows[n][index])], axis=1)
                    for n in range(per_owner)
                ],
                axis=0,
            )
            weights = jnp.dot(weights, ones, preferred_element_type=jnp.float32)
            for n in range(per_owner):
                term = weights[n * rows : (n + 1) * rows] * source(n, lanes).astype(jnp.float32)
                mixed[n] = term if index == 0 else mixed[n] + term
        for n in range(per_owner):
            store(n, lanes, mixed[n])


GROUP_CUTS = 2
WINDOW = 2


def normalise(source, out):
    rows = source.shape[0]
    step = 64
    for low in range(0, rows, step):
        out[low : low + step, :] = layer_norm(source[low : low + step, :]).astype(out.dtype)


def second_kernel(owners, parts, mix_ref, stat_ref, draft_ref, draft_stat, tokens_ref, memory_ref, wout_ref,
                  wo_ref, wcq_ref, win_ref, norm_out, shared_out, m_out, wout_out, win_out,
                  own, own_stat, got, got_stat, zin, zin_stat, memory, wout, wo, wcq, win, self_mix, total, cross,
                  load_sems, own_sems, hold_sems, y_send, y_recv, z_send, z_recv,
                  line_send, line_recv, wout_send, wout_recv, share_send, share_recv, win_send, win_recv):
    me, part = lax.axis_index("req"), lax.axis_index("grp")
    half = owners // 2
    place, side = me // 2, me % 2
    pair = flip(me, 1)
    per_owner = draft_stat.shape[0]
    width = draft_ref.shape[1]
    rows = draft_ref.shape[0] // per_owner
    span = BUNDLE * (width // HEADS)
    groups = memory_ref.shape[0]
    wide = memory_ref.shape[2] // 2
    lanes_in = wide // parts
    order = list(range(half - 1, -1, -1))

    own_loads = {}
    for mask in order:
        dest = flips(place, mask)
        own_loads[mask] = [
            pltpu.make_async_copy(mix_ref.at[dest * 2 + side], own.at[dest], own_sems.at[0, mask]),
            pltpu.make_async_copy(stat_ref.at[dest * 2 + side], own_stat.at[dest], own_sems.at[1, mask]),
        ]
        for copy in own_loads[mask]:
            copy.start()
    loads = []
    for kind in range(2):
        lanes = pl.ds(pl.multiple_of(kind * wide + part * lanes_in, 128), lanes_in)
        loads.append(pltpu.make_async_copy(memory_ref.at[:, :, lanes], memory.at[kind], load_sems.at[kind]))
    loads.append(pltpu.make_async_copy(wout_ref, wout, load_sems.at[2]))
    loads.append(pltpu.make_async_copy(win_ref, win, load_sems.at[5]))
    weights = [
        pltpu.make_async_copy(wo_ref, wo, load_sems.at[3]),
        pltpu.make_async_copy(wcq_ref, wcq, load_sems.at[4]),
    ]
    for copy in loads + weights:
        copy.start()
    meet(owners, parts)

    def to_pair(mask):
        dest = flips(place, mask)
        far = dest * 2 + flip(side, 1)
        return [
            pltpu.make_async_remote_copy(
                src_ref=source.at[far], dst_ref=target.at[dest], send_sem=y_send.at[k, mask],
                recv_sem=y_recv.at[k, mask], device_id={"req": pair}, device_id_type=MESH)
            for k, (source, target) in enumerate(((mix_ref, got), (stat_ref, got_stat)))
        ]

    def to_place(mask):
        dest = flips(place, mask)
        low = mask & -mask
        return [
            pltpu.make_async_remote_copy(
                src_ref=source.at[dest], dst_ref=target.at[mask], send_sem=z_send.at[k, mask],
                recv_sem=z_recv.at[k, mask], device_id={"req": flip(place, low) * 2 + side}, device_id_type=MESH)
            for k, (source, target) in enumerate(((own, zin), (own_stat, zin_stat)))
        ]

    def below(mask):
        bits, bit = [], 1
        while bit < (mask & -mask if mask else half):
            bits.append(mask + bit)
            bit *= 2
        return bits

    for mask in order[:WINDOW]:
        for copy in to_pair(mask):
            copy.start()

    cut = groups // GROUP_CUTS

    def slot(kind, first, owner):
        return m_out.at[owner, kind, pl.ds(first, cut)]

    items = [
        (memory.at[kind, pl.ds(index * cut, cut)], functools.partial(slot, kind, index * cut), index == 0)
        for kind in range(2)
        for index in range(GROUP_CUTS)
    ]
    line = Line(owners, items, line_send, line_recv)
    squares = [Square(win, win_out, win_send, win_recv), Square(wout, wout_out, wout_send, wout_recv)]
    for copy in loads[:2]:
        copy.wait()
    for item in range(len(items)):
        line.start(item)
    for copy in loads[2:]:
        copy.wait()
    for square in squares:
        square.start()
    holds = [
        pltpu.make_async_copy(win, win_out.at[part], hold_sems.at[2]),
        pltpu.make_async_copy(memory, m_out.at[me], hold_sems.at[0]),
        pltpu.make_async_copy(wout, wout_out.at[part], hold_sems.at[1]),
    ]
    for copy in holds:
        copy.start()

    def rows_at(n):
        return slice(n * rows, (n + 1) * rows)

    def take(ref, index):
        return lambda n, lanes: ref[index, rows_at(n), lanes]

    def take_stat(ref, index):
        return lambda n: ref[index, n]

    for turn, mask in enumerate(order):
        dest = flips(place, mask)
        for copy in to_pair(mask):
            copy.wait_recv()
        if turn + WINDOW < half:
            for copy in to_pair(order[turn + WINDOW]):
                copy.start()
        for copy in own_loads[mask]:
            copy.wait()

        senders = below(mask)
        for sender in senders:
            for copy in to_place(sender):
                copy.wait_recv()
        sources = [take(own, dest), take(got, dest)] + [take(zin, sender) for sender in senders]
        stats = [take_stat(own_stat, dest), take_stat(got_stat, dest)] + [take_stat(zin_stat, sender) for sender in senders]
        if mask:

            def store(n, lanes, value):
                own[dest, rows_at(n), lanes] = value.astype(own.dtype)

            def store_stat(n, value):
                own_stat[dest, n] = value

            merge(sources, stats, (per_owner, rows, span, store), store_stat, False)
            for copy in to_place(mask):
                copy.start()
        else:

            def store(n, lanes, value):
                self_mix[rows_at(n), lanes] = value.astype(self_mix.dtype)

            sources.append(lambda n, lanes: draft_ref[rows_at(n), lanes])
            stats.append(lambda n: draft_stat[n])
            merge(sources, stats, (per_owner, rows, span, store), None, True)
            for item in range(len(items)) if turn else ():
                line.step(item, turn)
                line.hand(item, turn)
        if turn == 0:
            for item in range(len(items)):
                line.start_wide(item)
        elif turn < half - 1:
            for item in range(len(items)):
                line.step(item, turn)
        if turn == half - 2 or half == 1:
            for distance in range(turn + 1):
                for item in range(len(items)):
                    line.hand(item, distance)
    for square in squares:
        square.forward()

    for copy in weights:
        copy.wait()
    for low in range(0, width, 256):
        lanes = slice(low, low + 256)
        total[:, lanes] = tokens_ref[:, lanes].astype(jnp.float32) + jnp.dot(
            self_mix[...], wo[:, lanes], preferred_element_type=jnp.float32
        )
    normalise(total, norm_out)

    def share(offset):
        other = lax.rem(part + offset, parts)
        return pltpu.make_async_remote_copy(
            src_ref=cross.at[offset], dst_ref=shared_out.at[part], send_sem=share_send.at[offset],
            recv_sem=share_recv.at[offset], device_id={"grp": other}, device_id_type=MESH)

    scale = (width // HEADS) ** (-0.5)
    for offset in list(range(1, parts)) + [0]:
        other = lax.rem(part + offset, parts)
        lanes = pl.ds(pl.multiple_of(other * lanes_in, 128), lanes_in)
        value = jnp.dot(norm_out[...], wcq[:, lanes], preferred_element_type=jnp.float32) * scale
        if offset:
            cross[offset] = value.astype(cross.dtype)
            share(offset).start()
        else:
            shared_out[part] = value.astype(cross.dtype)

    for item in range(len(items)):
        line.finish(item)
    for square in squares:
        square.finish()
    for offset in range(1, parts):
        share(offset).wait()
    for mask in range(half):
        for copy in to_pair(mask):
            copy.wait_send()
        if mask:
            for copy in to_place(mask):
                copy.wait_send()
    for copy in holds:
        copy.wait()


def second_exchange(mix, stat, draft, draft_stat, tokens, memory, w_out, w_output, w_cross_query, w_in, owners, parts):
    groups, local, both = memory.shape
    half = owners // 2
    rows_both, width = draft.shape
    stat = stat.reshape((owners,) + draft_stat.shape)
    sds = jax.ShapeDtypeStruct
    chunk = pltpu.VMEM((half, rows_both, width), mix.dtype)
    chunk_stat = pltpu.VMEM((half,) + draft_stat.shape, stat.dtype)
    weight = pltpu.VMEM(w_output.shape, w_output.dtype)
    items = 2 * GROUP_CUTS
    share = (parts, rows_both, width // parts)
    return pl.pallas_call(
        functools.partial(second_kernel, owners, parts),
        in_specs=[ANY, ANY, WHOLE, WHOLE, WHOLE] + [ANY] * 5,
        out_specs=[WHOLE, WHOLE] + [ANY] * 3,
        out_shape=[
            sds(draft.shape, draft.dtype),
            sds(share, draft.dtype),
            sds((owners, 2, groups, local, both // 2 // parts), memory.dtype),
            sds((parts,) + w_out.shape, w_out.dtype),
            sds((parts,) + w_in.shape, w_in.dtype),
        ],
        scratch_shapes=[
            chunk, chunk_stat, chunk, chunk_stat, chunk, chunk_stat,
            pltpu.VMEM((2, groups, local, both // 2 // parts), memory.dtype),
            pltpu.VMEM(w_out.shape, w_out.dtype),
            weight, weight,
            pltpu.VMEM(w_in.shape, w_in.dtype),
            pltpu.VMEM(draft.shape, draft.dtype),
            pltpu.VMEM(draft.shape, jnp.float32),
            pltpu.VMEM(share, draft.dtype),
            pltpu.SemaphoreType.DMA((6,)),
            pltpu.SemaphoreType.DMA((2, half)),
            pltpu.SemaphoreType.DMA((3,)),
            pltpu.SemaphoreType.DMA((2, half)),
            pltpu.SemaphoreType.DMA((2, half)),
            pltpu.SemaphoreType.DMA((2, half)),
            pltpu.SemaphoreType.DMA((2, half)),
            *line_sems(items, owners),
            *square_sems(parts),
            pltpu.SemaphoreType.DMA((parts,)),
            pltpu.SemaphoreType.DMA((parts,)),
            *square_sems(parts),
        ],
        compiler_params=pltpu.CompilerParams(
            collective_id=2, has_side_effects=True, vmem_limit_bytes=60 * MIB
        ),
    )(mix, stat, draft, draft_stat, tokens, memory, w_out, w_output, w_cross_query, w_in)


def gelu(values):
    return values * (1.0 + lax.erf(values * (0.5**0.5))) * 0.5


def third_kernel(owners, parts, ids_ref, counts_ref, shared_ref, norm_ref, m_ref, wco_ref, win_ref, wout_ref, out_ref,
                 memory, wco, win, wout, mixed, sent, total, second, load_sems, win_sems, wout_sems, back_send, back_recv):
    part = lax.axis_index("grp")
    loads = [
        pltpu.make_async_copy(m_ref, memory, load_sems.at[0]),
        pltpu.make_async_copy(wco_ref, wco, load_sems.at[1]),
    ]
    streams = [
        [pltpu.make_async_copy(source.at[index], target.at[index], sems.at[index]) for index in range(parts)]
        for source, target, sems in ((win_ref, win, win_sems), (wout_ref, wout, wout_sems))
    ]
    loads[0].start()
    barrier = pltpu.get_barrier_semaphore()
    for offset in range(1, parts):
        other = lax.rem(part + offset, parts)
        pl.semaphore_signal(barrier, inc=1, device_id={"grp": other}, device_id_type=MESH)
    pl.semaphore_wait(barrier, parts - 1)

    rows_both, span = shared_ref.shape[1:]
    width = span * parts
    per_owner = counts_ref.shape[1] // parts
    rows = rows_both // per_owner
    positions = memory.shape[0] * memory.shape[3]
    own = own_lanes(rows, span // BUNDLE)
    loads[0].wait()
    loads[1].start()
    for pieces in zip(*streams):
        for copy in pieces:
            copy.start()

    def back(offset):
        other = lax.rem(part + offset, parts)
        return pltpu.make_async_remote_copy(
            src_ref=sent.at[offset], dst_ref=mixed.at[part], send_sem=back_send.at[offset],
            recv_sem=back_recv.at[offset], device_id={"grp": other}, device_id_type=MESH)

    for offset in list(range(1, parts)) + [0]:
        other = lax.rem(part + offset, parts)
        groups = [ids_ref[other, 1, n] for n in range(per_owner)]
        results = attend(
            [shared_ref[other, n * rows : (n + 1) * rows, :] for n in range(per_owner)],
            [memory[:, 0, group].reshape(positions, span) for group in groups],
            [memory[:, 1, group].reshape(positions, span) for group in groups],
            None, own, True)
        for n, result in enumerate(results):
            at = slice(n * rows, (n + 1) * rows)
            if offset:
                sent[offset, at, :] = result.astype(sent.dtype)
            else:
                mixed[part, at, :] = result.astype(sent.dtype)
        if offset:
            back(offset).start()
    loads[1].wait()
    for offset in range(1, parts):
        back(offset).wait_recv()
    for low in range(0, width, 256):
        lanes = slice(low, low + 256)
        value = norm_ref[:, lanes].astype(jnp.float32)
        for index in range(parts):
            value = value + jnp.dot(
                mixed[index], wco[index * span : (index + 1) * span, lanes], preferred_element_type=jnp.float32
            )
        total[:, lanes] = value
    normalise(total, second)
    total[...] = second[...].astype(jnp.float32)
    for index in range(parts):
        streams[0][index].wait()
        streams[1][index].wait()

    def feed(index, carry):
        hidden = []
        for low in range(0, win.shape[2], 256):
            value = jnp.dot(second[...], win[index, :, low : low + 256], preferred_element_type=jnp.float32)
            hidden.append(gelu(value).astype(jnp.bfloat16))
        hidden = jnp.concatenate(hidden, axis=1)
        for low in range(0, width, 256):
            lanes = slice(low, low + 256)
            total[:, lanes] += jnp.dot(hidden, wout[index, :, lanes], preferred_element_type=jnp.float32)
        return carry

    lax.fori_loop(0, parts, feed, 0)
    for n in range(per_owner):
        at = slice(n * rows, (n + 1) * rows)
        normed = layer_norm(total[at, :])
        out_ref[at, :] = normed.astype(out_ref.dtype)
    for offset in range(1, parts):
        back(offset).wait_send()


def third_stage(ids, counts, shared, norm, memory, w_cross_output, w_in, w_out, owners, parts):
    any_vmem = lambda array: pltpu.VMEM(array.shape, array.dtype)
    return pl.pallas_call(
        functools.partial(third_kernel, owners, parts),
        in_specs=[SCALARS, SCALARS, WHOLE, WHOLE] + [ANY] * 4,
        out_specs=WHOLE,
        out_shape=jax.ShapeDtypeStruct(norm.shape, norm.dtype),
        scratch_shapes=[
            any_vmem(memory), any_vmem(w_cross_output), any_vmem(w_in), any_vmem(w_out),
            any_vmem(shared), any_vmem(shared),
            pltpu.VMEM(norm.shape, jnp.float32),
            any_vmem(norm),
            pltpu.SemaphoreType.DMA((2,)),
            pltpu.SemaphoreType.DMA((parts,)),
            pltpu.SemaphoreType.DMA((parts,)),
            pltpu.SemaphoreType.DMA((parts,)),
            pltpu.SemaphoreType.DMA((parts,)),
        ],
        compiler_params=pltpu.CompilerParams(
            collective_id=3, has_side_effects=True, vmem_limit_bytes=60 * MIB
        ),
    )(ids, counts, shared, norm, memory, w_cross_output, w_in, w_out)


def per_device(
    tokens,
    kv_pool,
    page_table,
    cache_lens,
    draft_lengths,
    draft_parents,
    accepted_path,
    prompt_group,
    memory_kv,
    w_query,
    w_key,
    w_value,
    w_output,
    w_cross_query,
    w_cross_output,
    w_in,
    w_out,
):
    req_count, draft_len, model_width = tokens.shape
    owners = page_table.shape[0]
    parts = lax.axis_size("grp")
    flat_rows = tokens.reshape(req_count * draft_len, model_width)
    query_all, lens, group_ids, accepted_kv, draft_mix, draft_stat = first_gather(
        flat_rows, w_query, w_key, w_value, draft_parents, accepted_path, cache_lens, prompt_group, owners, parts
    )
    mix, stat, accepted_kv = page_partials(page_table, lens, query_all, kv_pool, accepted_kv)
    first_norm, shared, memory_all, w_out_all, w_in_all = second_exchange(
        mix, stat, draft_mix, draft_stat, flat_rows, memory_kv, w_out, w_output, w_cross_query, w_in, owners, parts
    )
    result = third_stage(
        group_ids, draft_lengths, shared, first_norm, memory_all, w_cross_output, w_in_all, w_out_all, owners, parts
    )
    counts = lax.dynamic_slice_in_dim(draft_lengths[0], lax.axis_index("grp") * req_count, req_count, 0)
    live = jnp.arange(draft_len, dtype=jnp.int32)[None, :] < counts[:, None]
    result = result.reshape(req_count, draft_len, model_width)
    return (jnp.where(live[:, :, None], result, jnp.zeros((), result.dtype)), accepted_kv)


def solution(mesh):
    return jax.shard_map(
        per_device,
        mesh=mesh,
        in_specs=(
            P(("req", "grp"), None, None),
            P("req", "grp", None),
            P(None, "grp", None),
            P(("req", "grp")),
            P("req", None),
            P(("req", "grp"), None),
            P(("req", "grp"), None),
            P(("req", "grp")),
            P(None, "req", None),
            P(),
            P(),
            P(),
            P(),
            P(),
            P(),
            P(None, "grp"),
            P("grp", None),
        ),
        out_specs=(P(("req", "grp"), None, None), P(("req", "grp"), None, None)),
        check_vma=False,
    )
```
